32 devices in a mesh: row: 8 (over y, x, core), feat: 4 (over z).
Axes of the slice: x: 2, y: 2, z: 4, core: 2. Of those that a mesh axis runs over, the one named last changes fastest.
Arguments:
- bins: int32 [1024, 65536], P('feat', 'row'), may hold values from 0 to 255
- grads: bfloat16 [65536], P('row'), may hold values from -6 to 6
- hess: bfloat16 [65536], P('row'), may hold values from 0.049804688 to 1
- node: int32 [65536], P('row'), may hold values from 0 to 7
Outputs:
- shortfall: float32 [1024, 8, 256], P(('feat', 'row'))
- best: float32 [8], replicated
The draws below stay inside these ranges and needn't reach their ends.
All inputs are finite; a program needn't handle non-finite values.
Results may differ from the reference program's by a relative error of at most 0.0003.
Values sent between devices are 32-bit elements; how exact they have to be, the bound alone decides.
A program may use at most 64 MiB of HBM per device.

```python
import math
import jax
import jax.numpy as jnp
from jax import lax

FEATURES = 1024
BINS = 256
NODES = 8
ROWS = 65536


def plant(entries, key, smallest, largest):
    dims = entries.shape
    index_at = [jax.random.randint(jax.random.fold_in(key, axis), (), 0, dims[axis]) for axis in range(len(dims))]
    entries = entries.at[tuple(index_at)].set(smallest)
    longest = dims.index(max(dims))
    index_at[longest] = (index_at[longest] + 1) % dims[longest]
    return entries.at[tuple(index_at)].set(largest)


def block_levels(rng, shape, cuts, least, high):
    def one(axis_at, parts):
        steps = jax.random.uniform(jax.random.fold_in(jax.random.fold_in(rng, 6), axis_at), (parts,), jnp.float32, least / len(cuts), high / len(cuts))
        return jnp.repeat(jnp.exp(steps), shape[axis_at] // parts).reshape((-1,) + (1,) * (len(shape) - axis_at - 1))

    level = one(*cuts[0])
    for cut in cuts[1:]:
        level = level * one(*cut)
    return level


def scatter_about(stream_key, dims, spread, reach, split=(), held_as=jnp.bfloat16):
    loudness = block_levels(stream_key, dims, split, -0.22, 0.18) if split else 1.0
    result = jax.random.normal(stream_key, dims, jnp.float32) * spread * loudness
    return jnp.minimum(jnp.maximum(result, -reach), reach).astype(held_as)


def setup_inputs(seed: int = 0) -> dict:
    key_of = jax.random.split(jax.random.key(seed), 5)
    bins = plant(jax.random.randint(key_of[0], (FEATURES, ROWS), 0, BINS), jax.random.fold_in(key_of[0], 1), 0, BINS - 1).astype(jnp.int32)
    grads = scatter_about(key_of[1], (ROWS,), 1.0, 6.0, ((0, 8),))
    hess = jnp.clip(jnp.exp(math.log(1.0) - 2.9996462 * jax.random.uniform(key_of[2], (ROWS,), jnp.float32) ** block_levels(key_of[2], (ROWS,), ((0, 8),), -0.2, 0.2)), 0.049804688, 1.0).astype(jnp.bfloat16)
    node = plant(jax.random.randint(key_of[3], (ROWS,), 0, NODES), jax.random.fold_in(key_of[3], 1), 0, NODES - 1).astype(jnp.int32)
    return dict(bins=bins, grads=grads, hess=hess, node=node)


def reference(bins, grads, hess, node):
    stats = jnp.stack([grads.astype(jnp.float32), hess.astype(jnp.float32)], axis=1)

    def one_feature(column):
        labels = (node * BINS + column).astype(jnp.int32)
        summed = jax.ops.segment_sum(stats, labels, num_segments=NODES * BINS)
        return jnp.transpose(summed.reshape(NODES, BINS, 2), (2, 0, 1))

    hist = lax.map(one_feature, bins)
    totals = jax.ops.segment_sum(stats, node.astype(jnp.int32), num_segments=NODES)
    left = jnp.cumsum(hist, axis=3)
    grad_left = left[:, 0]
    hess_left = left[:, 1]
    grad_total = totals[:, 0][None, :, None]
    hess_total = totals[:, 1][None, :, None]
    gain = grad_left * grad_left / (hess_left + 1.0)
    gain = gain + (grad_total - grad_left) ** 2 / (hess_total - hess_left + 1.0)
    gain = gain - grad_total * grad_total / (hess_total + 1.0)
    best = jnp.max(gain, axis=(0, 2))
    return gain - best[None, :, None], best
```

```python
import functools
import jax
import jax.numpy as jnp
from jax import lax
from jax.experimental import pallas as pl
from jax.experimental.pallas import tpu as pltpu
from jax.sharding import PartitionSpec as P

BINS = 256
NODES = 8
LANES = 128
SUBLANES = 8
LOW = 64
TILE = 256
GROUP = TILE // LOW
HALVES = LANES // LOW
TOPS = BINS // LANES
SLOTS = NODES * TOPS
LINES = 2 * SLOTS
MESH = pl.DeviceIdType.MESH
F8 = jnp.float8_e4m3fn
SLOT = 256
PACK = 4
DIGIT = 32
BLOCKS = SUBLANES // 2
FINE = 16.0
H_SCALE = 256.0


def partner(me, k, n):
    if n & (n - 1):
        return (me + k) % n
    out, weight = 0, 1
    while weight < n:
        out = out + (((me // weight) % 2 + (k // weight) % 2) % 2) * weight
        weight *= 2
    return out


def direct(
    n, m, block, chunks, bins_hbm, node_ref, g_ref, h_ref, out_ref, best_ref,
    bins_buf, high_ref, low_ref, g_all, h_all, acc_ref, stage, landed, row_best, feat_best,
    load_sem, send_sem, recv_sem, row_send, row_recv, feat_send, feat_recv,
):
    rows = bins_buf.shape[2]
    me = lax.axis_index("row")
    mine = lax.axis_index("feat")
    steps = n * chunks
    sent = (n - 1) * chunks

    def place_of(s):
        return (partner(me, n - 1 - s // chunks, n) * chunks + s % chunks) * block

    def load(s):
        start = pl.multiple_of((place_of(s) // SUBLANES) * SUBLANES, SUBLANES)
        return pltpu.make_async_copy(
            bins_hbm.at[pl.ds(start, bins_buf.shape[1]), :], bins_buf.at[s % 2], load_sem.at[s % 2]
        )

    def send(s):
        k = n - 1 - s // chunks
        return pltpu.make_async_remote_copy(
            src_ref=stage.at[s],
            dst_ref=landed.at[s],
            send_sem=send_sem.at[s],
            recv_sem=recv_sem.at[s],
            device_id={"row": partner(me, k, n)},
            device_id_type=MESH,
        )

    load(0).start()
    barrier = pltpu.get_barrier_semaphore()
    for k in range(1, n):
        pl.semaphore_signal(barrier, inc=1, device_id={"row": (me + k) % n}, device_id_type=MESH)
    for k in range(1, m):
        pl.semaphore_signal(barrier, inc=1, device_id={"feat": (mine + k) % m}, device_id_type=MESH)

    g = g_ref[...].astype(jnp.float32)
    h = h_ref[...].astype(jnp.float32)
    for i in range(rows // LANES):
        cols = slice(i * LANES, (i + 1) * LANES)
        g_all[:, cols] = jnp.broadcast_to(g[i : i + 1, :], (SLOTS, LANES)).astype(jnp.bfloat16)
        h_all[:, cols] = jnp.broadcast_to(h[i : i + 1, :], (SLOTS, LANES)).astype(jnp.bfloat16)
    pl.semaphore_wait(barrier, n + m - 2)

    def step(s, carry):
        load(s).wait()

        @pl.when(s + 1 < steps)
        def _():
            load(s + 1).start()

        @pl.when((s >= 1) & (s <= sent))
        def _():
            send(s - 1).start()

        offset = 0 if block % SUBLANES == 0 else place_of(s) % SUBLANES
        bins = bins_buf[s % 2]
        upper = bins >= LANES
        rest = jnp.where(upper, bins - LANES, bins)
        second = rest >= LOW
        slot = node_ref[...] + jnp.where(upper, NODES, 0)
        high_ref[...] = jnp.where(second, slot + SLOTS, slot).astype(jnp.float32)
        low_ref[...] = jnp.where(second, rest - LOW, rest).astype(jnp.float32)
        place = lax.broadcasted_iota(jnp.int32, (SLOTS, rows), 0).astype(jnp.bfloat16)
        zero = jnp.zeros((SLOTS, rows), jnp.bfloat16)
        one = jnp.ones((SLOTS, rows), jnp.bfloat16)
        for first in range(0, block, GROUP):
            left, right = [], []
            for f in range(first, first + GROUP):
                row = pl.ds(offset + f, 1)
                high = jnp.broadcast_to(high_ref[row, :], (SLOTS, rows)).astype(jnp.bfloat16)
                low = jnp.broadcast_to(low_ref[row, :], (SLOTS, rows)).astype(jnp.bfloat16)
                for j in range(HALVES):
                    here = high == place + jnp.asarray(SLOTS * j, jnp.bfloat16)
                    left += [jnp.where(here, g_all[...], zero), jnp.where(here, h_all[...], zero)]
                for j in range(LOW // SLOTS):
                    here = low == place + jnp.asarray(SLOTS * j, jnp.bfloat16)
                    right.append(jnp.where(here, one, zero))
            acc_ref[...] = lax.dot_general(
                jnp.concatenate(left, 0),
                jnp.concatenate(right, 0),
                (((1,), (1,)), ((), ())),
                preferred_element_type=jnp.float32,
            )
            for i in range(GROUP):
                parts = []
                for j in range(HALVES):
                    top = (i * HALVES + j) * LINES
                    parts.append(acc_ref[top : top + LINES, i * LOW : (i + 1) * LOW])
                stage[s, first + i] = jnp.concatenate(parts, 1)
        return carry

    lax.fori_loop(0, steps, step, 0)

    def drain(s, carry):
        send(s).wait()
        return carry

    lax.fori_loop(0, sent, drain, 0)

    lane = lax.broadcasted_iota(jnp.int32, (block * 2 * TOPS * NODES, LANES), 1)

    def finish(c, top_gain):
        def add(k, total):
            return total + landed[k * chunks + c]

        x = lax.fori_loop(0, n - 1, add, stage[sent + c])
        x = x.reshape(block * LINES, LANES)
        shift = 1
        while shift < LANES:
            x = x + jnp.where(lane >= shift, pltpu.roll(x, shift, 1), 0.0)
            shift *= 2
        x = x.reshape(block, 2, TOPS, NODES, LANES)
        left, total = [], jnp.zeros((block, 2, NODES, LANES), jnp.float32)
        for t in range(TOPS):
            left.append(x[:, :, t] + total)
            total = total + jnp.broadcast_to(x[:, :, t, :, LANES - 1 :], total.shape)
        gt, ht = total[:, 0], total[:, 1]
        base = gt * gt / (ht + 1.0)
        for t in range(TOPS):
            gl, hl = left[t][:, 0], left[t][:, 1]
            gain = gl * gl / (hl + 1.0)
            gain = gain + (gt - gl) * (gt - gl) / (ht - hl + 1.0)
            gain = gain - base
            out_ref[pl.ds(c * block, block), :, t * LANES : (t + 1) * LANES] = gain
            top_gain = jnp.maximum(top_gain, jnp.max(gain, axis=0))
        return top_gain

    top_gain = lax.fori_loop(0, chunks, finish, jnp.full((NODES, LANES), -jnp.inf, jnp.float32))

    def exchange(value, slots, count, axis, index, sems, arrived):
        slots[0] = jnp.broadcast_to(jnp.max(value, axis=1, keepdims=True), (NODES, LANES))
        copies = []
        for k in range(1, count):
            copies.append(
                pltpu.make_async_remote_copy(
                    src_ref=slots.at[0],
                    dst_ref=slots.at[k],
                    send_sem=sems.at[k - 1],
                    recv_sem=arrived.at[k - 1],
                    device_id={axis: (index + k) % count},
                    device_id_type=MESH,
                )
            )
            copies[-1].start()
        for copy in copies:
            copy.wait()
        best = slots[0]
        for k in range(1, count):
            best = jnp.maximum(best, slots[k])
        return best

    best = exchange(top_gain, row_best, n, "row", me, row_send, row_recv)
    best = exchange(best, feat_best, m, "feat", mine, feat_send, feat_recv)
    across = lax.broadcasted_iota(jnp.int32, (NODES, LANES), 1)
    down = lax.broadcasted_iota(jnp.int32, (NODES, LANES), 0)
    flat = jnp.max(jnp.where(across == down, best, -jnp.inf), axis=0, keepdims=True)
    best_ref[...] = flat[:, :NODES]


def regroup(
    bins_hbm, node_ref, g_ref, h_ref, words_ref, gh_ref, keep_ref, last_ref,
    bins, pieces, pattern, spots_v, spots_s, load_sem, spots_sem,
):
    f32, bf16, i32 = jnp.float32, jnp.bfloat16, jnp.int32
    tiles = node_ref.shape[0]
    groups, features = bins.shape[:2]
    slots = words_ref.shape[0] // 2

    def load(t):
        return pltpu.make_async_copy(bins_hbm.at[pl.ds(t * features, features), :], bins.at[t], load_sem.at[t])

    for t in range(groups):
        load(t).start()
    node = node_ref[...]
    g = g_ref[...].astype(f32)
    h = h_ref[...].astype(f32)
    top = jnp.max(jnp.max(jnp.abs(g), axis=0, keepdims=True), axis=1, keepdims=True)
    top = jnp.broadcast_to(top, (SUBLANES, LANES))
    scale = jnp.ones((SUBLANES, LANES), f32)
    back = jnp.ones((SUBLANES, LANES), f32)
    for k in (32, 16, 8, 4, 2, 1):
        fits = top * (scale * 2.0**k) <= 448.0
        scale = jnp.where(fits, scale * 2.0**k, scale)
        back = jnp.where(fits, back * 2.0**-k, back)

    def split(x):
        coarse = x.astype(F8).astype(f32)
        return coarse, (x - coarse) * FINE

    for i, piece in enumerate(split(g * scale[:1]) + split(h * H_SCALE)):
        pieces[i] = piece

    row = lax.broadcasted_iota(i32, (LANES, LANES), 0)
    col = lax.broadcasted_iota(i32, (LANES, LANES), 1)
    upper = jnp.where(row <= col, 1.0, 0.0).astype(bf16)
    ones = jnp.ones((LANES, LANES), bf16)
    above = lax.broadcasted_iota(i32, (tiles, tiles), 1) < lax.broadcasted_iota(i32, (tiles, tiles), 0)
    lower = jnp.where(above, 1.0, 0.0).astype(bf16)
    dot = functools.partial(jnp.dot, preferred_element_type=f32)
    lane = lax.broadcasted_iota(i32, (tiles, LANES), 1)
    slot = lax.broadcasted_iota(i32, keep_ref.shape, 0)
    keep = jnp.ones(keep_ref.shape, f32)
    base = jnp.zeros((1, LANES), i32)
    last = jnp.zeros((1, LANES), i32)
    dest = jnp.zeros((tiles, LANES), i32)
    spots = jnp.zeros((tiles, LANES), i32)
    for n in range(NODES):
        hit = node == n
        x = jnp.where(hit, 1.0, 0.0).astype(bf16)
        rank = dot(x, upper).astype(i32)
        count = dot(x, ones)
        ahead = dot(lower, count.astype(bf16)).astype(i32)
        count = count.astype(i32)
        total = (ahead + count)[tiles - 1 : tiles]
        start = ahead + base
        dest = jnp.where(hit, start + rank - 1, dest)
        spots = jnp.where(lane == n, start, jnp.where(lane == NODES + n, start + count, spots))
        keep = jnp.where(slot * SLOT == base, 0.0, keep)
        base = base + jnp.maximum((total + (SLOT - 1)) // SLOT, 1) * SLOT
        last = jnp.where(lane[:1] == n, base // SLOT - 1, last)
    keep_ref[...] = jnp.where(slot == slots, jnp.broadcast_to(back[:1], keep_ref.shape), keep)
    last_ref[...] = last
    spots_v[...] = spots
    to_scalar = pltpu.make_async_copy(spots_v, spots_s, spots_sem)
    to_scalar.start()

    spot = dest & (LANES - 1)
    sub = lax.broadcasted_iota(i32, (NODES, LANES), 0)
    across = lax.broadcasted_iota(i32, (NODES, LANES), 1)
    none = jnp.zeros((NODES, LANES), i32)
    for b in range(0, tiles, 2):
        left, right = [], []
        for i in range(2):
            here = jnp.where(jnp.broadcast_to(node[b + i : b + i + 1], (NODES, LANES)) == sub, across, 0)
            left.append(jnp.concatenate([none] * i + [here] + [none] * (1 - i), 1))
            right.append(jnp.where(jnp.broadcast_to(spot[b + i : b + i + 1], (LANES, LANES)) == row, 1.0, 0.0))
        found = lax.dot_general(
            jnp.concatenate(left, 0).astype(f32).astype(bf16),
            jnp.concatenate(right, 1).astype(bf16),
            (((1,), (1,)), ((), ())),
            preferred_element_type=f32,
        ).astype(i32)
        pattern[b] = found[:NODES]
        pattern[b + 1] = found[NODES:]
    gh_ref[...] = jnp.zeros(gh_ref.shape, f32)
    to_scalar.wait()
    for t in range(groups):
        load(t).wait()

    def place(b, carry):
        cols = pl.ds(pl.multiple_of(b * LANES, LANES), LANES)
        words = []
        for t in range(groups):
            word = bins[t, :SUBLANES, cols]
            for k in range(1, PACK):
                word = word | lax.shift_left(bins[t, SUBLANES * k : SUBLANES * (k + 1), cols], 8 * k)
            words.append(word)
        piece = [jnp.broadcast_to(pieces[i, pl.ds(b, 1), :], (SUBLANES, LANES)) for i in range(4)]
        gh = jnp.where(sub == 0, piece[0], jnp.where(sub == 1, piece[1], jnp.where(sub == 2, piece[2], piece[3])))
        for n in range(NODES):
            first = spots_s[b, n]
            tile = lax.shift_right_logical(first, 7)
            low = first & (LANES - 1)
            high = low + spots_s[b, NODES + n] - first
            source = jnp.broadcast_to(pattern[b, n : n + 1, :], (SUBLANES, LANES))
            near = (across >= low) & (across < high)
            far = across < high - LANES
            for t in range(groups):
                moved = jnp.take_along_axis(words[t], source, axis=1)
                pltpu.store(words_ref.at[tile, t], moved, mask=near)
                pltpu.store(words_ref.at[tile + 1, t], moved, mask=far)
            moved = jnp.take_along_axis(gh, source, axis=1)
            pltpu.store(gh_ref.at[tile], moved, mask=near)
            pltpu.store(gh_ref.at[tile + 1], moved, mask=far)
        return carry

    lax.fori_loop(0, tiles, place, 0, unroll=8)


def sweep(
    n, m, words_hbm, gh_ref, keep_ref, last_ref, out_ref, best_ref,
    words, keys, gh, snap, stage, near, relay, far, own, row_best, feat_best,
    load_sem, near_send, near_recv, far_send, far_recv, row_send, row_recv, feat_send, feat_recv,
):
    f32 = jnp.float32
    tiles = words.shape[1]
    slots = tiles * LANES // SLOT
    pairs = n // 2
    me = lax.axis_index("row")
    mine = lax.axis_index("feat")
    chip, core = me // 2, me % 2

    def to_chip(k):
        return partner(chip, pairs - 1 - k, pairs)

    def load(t):
        group = 2 * to_chip(t // 2) + (t + 1 + core) % 2
        return pltpu.make_async_copy(
            words_hbm.at[pl.ds(0, tiles), group], words.at[t % 2], load_sem.at[t % 2]
        )

    def send_near(k, i):
        return pltpu.make_async_remote_copy(
            src_ref=stage.at[k, i],
            dst_ref=near.at[k, i],
            send_sem=near_send.at[k, i],
            recv_sem=near_recv.at[k, i],
            device_id={"row": 2 * chip + 1 - core},
            device_id_type=MESH,
        )

    def send_far(k, i):
        return pltpu.make_async_remote_copy(
            src_ref=relay.at[k, i],
            dst_ref=far.at[k, i],
            send_sem=far_send.at[k, i],
            recv_sem=far_recv.at[k, i],
            device_id={"row": 2 * to_chip(k) + core},
            device_id_type=MESH,
        )

    load(0).start()
    barrier = pltpu.get_barrier_semaphore()
    for k in range(1, n):
        pl.semaphore_signal(barrier, inc=1, device_id={"row": (me + k) % n}, device_id_type=MESH)
    for k in range(1, m):
        pl.semaphore_signal(barrier, inc=1, device_id={"feat": (mine + k) % m}, device_id_type=MESH)
    for p in range(4):
        for q in range(tiles):
            gh[p, :, q * LANES : (q + 1) * LANES] = jnp.broadcast_to(gh_ref[q, p : p + 1, :], (32, LANES)).astype(F8)
    pl.semaphore_wait(barrier, n + m - 2)

    wide = (32, SLOT)
    down = lax.broadcasted_iota(jnp.int32, wide, 0) % SUBLANES
    high_at = (down * DIGIT).astype(jnp.int8)
    low_at = [(down + SUBLANES * j).astype(jnp.int8) for j in range(4)]
    zero, one = jnp.zeros(wide, F8), jnp.ones(wide, F8)
    lane = lax.broadcasted_iota(jnp.int32, (SUBLANES, LANES), 1)
    sub = lax.broadcasted_iota(jnp.int32, (SUBLANES, LANES), 0)
    byte = (lane // SUBLANES) % PACK
    of = [byte == f for f in range(PACK - 1)]
    g_back = jnp.broadcast_to(keep_ref[slots : slots + 1, :], (SUBLANES, LANES))
    h_back = jnp.full((SUBLANES, LANES), 1.0 / H_SCALE, f32)

    def unpack(t):
        load(t).wait()

        @pl.when(t + 1 < n)
        def _():
            load(t + 1).start()

        for q in range(tiles):
            word = words[t % 2, q]
            for k in range(PACK):
                keys[k, :, q * LANES : (q + 1) * LANES] = lax.shift_right_logical(word, 8 * k)

    def one_hots(w, cols):
        rows = [jnp.broadcast_to(keys[k, pl.ds(w, 1), cols], (SUBLANES, SLOT)) for k in range(PACK)]
        key = jnp.concatenate(rows, 0).astype(jnp.int8)
        low, high = key & jnp.int8(DIGIT - 1), key & jnp.int8(-DIGIT)
        apart = high != high_at
        left = [jnp.where(apart, zero, gh[p, :, cols]) for p in range(4)]
        right = [jnp.where(low != low_at[j], zero, one) for j in range(4)]
        return left, right

    def block(i):
        total = [jnp.zeros((SUBLANES, LANES), f32) for _ in range(4)]
        for s in range(slots):
            cols = slice(s * SLOT, (s + 1) * SLOT)
            left0, right0 = one_hots(2 * i, cols)
            left1, right1 = one_hots(2 * i + 1, cols)
            found = lax.dot_general(
                jnp.concatenate(left0 + left1, 0),
                jnp.concatenate(right0 + right1, 0),
                (((1,), (1,)), ((), ())),
                preferred_element_type=f32,
            )
            kept = jnp.broadcast_to(keep_ref[s : s + 1, :], (SUBLANES, LANES))
            for q in range(2):
                square = found[q * LANES : (q + 1) * LANES, q * LANES : (q + 1) * LANES]
                dense = []
                for p in range(4):
                    part = [square[32 * p + 8 * f : 32 * p + 8 * f + 8] for f in range(PACK)]
                    dense.append(jnp.where(of[0], part[0], jnp.where(of[1], part[1], jnp.where(of[2], part[2], part[3]))))
                for v in range(2):
                    at = 2 * q + v
                    total[at] = total[at] * kept + (dense[2 * v] + dense[2 * v + 1] * (1.0 / FINE))
                    snap[s, at] = total[at]

    def hist(node, at):
        return snap[last_ref[0, node], at] * (h_back if at % 2 else g_back)

    def pair(k, carry):
        unpack(2 * k)

        def give(i, c):
            @pl.when(i > 0)
            def _():
                send_near(k, i - 1).start()

            @pl.when((i == 0) & (k > 0))
            def _():
                send_far(k - 1, BLOCKS - 1).start()

            block(i)
            for node in range(NODES):
                for at in range(4):
                    stage[k, i, node, at] = hist(node, at)
            return c

        lax.fori_loop(0, BLOCKS, give, 0)
        unpack(2 * k + 1)

        def hold(i, c):
            @pl.when(i == 0)
            def _():
                send_near(k, BLOCKS - 1).start()

            @pl.when((i > 0) & (k < pairs - 1))
            def _():
                send_far(k, i - 1).start()

            block(i)
            send_near(k, i).wait_recv()

            @pl.when(k < pairs - 1)
            def _():
                for node in range(NODES):
                    for at in range(4):
                        relay[k, i, node, at] = hist(node, at) + near[k, i, node, at]

            @pl.when(k == pairs - 1)
            def _():
                for node in range(NODES):
                    for at in range(4):
                        own[i, node, at] = hist(node, at) + near[k, i, node, at]

            return c

        lax.fori_loop(0, BLOCKS, hold, 0)
        return carry

    lax.fori_loop(0, pairs, pair, 0)

    def take(x, index):
        return jnp.take_along_axis(x, index, axis=1)

    tens, units = lane // (SUBLANES * PACK), lane % SUBLANES
    end_of_run = lane - units + (SUBLANES - 1)
    end_of_row = (LANES - DIGIT) + byte * SUBLANES + (SUBLANES - 1)

    def running(x):
        for shift in (1, 2, 4):
            x = x + jnp.where(units >= shift, pltpu.roll(x, shift, 1), 0.0)
        run = take(x, end_of_run)
        for j in range(1, 4):
            x = x + jnp.where(tens >= j, pltpu.roll(run, j * DIGIT, 1), 0.0)
        row = take(x, end_of_row)
        whole = row
        for shift in (1, 2, 4):
            whole = whole + jnp.where(sub >= shift, pltpu.roll(whole, shift, 0), 0.0)
        return x + (whole - row), jnp.broadcast_to(whole[SUBLANES - 1 :], whole.shape)

    def finish(i, best):
        for k in range(pairs - 1):
            send_far(k, i).wait_recv()
        for q in range(2):
            gains = []
            for node in range(NODES):
                sums = []
                for at in (2 * q, 2 * q + 1):
                    x = own[i, node, at]
                    for k in range(pairs - 1):
                        x = x + far[k, i, node, at]
                    sums.append(running(x))
                (gl, gt), (hl, ht) = sums
                gain = gl * gl / (hl + 1.0)
                gain = gain + (gt - gl) * (gt - gl) / (ht - hl + 1.0)
                gains.append(gain - gt * gt / (ht + 1.0))
            best = jnp.maximum(best, jnp.stack([jnp.max(x, axis=0) for x in gains], 0))
            turned = jnp.swapaxes(jnp.stack(gains, 0), 0, 1)
            for f in range(PACK):
                source = ((lane // SUBLANES) % 4) * DIGIT + f * SUBLANES + units
                for t in range(TOPS):
                    part = [take(turned[4 * t + j], source) for j in range(4)]
                    line = jnp.where(tens == 0, part[0], jnp.where(tens == 1, part[1], jnp.where(tens == 2, part[2], part[3])))
                    out_ref[SUBLANES * f + 2 * i + q, :, t * LANES : (t + 1) * LANES] = line
        return best

    top_gain = lax.fori_loop(0, BLOCKS, finish, jnp.full((NODES, LANES), -jnp.inf, f32))

    def exchange(value, slots, count, axis, index, sems, arrived):
        slots[0] = jnp.broadcast_to(jnp.max(value, axis=1, keepdims=True), (NODES, LANES))
        copies = []
        for k in range(1, count):
            copies.append(
                pltpu.make_async_remote_copy(
                    src_ref=slots.at[0],
                    dst_ref=slots.at[k],
                    send_sem=sems.at[k - 1],
                    recv_sem=arrived.at[k - 1],
                    device_id={axis: (index + k) % count},
                    device_id_type=MESH,
                )
            )
            copies[-1].start()
        for copy in copies:
            copy.wait()
        best = slots[0]
        for k in range(1, count):
            best = jnp.maximum(best, slots[k])
        return best

    best = exchange(top_gain, row_best, n, "row", me, row_send, row_recv)
    best = exchange(best, feat_best, m, "feat", mine, feat_send, feat_recv)
    flat = jnp.max(jnp.where(lane == sub, best, -jnp.inf), axis=0, keepdims=True)
    best_ref[...] = flat[:, :NODES]

    def drain(k, carry):
        for i in range(BLOCKS):
            send_near(k, i).wait_send()

            @pl.when(k < pairs - 1)
            def _():
                send_far(k, i).wait_send()

        return carry

    lax.fori_loop(0, pairs, drain, 0)


def grouped(n, m, bins, grads, hess, node):
    features, rows = bins.shape
    groups, tiles = features // 32, rows // LANES
    slots = rows // SLOT + NODES - 1
    held = 2 * slots
    vmem = pl.BlockSpec(memory_space=pltpu.VMEM)
    smem = pl.BlockSpec(memory_space=pltpu.SMEM)
    hbm = pl.BlockSpec(memory_space=pl.ANY)
    words, gh, keep, last = pl.pallas_call(
        regroup,
        in_specs=[hbm, vmem, vmem, vmem],
        out_specs=(vmem, vmem, vmem, vmem),
        out_shape=(
            jax.ShapeDtypeStruct((held + 1, groups, SUBLANES, LANES), jnp.int32),
            jax.ShapeDtypeStruct((held + 1, SUBLANES, LANES), jnp.float32),
            jax.ShapeDtypeStruct((-(-(slots + 1) // SUBLANES) * SUBLANES, LANES), jnp.float32),
            jax.ShapeDtypeStruct((1, LANES), jnp.int32),
        ),
        scratch_shapes=[
            pltpu.VMEM((groups, 32, rows), jnp.int32),
            pltpu.VMEM((4, tiles, LANES), jnp.float32),
            pltpu.VMEM((tiles, NODES, LANES), jnp.int32),
            pltpu.VMEM((tiles, LANES), jnp.int32),
            pltpu.SMEM((tiles, LANES), jnp.int32),
            pltpu.SemaphoreType.DMA((groups,)),
            pltpu.SemaphoreType.DMA,
        ],
        compiler_params=pltpu.CompilerParams(vmem_limit_bytes=56 << 20),
    )(bins, node.reshape(-1, LANES), grads.reshape(-1, LANES), hess.reshape(-1, LANES))
    pairs = n // 2
    piece = (BLOCKS, NODES, 4, SUBLANES, LANES)
    out, best = pl.pallas_call(
        functools.partial(sweep, n, m),
        in_specs=[hbm, vmem, vmem, smem],
        out_specs=(vmem, vmem),
        out_shape=(
            jax.ShapeDtypeStruct((32, NODES, BINS), jnp.float32),
            jax.ShapeDtypeStruct((1, NODES), jnp.float32),
        ),
        scratch_shapes=[
            pltpu.VMEM((2, held, SUBLANES, LANES), jnp.int32),
            pltpu.VMEM((PACK, SUBLANES, held * LANES), jnp.int32),
            pltpu.VMEM((4, 32, held * LANES), F8),
            pltpu.VMEM((slots, 4, SUBLANES, LANES), jnp.float32),
            pltpu.VMEM((pairs,) + piece, jnp.float32),
            pltpu.VMEM((pairs,) + piece, jnp.float32),
            pltpu.VMEM((pairs - 1,) + piece, jnp.float32),
            pltpu.VMEM((pairs - 1,) + piece, jnp.float32),
            pltpu.VMEM(piece, jnp.float32),
            pltpu.VMEM((n, NODES, LANES), jnp.float32),
            pltpu.VMEM((m, NODES, LANES), jnp.float32),
            pltpu.SemaphoreType.DMA((2,)),
            pltpu.SemaphoreType.DMA((pairs, BLOCKS)),
            pltpu.SemaphoreType.DMA((pairs, BLOCKS)),
            pltpu.SemaphoreType.DMA((pairs - 1, BLOCKS)),
            pltpu.SemaphoreType.DMA((pairs - 1, BLOCKS)),
            pltpu.SemaphoreType.DMA((n - 1,)),
            pltpu.SemaphoreType.DMA((n - 1,)),
            pltpu.SemaphoreType.DMA((m - 1,)),
            pltpu.SemaphoreType.DMA((m - 1,)),
        ],
        compiler_params=pltpu.CompilerParams(
            collective_id=0, has_side_effects=True, vmem_limit_bytes=56 << 20
        ),
    )(words, gh, keep, last)
    best = best.reshape(NODES)
    return out - best[None, :, None], best


def solution(mesh):
    n, m = mesh.shape["row"], mesh.shape["feat"]

    def per_device(bins, grads, hess, node):
        features, rows = bins.shape
        own = features // n
        if own == 32 and n % 2 == 0 and n > 2 and rows % (2 * SLOT) == 0:
            return grouped(n, m, bins, grads, hess, node)
        block = own if own < SUBLANES else next(b for b in (2 * SUBLANES, SUBLANES) if own % b == 0)
        held = max(block, SUBLANES)
        chunks = own // block
        vmem = pl.BlockSpec(memory_space=pltpu.VMEM)
        piece = (block, LINES, LANES)
        out, best = pl.pallas_call(
            functools.partial(direct, n, m, block, chunks),
            in_specs=[pl.BlockSpec(memory_space=pl.ANY), vmem, vmem, vmem],
            out_specs=(vmem, vmem),
            out_shape=(
                jax.ShapeDtypeStruct((own, NODES, BINS), jnp.float32),
                jax.ShapeDtypeStruct((1, NODES), jnp.float32),
            ),
            scratch_shapes=[
                pltpu.VMEM((2, held, rows), jnp.int32),
                pltpu.VMEM((held, rows), jnp.float32),
                pltpu.VMEM((held, rows), jnp.float32),
                pltpu.VMEM((SLOTS, rows), jnp.bfloat16),
                pltpu.VMEM((SLOTS, rows), jnp.bfloat16),
                pltpu.VMEM((GROUP * HALVES * LINES, TILE), jnp.float32),
                pltpu.VMEM((n * chunks,) + piece, jnp.float32),
                pltpu.VMEM(((n - 1) * chunks,) + piece, jnp.float32),
                pltpu.VMEM((n, NODES, LANES), jnp.float32),
                pltpu.VMEM((m, NODES, LANES), jnp.float32),
                pltpu.SemaphoreType.DMA((2,)),
                pltpu.SemaphoreType.DMA(((n - 1) * chunks,)),
                pltpu.SemaphoreType.DMA(((n - 1) * chunks,)),
                pltpu.SemaphoreType.DMA((n - 1,)),
                pltpu.SemaphoreType.DMA((n - 1,)),
                pltpu.SemaphoreType.DMA((m - 1,)),
                pltpu.SemaphoreType.DMA((m - 1,)),
            ],
            compiler_params=pltpu.CompilerParams(
                collective_id=0, has_side_effects=True, vmem_limit_bytes=56 << 20
            ),
        )(bins, node.reshape(1, rows), grads.reshape(-1, LANES), hess.reshape(-1, LANES))
        best = best.reshape(NODES)
        return out - best[None, :, None], best

    return jax.shard_map(
        per_device,
        mesh=mesh,
        in_specs=(P("feat", "row"), P("row"), P("row"), P("row")),
        out_specs=(P(("feat", "row"), None, None), P()),
        check_vma=False,
    )
```

```python
import functools
import jax
import jax.numpy as jnp
from jax import lax
from jax.experimental import pallas as pl
from jax.experimental.pallas import tpu as pltpu
from jax.sharding import PartitionSpec as P

BINS = 256
NODES = 8
LANES = 128
SUBLANES = 8
LOW = 64
TILE = 256
GROUP = TILE // LOW
HALVES = LANES // LOW
TOPS = BINS // LANES
SLOTS = NODES * TOPS
LINES = 2 * SLOTS
MESH = pl.DeviceIdType.MESH
F8 = jnp.float8_e4m3fn
SLOT = 256
PACK = 4
DIGIT = 32
BLOCKS = SUBLANES // 2


def partner(me, k, n):
    if n & (n - 1):
        return (me + k) % n
    out, weight = 0, 1
    while weight < n:
        out = out + (((me // weight) % 2 + (k // weight) % 2) % 2) * weight
        weight *= 2
    return out


def direct(
    n, m, block, chunks, bins_hbm, node_ref, g_ref, h_ref, out_ref, best_ref,
    bins_buf, high_ref, low_ref, g_all, h_all, acc_ref, stage, landed, row_best, feat_best,
    load_sem, send_sem, recv_sem, row_send, row_recv, feat_send, feat_recv,
):
    rows = bins_buf.shape[2]
    me = lax.axis_index("row")
    mine = lax.axis_index("feat")
    steps = n * chunks
    sent = (n - 1) * chunks

    def place_of(s):
        return (partner(me, n - 1 - s // chunks, n) * chunks + s % chunks) * block

    def load(s):
        start = pl.multiple_of((place_of(s) // SUBLANES) * SUBLANES, SUBLANES)
        return pltpu.make_async_copy(
            bins_hbm.at[pl.ds(start, bins_buf.shape[1]), :], bins_buf.at[s % 2], load_sem.at[s % 2]
        )

    def send(s):
        k = n - 1 - s // chunks
        return pltpu.make_async_remote_copy(
            src_ref=stage.at[s],
            dst_ref=landed.at[s],
            send_sem=send_sem.at[s],
            recv_sem=recv_sem.at[s],
            device_id={"row": partner(me, k, n)},
            device_id_type=MESH,
        )

    load(0).start()
    barrier = pltpu.get_barrier_semaphore()
    for k in range(1, n):
        pl.semaphore_signal(barrier, inc=1, device_id={"row": (me + k) % n}, device_id_type=MESH)
    for k in range(1, m):
        pl.semaphore_signal(barrier, inc=1, device_id={"feat": (mine + k) % m}, device_id_type=MESH)

    g = g_ref[...].astype(jnp.float32)
    h = h_ref[...].astype(jnp.float32)
    for i in range(rows // LANES):
        cols = slice(i * LANES, (i + 1) * LANES)
        g_all[:, cols] = jnp.broadcast_to(g[i : i + 1, :], (SLOTS, LANES)).astype(jnp.bfloat16)
        h_all[:, cols] = jnp.broadcast_to(h[i : i + 1, :], (SLOTS, LANES)).astype(jnp.bfloat16)
    pl.semaphore_wait(barrier, n + m - 2)

    def step(s, carry):
        load(s).wait()

        @pl.when(s + 1 < steps)
        def _():
            load(s + 1).start()

        @pl.when((s >= 1) & (s <= sent))
        def _():
            send(s - 1).start()

        offset = 0 if block % SUBLANES == 0 else place_of(s) % SUBLANES
        bins = bins_buf[s % 2]
        upper = bins >= LANES
        rest = jnp.where(upper, bins - LANES, bins)
        second = rest >= LOW
        slot = node_ref[...] + jnp.where(upper, NODES, 0)
        high_ref[...] = jnp.where(second, slot + SLOTS, slot).astype(jnp.float32)
        low_ref[...] = jnp.where(second, rest - LOW, rest).astype(jnp.float32)
        place = lax.broadcasted_iota(jnp.int32, (SLOTS, rows), 0).astype(jnp.bfloat16)
        zero = jnp.zeros((SLOTS, rows), jnp.bfloat16)
        one = jnp.ones((SLOTS, rows), jnp.bfloat16)
        for first in range(0, block, GROUP):
            left, right = [], []
            for f in range(first, first + GROUP):
                row = pl.ds(offset + f, 1)
                high = jnp.broadcast_to(high_ref[row, :], (SLOTS, rows)).astype(jnp.bfloat16)
                low = jnp.broadcast_to(low_ref[row, :], (SLOTS, rows)).astype(jnp.bfloat16)
                for j in range(HALVES):
                    here = high == place + jnp.asarray(SLOTS * j, jnp.bfloat16)
                    left += [jnp.where(here, g_all[...], zero), jnp.where(here, h_all[...], zero)]
                for j in range(LOW // SLOTS):
                    here = low == place + jnp.asarray(SLOTS * j, jnp.bfloat16)
                    right.append(jnp.where(here, one, zero))
            acc_ref[...] = lax.dot_general(
                jnp.concatenate(left, 0),
                jnp.concatenate(right, 0),
                (((1,), (1,)), ((), ())),
                preferred_element_type=jnp.float32,
            )
            for i in range(GROUP):
                parts = []
                for j in range(HALVES):
                    top = (i * HALVES + j) * LINES
                    parts.append(acc_ref[top : top + LINES, i * LOW : (i + 1) * LOW])
                stage[s, first + i] = jnp.concatenate(parts, 1)
        return carry

    lax.fori_loop(0, steps, step, 0)

    def drain(s, carry):
        send(s).wait()
        return carry

    lax.fori_loop(0, sent, drain, 0)

    lane = lax.broadcasted_iota(jnp.int32, (block * 2 * TOPS * NODES, LANES), 1)

    def finish(c, top_gain):
        def add(k, total):
            return total + landed[k * chunks + c]

        x = lax.fori_loop(0, n - 1, add, stage[sent + c])
        x = x.reshape(block * LINES, LANES)
        shift = 1
        while shift < LANES:
            x = x + jnp.where(lane >= shift, pltpu.roll(x, shift, 1), 0.0)
            shift *= 2
        x = x.reshape(block, 2, TOPS, NODES, LANES)
        left, total = [], jnp.zeros((block, 2, NODES, LANES), jnp.float32)
        for t in range(TOPS):
            left.append(x[:, :, t] + total)
            total = total + jnp.broadcast_to(x[:, :, t, :, LANES - 1 :], total.shape)
        gt, ht = total[:, 0], total[:, 1]
        base = gt * gt / (ht + 1.0)
        for t in range(TOPS):
            gl, hl = left[t][:, 0], left[t][:, 1]
            gain = gl * gl / (hl + 1.0)
            gain = gain + (gt - gl) * (gt - gl) / (ht - hl + 1.0)
            gain = gain - base
            out_ref[pl.ds(c * block, block), :, t * LANES : (t + 1) * LANES] = gain
            top_gain = jnp.maximum(top_gain, jnp.max(gain, axis=0))
        return top_gain

    top_gain = lax.fori_loop(0, chunks, finish, jnp.full((NODES, LANES), -jnp.inf, jnp.float32))

    def exchange(value, slots, count, axis, index, sems, arrived):
        slots[0] = jnp.broadcast_to(jnp.max(value, axis=1, keepdims=True), (NODES, LANES))
        copies = []
        for k in range(1, count):
            copies.append(
                pltpu.make_async_remote_copy(
                    src_ref=slots.at[0],
                    dst_ref=slots.at[k],
                    send_sem=sems.at[k - 1],
                    recv_sem=arrived.at[k - 1],
                    device_id={axis: (index + k) % count},
                    device_id_type=MESH,
                )
            )
            copies[-1].start()
        for copy in copies:
            copy.wait()
        best = slots[0]
        for k in range(1, count):
            best = jnp.maximum(best, slots[k])
        return best

    best = exchange(top_gain, row_best, n, "row", me, row_send, row_recv)
    best = exchange(best, feat_best, m, "feat", mine, feat_send, feat_recv)
    across = lax.broadcasted_iota(jnp.int32, (NODES, LANES), 1)
    down = lax.broadcasted_iota(jnp.int32, (NODES, LANES), 0)
    flat = jnp.max(jnp.where(across == down, best, -jnp.inf), axis=0, keepdims=True)
    best_ref[...] = flat[:, :NODES]


def regroup(
    bins_hbm, node_ref, g_ref, h_ref, words_ref, gh_ref, keep_ref, last_ref,
    bins, pieces, pattern, spots_v, spots_s, load_sem, spots_sem,
):
    f32, bf16, i32 = jnp.float32, jnp.bfloat16, jnp.int32
    tiles = node_ref.shape[0]
    groups, features = bins.shape[:2]

    def load(t):
        return pltpu.make_async_copy(bins_hbm.at[pl.ds(t * features, features), :], bins.at[t], load_sem.at[t])

    for t in range(groups):
        load(t).start()
    node = node_ref[...]
    pieces[0] = g_ref[...].astype(f32)
    pieces[1] = h_ref[...].astype(f32)
    row = lax.broadcasted_iota(i32, (LANES, LANES), 0)
    col = lax.broadcasted_iota(i32, (LANES, LANES), 1)
    upper = jnp.where(row <= col, 1.0, 0.0).astype(bf16)
    ones = jnp.ones((LANES, LANES), bf16)
    above = lax.broadcasted_iota(i32, (tiles, tiles), 1) < lax.broadcasted_iota(i32, (tiles, tiles), 0)
    lower = jnp.where(above, 1.0, 0.0).astype(bf16)
    dot = functools.partial(jnp.dot, preferred_element_type=f32)
    lane = lax.broadcasted_iota(i32, (tiles, LANES), 1)
    slot = lax.broadcasted_iota(i32, keep_ref.shape, 0)
    keep = jnp.ones(keep_ref.shape, f32)
    base = jnp.zeros((1, LANES), i32)
    last = jnp.zeros((1, LANES), i32)
    dest = jnp.zeros((tiles, LANES), i32)
    spots = jnp.zeros((tiles, LANES), i32)
    for n in range(NODES):
        hit = node == n
        x = jnp.where(hit, 1.0, 0.0).astype(bf16)
        rank = dot(x, upper).astype(i32)
        count = dot(x, ones)
        ahead = dot(lower, count.astype(bf16)).astype(i32)
        count = count.astype(i32)
        total = (ahead + count)[tiles - 1 : tiles]
        start = ahead + base
        dest = jnp.where(hit, start + rank - 1, dest)
        spots = jnp.where(lane == n, start, jnp.where(lane == NODES + n, start + count, spots))
        keep = jnp.where(slot * SLOT == base, 0.0, keep)
        base = base + jnp.maximum((total + (SLOT - 1)) // SLOT, 1) * SLOT
        last = jnp.where(lane[:1] == n, base // SLOT - 1, last)
    keep_ref[...] = keep
    last_ref[...] = last
    spots_v[...] = spots
    to_scalar = pltpu.make_async_copy(spots_v, spots_s, spots_sem)
    to_scalar.start()

    spot = dest & (LANES - 1)
    sub = lax.broadcasted_iota(i32, (NODES, LANES), 0)
    across = lax.broadcasted_iota(i32, (NODES, LANES), 1)
    none = jnp.zeros((NODES, LANES), i32)
    for b in range(0, tiles, 2):
        left, right = [], []
        for i in range(2):
            here = jnp.where(jnp.broadcast_to(node[b + i : b + i + 1], (NODES, LANES)) == sub, across, 0)
            left.append(jnp.concatenate([none] * i + [here] + [none] * (1 - i), 1))
            right.append(jnp.where(jnp.broadcast_to(spot[b + i : b + i + 1], (LANES, LANES)) == row, 1.0, 0.0))
        found = lax.dot_general(
            jnp.concatenate(left, 0).astype(f32).astype(bf16),
            jnp.concatenate(right, 1).astype(bf16),
            (((1,), (1,)), ((), ())),
            preferred_element_type=f32,
        ).astype(i32)
        pattern[b] = found[:NODES]
        pattern[b + 1] = found[NODES:]
    gh_ref[...] = jnp.zeros(gh_ref.shape, f32)
    to_scalar.wait()
    for t in range(groups):
        load(t).wait()

    def place(b, carry):
        cols = pl.ds(pl.multiple_of(b * LANES, LANES), LANES)
        words = []
        for t in range(groups):
            word = bins[t, :SUBLANES, cols]
            for k in range(1, PACK):
                word = word | lax.shift_left(bins[t, SUBLANES * k : SUBLANES * (k + 1), cols], 8 * k)
            words.append(word)
        piece = [jnp.broadcast_to(pieces[i, pl.ds(b, 1), :], (SUBLANES, LANES)) for i in range(2)]
        gh = jnp.where(sub == 0, piece[0], piece[1])
        for n in range(NODES):
            first = spots_s[b, n]
            tile = lax.shift_right_logical(first, 7)
            low = first & (LANES - 1)
            high = low + spots_s[b, NODES + n] - first
            source = jnp.broadcast_to(pattern[b, n : n + 1, :], (SUBLANES, LANES))
            near = (across >= low) & (across < high)
            far = across < high - LANES
            for t in range(groups):
                moved = jnp.take_along_axis(words[t], source, axis=1)
                pltpu.store(words_ref.at[tile, t], moved, mask=near)
                pltpu.store(words_ref.at[tile + 1, t], moved, mask=far)
            moved = jnp.take_along_axis(gh, source, axis=1)
            pltpu.store(gh_ref.at[tile], moved, mask=near)
            pltpu.store(gh_ref.at[tile + 1], moved, mask=far)
        return carry

    lax.fori_loop(0, tiles, place, 0, unroll=8)


def sweep(
    n, m, words_hbm, gh_ref, keep_ref, last_ref, out_ref, best_ref,
    words, keys, gh, snap, stage, near, relay, far, own, row_best, feat_best,
    load_sem, near_send, near_recv, far_send, far_recv, row_send, row_recv, feat_send, feat_recv,
):
    f32 = jnp.float32
    tiles = words.shape[1]
    slots = tiles * LANES // SLOT
    pairs = n // 2
    me = lax.axis_index("row")
    mine = lax.axis_index("feat")
    chip, core = me // 2, me % 2

    def to_chip(k):
        return partner(chip, pairs - 1 - k, pairs)

    def load(t):
        group = 2 * to_chip(t // 2) + (t + 1 + core) % 2
        return pltpu.make_async_copy(
            words_hbm.at[pl.ds(0, tiles), group], words.at[t % 2], load_sem.at[t % 2]
        )

    def send_near(k, i):
        return pltpu.make_async_remote_copy(
            src_ref=stage.at[k, i],
            dst_ref=near.at[k, i],
            send_sem=near_send.at[k, i],
            recv_sem=near_recv.at[k, i],
            device_id={"row": 2 * chip + 1 - core},
            device_id_type=MESH,
        )

    def send_far(k, i):
        return pltpu.make_async_remote_copy(
            src_ref=relay.at[k, i],
            dst_ref=far.at[k, i],
            send_sem=far_send.at[k, i],
            recv_sem=far_recv.at[k, i],
            device_id={"row": 2 * to_chip(k) + core},
            device_id_type=MESH,
        )

    load(0).start()
    barrier = pltpu.get_barrier_semaphore()
    for k in range(1, n):
        pl.semaphore_signal(barrier, inc=1, device_id={"row": (me + k) % n}, device_id_type=MESH)
    for k in range(1, m):
        pl.semaphore_signal(barrier, inc=1, device_id={"feat": (mine + k) % m}, device_id_type=MESH)
    for p in range(2):
        for q in range(tiles):
            gh[p, :, q * LANES : (q + 1) * LANES] = jnp.broadcast_to(gh_ref[q, p : p + 1, :], (16, LANES)).astype(jnp.bfloat16)
    pl.semaphore_wait(barrier, n + m - 2)

    wide = (32, SLOT)
    down = lax.broadcasted_iota(jnp.int32, wide, 0) % SUBLANES
    high_at = (down[:16] * DIGIT).astype(jnp.int16)
    low_at = [(down + SUBLANES * j).astype(jnp.int8) for j in range(4)]
    zero, one = jnp.zeros(wide, F8), jnp.ones(wide, F8)
    nil = jnp.zeros((16, SLOT), jnp.bfloat16)
    lane = lax.broadcasted_iota(jnp.int32, (SUBLANES, LANES), 1)
    sub = lax.broadcasted_iota(jnp.int32, (SUBLANES, LANES), 0)
    byte = (lane // SUBLANES) % PACK
    of = [byte == f for f in range(PACK - 1)]
    def unpack(t):
        load(t).wait()

        @pl.when(t + 1 < n)
        def _():
            load(t + 1).start()

        for q in range(tiles):
            word = words[t % 2, q]
            for k in range(PACK):
                keys[k, :, q * LANES : (q + 1) * LANES] = lax.shift_right_logical(word, 8 * k)

    def one_hots(w, cols):
        rows = [jnp.broadcast_to(keys[k, pl.ds(w, 1), cols], (SUBLANES, SLOT)) for k in range(PACK)]
        twos = [jnp.concatenate(rows[i : i + 2], 0).astype(jnp.int16) for i in (0, 2)]
        low = jnp.concatenate(rows, 0).astype(jnp.int8) & jnp.int8(DIGIT - 1)
        left = []
        for two in twos:
            apart = (two & jnp.int16(BINS - DIGIT)) != high_at
            left += [jnp.where(apart, nil, gh[v, :, cols]) for v in range(2)]
        right = [jnp.where(low != low_at[j], zero, one) for j in range(4)]
        return left, right

    def block(i):
        total = [jnp.zeros((SUBLANES, LANES), f32) for _ in range(4)]
        for s in range(slots):
            cols = slice(s * SLOT, (s + 1) * SLOT)
            left0, right0 = one_hots(2 * i, cols)
            left1, right1 = one_hots(2 * i + 1, cols)
            found = lax.dot_general(
                jnp.concatenate(left0 + left1, 0),
                jnp.concatenate(right0 + right1, 0),
                (((1,), (1,)), ((), ())),
                preferred_element_type=f32,
            )
            kept = jnp.broadcast_to(keep_ref[s : s + 1, :], (SUBLANES, LANES))
            for q in range(2):
                square = found[64 * q : 64 * (q + 1), q * LANES : (q + 1) * LANES]
                for v in range(2):
                    part = [square[at : at + SUBLANES] for at in (16 * v, 16 * v + 8, 16 * v + 32, 16 * v + 40)]
                    dense = jnp.where(of[0], part[0], jnp.where(of[1], part[1], jnp.where(of[2], part[2], part[3])))
                    at = 2 * q + v
                    total[at] = total[at] * kept + dense
                    snap[s, at] = total[at]

    def hist(node, at):
        return snap[last_ref[0, node], at]

    def pair(k, carry):
        unpack(2 * k)

        def give(i, c):
            @pl.when(i > 0)
            def _():
                send_near(k, i - 1).start()

            @pl.when((i == 0) & (k > 0))
            def _():
                send_far(k - 1, BLOCKS - 1).start()

            block(i)
            for node in range(NODES):
                for at in range(4):
                    stage[k, i, node, at] = hist(node, at)
            return c

        lax.fori_loop(0, BLOCKS, give, 0)
        unpack(2 * k + 1)

        def hold(i, c):
            @pl.when(i == 0)
            def _():
                send_near(k, BLOCKS - 1).start()

            @pl.when((i > 0) & (k < pairs - 1))
            def _():
                send_far(k, i - 1).start()

            block(i)
            send_near(k, i).wait_recv()

            @pl.when(k < pairs - 1)
            def _():
                for node in range(NODES):
                    for at in range(4):
                        relay[k, i, node, at] = hist(node, at) + near[k, i, node, at]

            @pl.when(k == pairs - 1)
            def _():
                for node in range(NODES):
                    for at in range(4):
                        own[i, node, at] = hist(node, at) + near[k, i, node, at]

            return c

        lax.fori_loop(0, BLOCKS, hold, 0)
        return carry

    lax.fori_loop(0, pairs, pair, 0)

    def take(x, index):
        return jnp.take_along_axis(x, index, axis=1)

    tens, units = lane // (SUBLANES * PACK), lane % SUBLANES
    end_of_run = lane - units + (SUBLANES - 1)
    end_of_row = (LANES - DIGIT) + byte * SUBLANES + (SUBLANES - 1)

    def running(x):
        for shift in (1, 2, 4):
            x = x + jnp.where(units >= shift, pltpu.roll(x, shift, 1), 0.0)
        run = take(x, end_of_run)
        for j in range(1, 4):
            x = x + jnp.where(tens >= j, pltpu.roll(run, j * DIGIT, 1), 0.0)
        row = take(x, end_of_row)
        whole = row
        for shift in (1, 2, 4):
            whole = whole + jnp.where(sub >= shift, pltpu.roll(whole, shift, 0), 0.0)
        return x + (whole - row), jnp.broadcast_to(whole[SUBLANES - 1 :], whole.shape)

    def finish(i, best):
        for k in range(pairs - 1):
            send_far(k, i).wait_recv()
        for q in range(2):
            gains = []
            for node in range(NODES):
                sums = []
                for at in (2 * q, 2 * q + 1):
                    x = own[i, node, at]
                    for k in range(pairs - 1):
                        x = x + far[k, i, node, at]
                    sums.append(running(x))
                (gl, gt), (hl, ht) = sums
                gain = gl * gl / (hl + 1.0)
                gain = gain + (gt - gl) * (gt - gl) / (ht - hl + 1.0)
                gains.append(gain - gt * gt / (ht + 1.0))
            best = jnp.maximum(best, jnp.stack([jnp.max(x, axis=0) for x in gains], 0))
            turned = jnp.swapaxes(jnp.stack(gains, 0), 0, 1)
            for f in range(PACK):
                source = ((lane // SUBLANES) % 4) * DIGIT + f * SUBLANES + units
                for t in range(TOPS):
                    part = [take(turned[4 * t + j], source) for j in range(4)]
                    line = jnp.where(tens == 0, part[0], jnp.where(tens == 1, part[1], jnp.where(tens == 2, part[2], part[3])))
                    out_ref[SUBLANES * f + 2 * i + q, :, t * LANES : (t + 1) * LANES] = line
        return best

    top_gain = lax.fori_loop(0, BLOCKS, finish, jnp.full((NODES, LANES), -jnp.inf, f32))

    def exchange(value, slots, count, axis, index, sems, arrived):
        slots[0] = jnp.broadcast_to(jnp.max(value, axis=1, keepdims=True), (NODES, LANES))
        copies = []
        for k in range(1, count):
            copies.append(
                pltpu.make_async_remote_copy(
                    src_ref=slots.at[0],
                    dst_ref=slots.at[k],
                    send_sem=sems.at[k - 1],
                    recv_sem=arrived.at[k - 1],
                    device_id={axis: (index + k) % count},
                    device_id_type=MESH,
                )
            )
            copies[-1].start()
        for copy in copies:
            copy.wait()
        best = slots[0]
        for k in range(1, count):
            best = jnp.maximum(best, slots[k])
        return best

    best = exchange(top_gain, row_best, n, "row", me, row_send, row_recv)
    best = exchange(best, feat_best, m, "feat", mine, feat_send, feat_recv)
    flat = jnp.max(jnp.where(lane == sub, best, -jnp.inf), axis=0, keepdims=True)
    best_ref[...] = flat[:, :NODES]

    def drain(k, carry):
        for i in range(BLOCKS):
            send_near(k, i).wait_send()

            @pl.when(k < pairs - 1)
            def _():
                send_far(k, i).wait_send()

        return carry

    lax.fori_loop(0, pairs, drain, 0)


def grouped(n, m, bins, grads, hess, node):
    features, rows = bins.shape
    groups, tiles = features // 32, rows // LANES
    slots = rows // SLOT + NODES - 1
    held = 2 * slots
    vmem = pl.BlockSpec(memory_space=pltpu.VMEM)
    smem = pl.BlockSpec(memory_space=pltpu.SMEM)
    hbm = pl.BlockSpec(memory_space=pl.ANY)
    words, gh, keep, last = pl.pallas_call(
        regroup,
        in_specs=[hbm, vmem, vmem, vmem],
        out_specs=(vmem, vmem, vmem, vmem),
        out_shape=(
            jax.ShapeDtypeStruct((held + 1, groups, SUBLANES, LANES), jnp.int32),
            jax.ShapeDtypeStruct((held + 1, SUBLANES, LANES), jnp.float32),
            jax.ShapeDtypeStruct((-(-slots // SUBLANES) * SUBLANES, LANES), jnp.float32),
            jax.ShapeDtypeStruct((1, LANES), jnp.int32),
        ),
        scratch_shapes=[
            pltpu.VMEM((groups, 32, rows), jnp.int32),
            pltpu.VMEM((2, tiles, LANES), jnp.float32),
            pltpu.VMEM((tiles, NODES, LANES), jnp.int32),
            pltpu.VMEM((tiles, LANES), jnp.int32),
            pltpu.SMEM((tiles, LANES), jnp.int32),
            pltpu.SemaphoreType.DMA((groups,)),
            pltpu.SemaphoreType.DMA,
        ],
        compiler_params=pltpu.CompilerParams(vmem_limit_bytes=56 << 20),
    )(bins, node.reshape(-1, LANES), grads.reshape(-1, LANES), hess.reshape(-1, LANES))
    pairs = n // 2
    piece = (BLOCKS, NODES, 4, SUBLANES, LANES)
    out, best = pl.pallas_call(
        functools.partial(sweep, n, m),
        in_specs=[hbm, vmem, vmem, smem],
        out_specs=(vmem, vmem),
        out_shape=(
            jax.ShapeDtypeStruct((32, NODES, BINS), jnp.float32),
            jax.ShapeDtypeStruct((1, NODES), jnp.float32),
        ),
        scratch_shapes=[
            pltpu.VMEM((2, held, SUBLANES, LANES), jnp.int32),
            pltpu.VMEM((PACK, SUBLANES, held * LANES), jnp.int32),
            pltpu.VMEM((2, 16, held * LANES), jnp.bfloat16),
            pltpu.VMEM((slots, 4, SUBLANES, LANES), jnp.float32),
            pltpu.VMEM((pairs,) + piece, jnp.float32),
            pltpu.VMEM((pairs,) + piece, jnp.float32),
            pltpu.VMEM((pairs - 1,) + piece, jnp.float32),
            pltpu.VMEM((pairs - 1,) + piece, jnp.float32),
            pltpu.VMEM(piece, jnp.float32),
            pltpu.VMEM((n, NODES, LANES), jnp.float32),
            pltpu.VMEM((m, NODES, LANES), jnp.float32),
            pltpu.SemaphoreType.DMA((2,)),
            pltpu.SemaphoreType.DMA((pairs, BLOCKS)),
            pltpu.SemaphoreType.DMA((pairs, BLOCKS)),
            pltpu.SemaphoreType.DMA((pairs - 1, BLOCKS)),
            pltpu.SemaphoreType.DMA((pairs - 1, BLOCKS)),
            pltpu.SemaphoreType.DMA((n - 1,)),
            pltpu.SemaphoreType.DMA((n - 1,)),
            pltpu.SemaphoreType.DMA((m - 1,)),
            pltpu.SemaphoreType.DMA((m - 1,)),
        ],
        compiler_params=pltpu.CompilerParams(
            collective_id=0, has_side_effects=True, vmem_limit_bytes=56 << 20
        ),
    )(words, gh, keep, last)
    best = best.reshape(NODES)
    return out - best[None, :, None], best


def solution(mesh):
    n, m = mesh.shape["row"], mesh.shape["feat"]

    def per_device(bins, grads, hess, node):
        features, rows = bins.shape
        own = features // n
        if own == 32 and n % 2 == 0 and n > 2 and rows % (2 * SLOT) == 0:
            return grouped(n, m, bins, grads, hess, node)
        block = own if own < SUBLANES else next(b for b in (2 * SUBLANES, SUBLANES) if own % b == 0)
        held = max(block, SUBLANES)
        chunks = own // block
        vmem = pl.BlockSpec(memory_space=pltpu.VMEM)
        piece = (block, LINES, LANES)
        out, best = pl.pallas_call(
            functools.partial(direct, n, m, block, chunks),
            in_specs=[pl.BlockSpec(memory_space=pl.ANY), vmem, vmem, vmem],
            out_specs=(vmem, vmem),
            out_shape=(
                jax.ShapeDtypeStruct((own, NODES, BINS), jnp.float32),
                jax.ShapeDtypeStruct((1, NODES), jnp.float32),
            ),
            scratch_shapes=[
                pltpu.VMEM((2, held, rows), jnp.int32),
                pltpu.VMEM((held, rows), jnp.float32),
                pltpu.VMEM((held, rows), jnp.float32),
                pltpu.VMEM((SLOTS, rows), jnp.bfloat16),
                pltpu.VMEM((SLOTS, rows), jnp.bfloat16),
                pltpu.VMEM((GROUP * HALVES * LINES, TILE), jnp.float32),
                pltpu.VMEM((n * chunks,) + piece, jnp.float32),
                pltpu.VMEM(((n - 1) * chunks,) + piece, jnp.float32),
                pltpu.VMEM((n, NODES, LANES), jnp.float32),
                pltpu.VMEM((m, NODES, LANES), jnp.float32),
                pltpu.SemaphoreType.DMA((2,)),
                pltpu.SemaphoreType.DMA(((n - 1) * chunks,)),
                pltpu.SemaphoreType.DMA(((n - 1) * chunks,)),
                pltpu.SemaphoreType.DMA((n - 1,)),
                pltpu.SemaphoreType.DMA((n - 1,)),
                pltpu.SemaphoreType.DMA((m - 1,)),
                pltpu.SemaphoreType.DMA((m - 1,)),
            ],
            compiler_params=pltpu.CompilerParams(
                collective_id=0, has_side_effects=True, vmem_limit_bytes=56 << 20
            ),
        )(bins, node.reshape(1, rows), grads.reshape(-1, LANES), hess.reshape(-1, LANES))
        best = best.reshape(NODES)
        return out - best[None, :, None], best

    return jax.shard_map(
        per_device,
        mesh=mesh,
        in_specs=(P("feat", "row"), P("row"), P("row"), P("row")),
        out_specs=(P(("feat", "row"), None, None), P()),
        check_vma=False,
    )
```

```python
import functools
import jax
import jax.numpy as jnp
from jax import lax
from jax.experimental import pallas as pl
from jax.experimental.pallas import tpu as pltpu
from jax.sharding import PartitionSpec as P

BINS = 256
NODES = 8
LANES = 128
SUBLANES = 8
LOW = 64
TILE = 256
GROUP = TILE // LOW
HALVES = LANES // LOW
TOPS = BINS // LANES
SLOTS = NODES * TOPS
LINES = 2 * SLOTS
MESH = pl.DeviceIdType.MESH
F8 = jnp.float8_e4m3fn
SLOT = 256
PACK = 4
CHUNK = 8
DIGIT = 32
BLOCKS = SUBLANES // 2


def partner(me, k, n):
    if n & (n - 1):
        return (me + k) % n
    out, weight = 0, 1
    while weight < n:
        out = out + (((me // weight) % 2 + (k // weight) % 2) % 2) * weight
        weight *= 2
    return out


def direct(
    n, m, block, chunks, bins_hbm, node_ref, g_ref, h_ref, out_ref, best_ref,
    bins_buf, high_ref, low_ref, g_all, h_all, acc_ref, stage, landed, row_best, feat_best,
    load_sem, send_sem, recv_sem, row_send, row_recv, feat_send, feat_recv,
):
    rows = bins_buf.shape[2]
    me = lax.axis_index("row")
    mine = lax.axis_index("feat")
    steps = n * chunks
    sent = (n - 1) * chunks

    def place_of(s):
        return (partner(me, n - 1 - s // chunks, n) * chunks + s % chunks) * block

    def load(s):
        start = pl.multiple_of((place_of(s) // SUBLANES) * SUBLANES, SUBLANES)
        return pltpu.make_async_copy(
            bins_hbm.at[pl.ds(start, bins_buf.shape[1]), :], bins_buf.at[s % 2], load_sem.at[s % 2]
        )

    def send(s):
        k = n - 1 - s // chunks
        return pltpu.make_async_remote_copy(
            src_ref=stage.at[s],
            dst_ref=landed.at[s],
            send_sem=send_sem.at[s],
            recv_sem=recv_sem.at[s],
            device_id={"row": partner(me, k, n)},
            device_id_type=MESH,
        )

    load(0).start()
    barrier = pltpu.get_barrier_semaphore()
    for k in range(1, n):
        pl.semaphore_signal(barrier, inc=1, device_id={"row": (me + k) % n}, device_id_type=MESH)
    for k in range(1, m):
        pl.semaphore_signal(barrier, inc=1, device_id={"feat": (mine + k) % m}, device_id_type=MESH)

    g = g_ref[...].astype(jnp.float32)
    h = h_ref[...].astype(jnp.float32)
    for i in range(rows // LANES):
        cols = slice(i * LANES, (i + 1) * LANES)
        g_all[:, cols] = jnp.broadcast_to(g[i : i + 1, :], (SLOTS, LANES)).astype(jnp.bfloat16)
        h_all[:, cols] = jnp.broadcast_to(h[i : i + 1, :], (SLOTS, LANES)).astype(jnp.bfloat16)
    pl.semaphore_wait(barrier, n + m - 2)

    def step(s, carry):
        load(s).wait()

        @pl.when(s + 1 < steps)
        def _():
            load(s + 1).start()

        @pl.when((s >= 1) & (s <= sent))
        def _():
            send(s - 1).start()

        offset = 0 if block % SUBLANES == 0 else place_of(s) % SUBLANES
        bins = bins_buf[s % 2]
        upper = bins >= LANES
        rest = jnp.where(upper, bins - LANES, bins)
        second = rest >= LOW
        slot = node_ref[...] + jnp.where(upper, NODES, 0)
        high_ref[...] = jnp.where(second, slot + SLOTS, slot).astype(jnp.float32)
        low_ref[...] = jnp.where(second, rest - LOW, rest).astype(jnp.float32)
        place = lax.broadcasted_iota(jnp.int32, (SLOTS, rows), 0).astype(jnp.bfloat16)
        zero = jnp.zeros((SLOTS, rows), jnp.bfloat16)
        one = jnp.ones((SLOTS, rows), jnp.bfloat16)
        for first in range(0, block, GROUP):
            left, right = [], []
            for f in range(first, first + GROUP):
                row = pl.ds(offset + f, 1)
                high = jnp.broadcast_to(high_ref[row, :], (SLOTS, rows)).astype(jnp.bfloat16)
                low = jnp.broadcast_to(low_ref[row, :], (SLOTS, rows)).astype(jnp.bfloat16)
                for j in range(HALVES):
                    here = high == place + jnp.asarray(SLOTS * j, jnp.bfloat16)
                    left += [jnp.where(here, g_all[...], zero), jnp.where(here, h_all[...], zero)]
                for j in range(LOW // SLOTS):
                    here = low == place + jnp.asarray(SLOTS * j, jnp.bfloat16)
                    right.append(jnp.where(here, one, zero))
            acc_ref[...] = lax.dot_general(
                jnp.concatenate(left, 0),
                jnp.concatenate(right, 0),
                (((1,), (1,)), ((), ())),
                preferred_element_type=jnp.float32,
            )
            for i in range(GROUP):
                parts = []
                for j in range(HALVES):
                    top = (i * HALVES + j) * LINES
                    parts.append(acc_ref[top : top + LINES, i * LOW : (i + 1) * LOW])
                stage[s, first + i] = jnp.concatenate(parts, 1)
        return carry

    lax.fori_loop(0, steps, step, 0)

    def drain(s, carry):
        send(s).wait()
        return carry

    lax.fori_loop(0, sent, drain, 0)

    lane = lax.broadcasted_iota(jnp.int32, (block * 2 * TOPS * NODES, LANES), 1)

    def finish(c, top_gain):
        def add(k, total):
            return total + landed[k * chunks + c]

        x = lax.fori_loop(0, n - 1, add, stage[sent + c])
        x = x.reshape(block * LINES, LANES)
        shift = 1
        while shift < LANES:
            x = x + jnp.where(lane >= shift, pltpu.roll(x, shift, 1), 0.0)
            shift *= 2
        x = x.reshape(block, 2, TOPS, NODES, LANES)
        left, total = [], jnp.zeros((block, 2, NODES, LANES), jnp.float32)
        for t in range(TOPS):
            left.append(x[:, :, t] + total)
            total = total + jnp.broadcast_to(x[:, :, t, :, LANES - 1 :], total.shape)
        gt, ht = total[:, 0], total[:, 1]
        base = gt * gt / (ht + 1.0)
        for t in range(TOPS):
            gl, hl = left[t][:, 0], left[t][:, 1]
            gain = gl * gl / (hl + 1.0)
            gain = gain + (gt - gl) * (gt - gl) / (ht - hl + 1.0)
            gain = gain - base
            out_ref[pl.ds(c * block, block), :, t * LANES : (t + 1) * LANES] = gain
            top_gain = jnp.maximum(top_gain, jnp.max(gain, axis=0))
        return top_gain

    top_gain = lax.fori_loop(0, chunks, finish, jnp.full((NODES, LANES), -jnp.inf, jnp.float32))

    def exchange(value, slots, count, axis, index, sems, arrived):
        slots[0] = jnp.broadcast_to(jnp.max(value, axis=1, keepdims=True), (NODES, LANES))
        copies = []
        for k in range(1, count):
            copies.append(
                pltpu.make_async_remote_copy(
                    src_ref=slots.at[0],
                    dst_ref=slots.at[k],
                    send_sem=sems.at[k - 1],
                    recv_sem=arrived.at[k - 1],
                    device_id={axis: (index + k) % count},
                    device_id_type=MESH,
                )
            )
            copies[-1].start()
        for copy in copies:
            copy.wait()
        best = slots[0]
        for k in range(1, count):
            best = jnp.maximum(best, slots[k])
        return best

    best = exchange(top_gain, row_best, n, "row", me, row_send, row_recv)
    best = exchange(best, feat_best, m, "feat", mine, feat_send, feat_recv)
    across = lax.broadcasted_iota(jnp.int32, (NODES, LANES), 1)
    down = lax.broadcasted_iota(jnp.int32, (NODES, LANES), 0)
    flat = jnp.max(jnp.where(across == down, best, -jnp.inf), axis=0, keepdims=True)
    best_ref[...] = flat[:, :NODES]


def take(x, index):
    return jnp.take_along_axis(x, index, axis=1, mode="promise_in_bounds")


def regroup(
    bins_hbm, node_ref, g_ref, h_ref, words_ref, gh_ref, keep_ref, last_ref,
    bins, pieces, pattern, spots_v, spots_s, load_sem, spots_sem,
):
    f32, bf16, i32 = jnp.float32, jnp.bfloat16, jnp.int32
    tiles = node_ref.shape[0]
    groups = bins.shape[0] // 32
    chunks = tiles // CHUNK

    def load(c):
        cols = pl.ds(pl.multiple_of(c * (CHUNK * LANES), CHUNK * LANES), CHUNK * LANES)
        return pltpu.make_async_copy(bins_hbm.at[:, cols], bins.at[:, cols], load_sem.at[c])

    for c in range(chunks):
        load(c).start()
    node = node_ref[...]
    pieces[0] = g_ref[...].astype(f32)
    pieces[1] = h_ref[...].astype(f32)
    row = lax.broadcasted_iota(i32, (LANES, LANES), 0)
    col = lax.broadcasted_iota(i32, (LANES, LANES), 1)
    upper = jnp.where(row <= col, 1.0, 0.0).astype(bf16)
    ones = jnp.ones((LANES, LANES), bf16)
    above = lax.broadcasted_iota(i32, (tiles, tiles), 1) < lax.broadcasted_iota(i32, (tiles, tiles), 0)
    lower = jnp.where(above, 1.0, 0.0).astype(bf16)
    dot = functools.partial(jnp.dot, preferred_element_type=f32)
    lane = lax.broadcasted_iota(i32, (tiles, LANES), 1)
    slot = lax.broadcasted_iota(i32, keep_ref.shape, 0)
    keep = jnp.ones(keep_ref.shape, f32)
    base = jnp.zeros((1, LANES), i32)
    last = jnp.zeros((1, LANES), i32)
    dest = jnp.zeros((tiles, LANES), i32)
    spots = jnp.zeros((tiles, LANES), i32)
    for n in range(NODES):
        hit = node == n
        x = jnp.where(hit, 1.0, 0.0).astype(bf16)
        rank = dot(x, upper).astype(i32)
        count = dot(x, ones)
        ahead = dot(lower, count.astype(bf16)).astype(i32)
        count = count.astype(i32)
        total = (ahead + count)[tiles - 1 : tiles]
        start = ahead + base
        dest = jnp.where(hit, start + rank - 1, dest)
        spots = jnp.where(lane == n, start, jnp.where(lane == NODES + n, start + count, spots))
        keep = jnp.where(slot * SLOT == base, 0.0, keep)
        base = base + jnp.maximum((total + (SLOT - 1)) // SLOT, 1) * SLOT
        last = jnp.where(lane[:1] == n, base // SLOT - 1, last)
    keep_ref[...] = keep
    last_ref[...] = last
    spots_v[...] = spots
    to_scalar = pltpu.make_async_copy(spots_v, spots_s, spots_sem)
    to_scalar.start()

    spot = dest & (LANES - 1)
    sub = lax.broadcasted_iota(i32, (NODES, LANES), 0)
    across = lax.broadcasted_iota(i32, (NODES, LANES), 1)
    none = jnp.zeros((NODES, LANES), i32)
    for b in range(0, tiles, 2):
        left, right = [], []
        for i in range(2):
            here = jnp.where(jnp.broadcast_to(node[b + i : b + i + 1], (NODES, LANES)) == sub, across, 0)
            left.append(jnp.concatenate([none] * i + [here] + [none] * (1 - i), 1))
            right.append(jnp.where(jnp.broadcast_to(spot[b + i : b + i + 1], (LANES, LANES)) == row, 1.0, 0.0))
        found = lax.dot_general(
            jnp.concatenate(left, 0).astype(f32).astype(bf16),
            jnp.concatenate(right, 1).astype(bf16),
            (((1,), (1,)), ((), ())),
            preferred_element_type=f32,
        ).astype(i32)
        pattern[b] = found[:NODES]
        pattern[b + 1] = found[NODES:]
    gh_ref[...] = jnp.zeros(gh_ref.shape, f32)
    to_scalar.wait()

    def place(b):
        cols = pl.ds(pl.multiple_of(b * LANES, LANES), LANES)
        words = []
        for t in range(groups):
            word = bins[32 * t : 32 * t + SUBLANES, cols]
            for k in range(1, PACK):
                word = word | lax.shift_left(bins[32 * t + SUBLANES * k : 32 * t + SUBLANES * (k + 1), cols], 8 * k)
            words.append(word)
        piece = [jnp.broadcast_to(pieces[i, pl.ds(b, 1), :], (SUBLANES, LANES)) for i in range(2)]
        gh = jnp.where(sub == 0, piece[0], piece[1])
        for n in range(NODES):
            first = spots_s[b, n]
            tile = lax.shift_right_logical(first, 7)
            low = first & (LANES - 1)
            high = low + spots_s[b, NODES + n] - first
            source = jnp.broadcast_to(pattern[b, n : n + 1, :], (SUBLANES, LANES))
            near = (across >= low) & (across < high)
            far = across < high - LANES
            for t in range(groups):
                moved = take(words[t], source)
                pltpu.store(words_ref.at[tile, t], moved, mask=near)
                pltpu.store(words_ref.at[tile + 1, t], moved, mask=far)
            moved = take(gh, source)
            pltpu.store(gh_ref.at[tile], moved, mask=near)
            pltpu.store(gh_ref.at[tile + 1], moved, mask=far)

    def chunk(c, carry):
        load(c).wait()
        for j in range(CHUNK):
            place(c * CHUNK + j)
        return carry

    lax.fori_loop(0, chunks, chunk, 0)


def sweep(
    n, m, words_hbm, gh_ref, keep_ref, last_ref, out_ref, best_ref,
    words, keys, gh, snap, stage, near, relay, far, row_best, feat_best,
    load_sem, near_send, near_recv, far_send, far_recv, row_send, row_recv, feat_send, feat_recv,
):
    f32 = jnp.float32
    tiles = words.shape[1]
    slots = tiles * LANES // SLOT
    pairs = n // 2
    me = lax.axis_index("row")
    mine = lax.axis_index("feat")
    chip, core = me // 2, me % 2

    def to_chip(k):
        return partner(chip, pairs - 1 - k, pairs)

    def load(t):
        group = 2 * to_chip(t // 2) + (t + 1 + core) % 2
        return pltpu.make_async_copy(
            words_hbm.at[pl.ds(0, tiles), group], words.at[t % 2], load_sem.at[t % 2]
        )

    def send_near(k, i):
        return pltpu.make_async_remote_copy(
            src_ref=stage.at[k, i],
            dst_ref=near.at[k, i],
            send_sem=near_send.at[k, i],
            recv_sem=near_recv.at[k, i],
            device_id={"row": 2 * chip + 1 - core},
            device_id_type=MESH,
        )

    def send_far(k, i):
        return pltpu.make_async_remote_copy(
            src_ref=relay.at[k, i],
            dst_ref=far.at[k, i],
            send_sem=far_send.at[k, i],
            recv_sem=far_recv.at[k, i],
            device_id={"row": 2 * to_chip(k) + core},
            device_id_type=MESH,
        )

    load(0).start()
    barrier = pltpu.get_barrier_semaphore()
    for k in range(1, n):
        pl.semaphore_signal(barrier, inc=1, device_id={"row": (me + k) % n}, device_id_type=MESH)
    for k in range(1, m):
        pl.semaphore_signal(barrier, inc=1, device_id={"feat": (mine + k) % m}, device_id_type=MESH)
    for p in range(2):
        for q in range(tiles):
            gh[p, :, q * LANES : (q + 1) * LANES] = jnp.broadcast_to(gh_ref[q, p : p + 1, :], (16, LANES)).astype(jnp.bfloat16)
    pl.semaphore_wait(barrier, n + m - 2)

    wide = (32, SLOT)
    down = lax.broadcasted_iota(jnp.int32, wide, 0) % SUBLANES
    high_at = (down[:16] * DIGIT).astype(jnp.int16)
    low_at = [(down + SUBLANES * j).astype(jnp.int8) for j in range(4)]
    zero, one = jnp.zeros(wide, F8), jnp.ones(wide, F8)
    nil = jnp.zeros((16, SLOT), jnp.bfloat16)
    lane = lax.broadcasted_iota(jnp.int32, (SUBLANES, LANES), 1)
    sub = lax.broadcasted_iota(jnp.int32, (SUBLANES, LANES), 0)
    byte = (lane // SUBLANES) % PACK
    of = [byte == f for f in range(PACK - 1)]
    def unpack(t):
        load(t).wait()

        @pl.when(t + 1 < n)
        def _():
            load(t + 1).start()

        for q in range(tiles):
            word = words[t % 2, q]
            for k in range(PACK):
                keys[k, :, q * LANES : (q + 1) * LANES] = lax.shift_right_logical(word, 8 * k)

    def one_hots(w, cols):
        rows = [jnp.broadcast_to(keys[k, pl.ds(w, 1), cols], (SUBLANES, SLOT)) for k in range(PACK)]
        twos = [jnp.concatenate(rows[i : i + 2], 0).astype(jnp.int16) for i in (0, 2)]
        low = jnp.concatenate(rows, 0).astype(jnp.int8) & jnp.int8(DIGIT - 1)
        left = []
        for two in twos:
            apart = (two & jnp.int16(BINS - DIGIT)) != high_at
            left += [jnp.where(apart, nil, gh[v, :, cols]) for v in range(2)]
        right = [jnp.where(low != low_at[j], zero, one) for j in range(4)]
        return left, right

    def block(i):
        total = [jnp.zeros((SUBLANES, LANES), f32) for _ in range(4)]
        for s in range(slots):
            cols = slice(s * SLOT, (s + 1) * SLOT)
            left0, right0 = one_hots(2 * i, cols)
            left1, right1 = one_hots(2 * i + 1, cols)
            found = lax.dot_general(
                jnp.concatenate(left0 + left1, 0),
                jnp.concatenate(right0 + right1, 0),
                (((1,), (1,)), ((), ())),
                preferred_element_type=f32,
            )
            kept = jnp.broadcast_to(keep_ref[s : s + 1, :], (SUBLANES, LANES))
            for q in range(2):
                square = found[64 * q : 64 * (q + 1), q * LANES : (q + 1) * LANES]
                for v in range(2):
                    part = [square[at : at + SUBLANES] for at in (16 * v, 16 * v + 8, 16 * v + 32, 16 * v + 40)]
                    dense = jnp.where(of[0], part[0], jnp.where(of[1], part[1], jnp.where(of[2], part[2], part[3])))
                    at = 2 * q + v
                    total[at] = total[at] * kept + dense
                    snap[i % 2, s, at] = total[at]

    def store(ref, k, i):
        for node in range(NODES):
            for at in range(4):
                ref[k, i, node, at] = snap[i % 2, last_ref[0, node], at]

    def merge(k, i):
        send_near(k, i).wait_recv()
        for node in range(NODES):
            for at in range(4):
                relay[k, i, node, at] += near[k, i, node, at]

    def pair(k, carry):
        unpack(2 * k)

        @pl.when(k > 0)
        def _():
            for i in range(2, BLOCKS):
                send_far(k - 1, i).start()

        for i in range(BLOCKS):
            block(i)
            if i > 0:
                send_near(k, i - 1).start()
            store(stage, k, i)
        unpack(2 * k + 1)
        for i in range(BLOCKS):
            if i == 0:
                send_near(k, BLOCKS - 1).start()
            if i == BLOCKS - 1:

                @pl.when(k < pairs - 1)
                def _():
                    for j in range(2):
                        send_far(k, j).start()

            block(i)
            store(relay, k, i)
            if i == 1:
                merge(k, 0)
                merge(k, 1)
        for i in range(2, BLOCKS):
            merge(k, i)
        return carry

    lax.fori_loop(0, pairs, pair, 0)

    tens, units = lane // (SUBLANES * PACK), lane % SUBLANES
    end_of_run = lane - units + (SUBLANES - 1)
    end_of_row = (LANES - DIGIT) + byte * SUBLANES + (SUBLANES - 1)

    def running(x):
        for shift in (1, 2, 4):
            x = x + jnp.where(units >= shift, pltpu.roll(x, shift, 1), 0.0)
        run = take(x, end_of_run)
        for j in range(1, 4):
            x = x + jnp.where(tens >= j, pltpu.roll(run, j * DIGIT, 1), 0.0)
        row = take(x, end_of_row)
        whole = row
        for shift in (1, 2, 4):
            whole = whole + jnp.where(sub >= shift, pltpu.roll(whole, shift, 0), 0.0)
        return x + (whole - row), jnp.broadcast_to(whole[SUBLANES - 1 :], whole.shape)

    def finish(i, best):
        for k in range(pairs - 1):
            send_far(k, i).wait_recv()
        for q in range(2):
            gains = []
            for node in range(NODES):
                sums = []
                for at in (2 * q, 2 * q + 1):
                    x = relay[pairs - 1, i, node, at]
                    for k in range(pairs - 1):
                        x = x + far[k, i, node, at]
                    sums.append(running(x))
                (gl, gt), (hl, ht) = sums
                gain = gl * gl / (hl + 1.0)
                gain = gain + (gt - gl) * (gt - gl) / (ht - hl + 1.0)
                gains.append(gain - gt * gt / (ht + 1.0))
            best = jnp.maximum(best, jnp.stack([jnp.max(x, axis=0) for x in gains], 0))
            turned = jnp.swapaxes(jnp.stack(gains, 0), 0, 1)
            for f in range(PACK):
                source = ((lane // SUBLANES) % 4) * DIGIT + f * SUBLANES + units
                for t in range(TOPS):
                    part = [take(turned[4 * t + j], source) for j in range(4)]
                    line = jnp.where(tens == 0, part[0], jnp.where(tens == 1, part[1], jnp.where(tens == 2, part[2], part[3])))
                    out_ref[SUBLANES * f + 2 * i + q, :, t * LANES : (t + 1) * LANES] = line
        return best

    top_gain = lax.fori_loop(0, BLOCKS, finish, jnp.full((NODES, LANES), -jnp.inf, f32))

    def exchange(value, slots, count, axis, index, sems, arrived):
        slots[0] = jnp.broadcast_to(jnp.max(value, axis=1, keepdims=True), (NODES, LANES))
        copies = []
        for k in range(1, count):
            copies.append(
                pltpu.make_async_remote_copy(
                    src_ref=slots.at[0],
                    dst_ref=slots.at[k],
                    send_sem=sems.at[k - 1],
                    recv_sem=arrived.at[k - 1],
                    device_id={axis: (index + k) % count},
                    device_id_type=MESH,
                )
            )
            copies[-1].start()
        for copy in copies:
            copy.wait()
        best = slots[0]
        for k in range(1, count):
            best = jnp.maximum(best, slots[k])
        return best

    best = exchange(top_gain, row_best, n, "row", me, row_send, row_recv)
    best = exchange(best, feat_best, m, "feat", mine, feat_send, feat_recv)
    flat = jnp.max(jnp.where(lane == sub, best, -jnp.inf), axis=0, keepdims=True)
    best_ref[...] = flat[:, :NODES]

    def drain(k, carry):
        for i in range(BLOCKS):
            send_near(k, i).wait_send()

            @pl.when(k < pairs - 1)
            def _():
                send_far(k, i).wait_send()

        return carry

    lax.fori_loop(0, pairs, drain, 0)


def grouped(n, m, bins, grads, hess, node):
    features, rows = bins.shape
    groups, tiles = features // 32, rows // LANES
    slots = rows // SLOT + NODES - 1
    held = 2 * slots
    vmem = pl.BlockSpec(memory_space=pltpu.VMEM)
    smem = pl.BlockSpec(memory_space=pltpu.SMEM)
    hbm = pl.BlockSpec(memory_space=pl.ANY)
    words, gh, keep, last = pl.pallas_call(
        regroup,
        in_specs=[hbm, vmem, vmem, vmem],
        out_specs=(vmem, vmem, vmem, vmem),
        out_shape=(
            jax.ShapeDtypeStruct((held + 1, groups, SUBLANES, LANES), jnp.int32),
            jax.ShapeDtypeStruct((held + 1, SUBLANES, LANES), jnp.float32),
            jax.ShapeDtypeStruct((-(-slots // SUBLANES) * SUBLANES, LANES), jnp.float32),
            jax.ShapeDtypeStruct((1, LANES), jnp.int32),
        ),
        scratch_shapes=[
            pltpu.VMEM((features, rows), jnp.int32),
            pltpu.VMEM((2, tiles, LANES), jnp.float32),
            pltpu.VMEM((tiles, NODES, LANES), jnp.int32),
            pltpu.VMEM((tiles, LANES), jnp.int32),
            pltpu.SMEM((tiles, LANES), jnp.int32),
            pltpu.SemaphoreType.DMA((tiles // CHUNK,)),
            pltpu.SemaphoreType.DMA,
        ],
        compiler_params=pltpu.CompilerParams(vmem_limit_bytes=56 << 20),
    )(bins, node.reshape(-1, LANES), grads.reshape(-1, LANES), hess.reshape(-1, LANES))
    pairs = n // 2
    piece = (BLOCKS, NODES, 4, SUBLANES, LANES)
    out, best = pl.pallas_call(
        functools.partial(sweep, n, m),
        in_specs=[hbm, vmem, vmem, smem],
        out_specs=(vmem, vmem),
        out_shape=(
            jax.ShapeDtypeStruct((32, NODES, BINS), jnp.float32),
            jax.ShapeDtypeStruct((1, NODES), jnp.float32),
        ),
        scratch_shapes=[
            pltpu.VMEM((2, held, SUBLANES, LANES), jnp.int32),
            pltpu.VMEM((PACK, SUBLANES, held * LANES), jnp.int32),
            pltpu.VMEM((2, 16, held * LANES), jnp.bfloat16),
            pltpu.VMEM((2, slots, 4, SUBLANES, LANES), jnp.float32),
            pltpu.VMEM((pairs,) + piece, jnp.float32),
            pltpu.VMEM((pairs,) + piece, jnp.float32),
            pltpu.VMEM((pairs,) + piece, jnp.float32),
            pltpu.VMEM((pairs - 1,) + piece, jnp.float32),
            pltpu.VMEM((n, NODES, LANES), jnp.float32),
            pltpu.VMEM((m, NODES, LANES), jnp.float32),
            pltpu.SemaphoreType.DMA((2,)),
            pltpu.SemaphoreType.DMA((pairs, BLOCKS)),
            pltpu.SemaphoreType.DMA((pairs, BLOCKS)),
            pltpu.SemaphoreType.DMA((pairs - 1, BLOCKS)),
            pltpu.SemaphoreType.DMA((pairs - 1, BLOCKS)),
            pltpu.SemaphoreType.DMA((n - 1,)),
            pltpu.SemaphoreType.DMA((n - 1,)),
            pltpu.SemaphoreType.DMA((m - 1,)),
            pltpu.SemaphoreType.DMA((m - 1,)),
        ],
        compiler_params=pltpu.CompilerParams(
            collective_id=0, has_side_effects=True, vmem_limit_bytes=56 << 20
        ),
    )(words, gh, keep, last)
    best = best.reshape(NODES)
    return out - best[None, :, None], best


def solution(mesh):
    n, m = mesh.shape["row"], mesh.shape["feat"]

    def per_device(bins, grads, hess, node):
        features, rows = bins.shape
        own = features // n
        if own == 32 and n % 2 == 0 and n > 2 and rows % (CHUNK * LANES) == 0:
            return grouped(n, m, bins, grads, hess, node)
        block = own if own < SUBLANES else next(b for b in (2 * SUBLANES, SUBLANES) if own % b == 0)
        held = max(block, SUBLANES)
        chunks = own // block
        vmem = pl.BlockSpec(memory_space=pltpu.VMEM)
        piece = (block, LINES, LANES)
        out, best = pl.pallas_call(
            functools.partial(direct, n, m, block, chunks),
            in_specs=[pl.BlockSpec(memory_space=pl.ANY), vmem, vmem, vmem],
            out_specs=(vmem, vmem),
            out_shape=(
                jax.ShapeDtypeStruct((own, NODES, BINS), jnp.float32),
                jax.ShapeDtypeStruct((1, NODES), jnp.float32),
            ),
            scratch_shapes=[
                pltpu.VMEM((2, held, rows), jnp.int32),
                pltpu.VMEM((held, rows), jnp.float32),
                pltpu.VMEM((held, rows), jnp.float32),
                pltpu.VMEM((SLOTS, rows), jnp.bfloat16),
                pltpu.VMEM((SLOTS, rows), jnp.bfloat16),
                pltpu.VMEM((GROUP * HALVES * LINES, TILE), jnp.float32),
                pltpu.VMEM((n * chunks,) + piece, jnp.float32),
                pltpu.VMEM(((n - 1) * chunks,) + piece, jnp.float32),
                pltpu.VMEM((n, NODES, LANES), jnp.float32),
                pltpu.VMEM((m, NODES, LANES), jnp.float32),
                pltpu.SemaphoreType.DMA((2,)),
                pltpu.SemaphoreType.DMA(((n - 1) * chunks,)),
                pltpu.SemaphoreType.DMA(((n - 1) * chunks,)),
                pltpu.SemaphoreType.DMA((n - 1,)),
                pltpu.SemaphoreType.DMA((n - 1,)),
                pltpu.SemaphoreType.DMA((m - 1,)),
                pltpu.SemaphoreType.DMA((m - 1,)),
            ],
            compiler_params=pltpu.CompilerParams(
                collective_id=0, has_side_effects=True, vmem_limit_bytes=56 << 20
            ),
        )(bins, node.reshape(1, rows), grads.reshape(-1, LANES), hess.reshape(-1, LANES))
        best = best.reshape(NODES)
        return out - best[None, :, None], best

    return jax.shard_map(
        per_device,
        mesh=mesh,
        in_specs=(P("feat", "row"), P("row"), P("row"), P("row")),
        out_specs=(P(("feat", "row"), None, None), P()),
        check_vma=False,
    )
```

```python
import functools
import jax
import jax.numpy as jnp
from jax import lax
from jax.experimental import pallas as pl
from jax.experimental.pallas import tpu as pltpu
from jax.sharding import PartitionSpec as P

BINS = 256
NODES = 8
LANES = 128
SUBLANES = 8
LOW = 64
TILE = 256
GROUP = TILE // LOW
HALVES = LANES // LOW
TOPS = BINS // LANES
SLOTS = NODES * TOPS
LINES = 2 * SLOTS
MESH = pl.DeviceIdType.MESH
F8 = jnp.float8_e4m3fn
SLOT = 256
PACK = 4
CHUNK = 8
DIGIT = 32


def partner(me, k, n):
    if n & (n - 1):
        return (me + k) % n
    out, weight = 0, 1
    while weight < n:
        out = out + (((me // weight) % 2 + (k // weight) % 2) % 2) * weight
        weight *= 2
    return out


def direct(
    n, m, block, chunks, bins_hbm, node_ref, g_ref, h_ref, out_ref, best_ref,
    bins_buf, high_ref, low_ref, g_all, h_all, acc_ref, stage, landed, row_best, feat_best,
    load_sem, send_sem, recv_sem, row_send, row_recv, feat_send, feat_recv,
):
    rows = bins_buf.shape[2]
    me = lax.axis_index("row")
    mine = lax.axis_index("feat")
    steps = n * chunks
    sent = (n - 1) * chunks

    def place_of(s):
        return (partner(me, n - 1 - s // chunks, n) * chunks + s % chunks) * block

    def load(s):
        start = pl.multiple_of((place_of(s) // SUBLANES) * SUBLANES, SUBLANES)
        return pltpu.make_async_copy(
            bins_hbm.at[pl.ds(start, bins_buf.shape[1]), :], bins_buf.at[s % 2], load_sem.at[s % 2]
        )

    def send(s):
        k = n - 1 - s // chunks
        return pltpu.make_async_remote_copy(
            src_ref=stage.at[s],
            dst_ref=landed.at[s],
            send_sem=send_sem.at[s],
            recv_sem=recv_sem.at[s],
            device_id={"row": partner(me, k, n)},
            device_id_type=MESH,
        )

    load(0).start()
    barrier = pltpu.get_barrier_semaphore()
    for k in range(1, n):
        pl.semaphore_signal(barrier, inc=1, device_id={"row": (me + k) % n}, device_id_type=MESH)
    for k in range(1, m):
        pl.semaphore_signal(barrier, inc=1, device_id={"feat": (mine + k) % m}, device_id_type=MESH)

    g = g_ref[...].astype(jnp.float32)
    h = h_ref[...].astype(jnp.float32)
    for i in range(rows // LANES):
        cols = slice(i * LANES, (i + 1) * LANES)
        g_all[:, cols] = jnp.broadcast_to(g[i : i + 1, :], (SLOTS, LANES)).astype(jnp.bfloat16)
        h_all[:, cols] = jnp.broadcast_to(h[i : i + 1, :], (SLOTS, LANES)).astype(jnp.bfloat16)
    pl.semaphore_wait(barrier, n + m - 2)

    def step(s, carry):
        load(s).wait()

        @pl.when(s + 1 < steps)
        def _():
            load(s + 1).start()

        @pl.when((s >= 1) & (s <= sent))
        def _():
            send(s - 1).start()

        offset = 0 if block % SUBLANES == 0 else place_of(s) % SUBLANES
        bins = bins_buf[s % 2]
        upper = bins >= LANES
        rest = jnp.where(upper, bins - LANES, bins)
        second = rest >= LOW
        slot = node_ref[...] + jnp.where(upper, NODES, 0)
        high_ref[...] = jnp.where(second, slot + SLOTS, slot).astype(jnp.float32)
        low_ref[...] = jnp.where(second, rest - LOW, rest).astype(jnp.float32)
        place = lax.broadcasted_iota(jnp.int32, (SLOTS, rows), 0).astype(jnp.bfloat16)
        zero = jnp.zeros((SLOTS, rows), jnp.bfloat16)
        one = jnp.ones((SLOTS, rows), jnp.bfloat16)
        for first in range(0, block, GROUP):
            left, right = [], []
            for f in range(first, first + GROUP):
                row = pl.ds(offset + f, 1)
                high = jnp.broadcast_to(high_ref[row, :], (SLOTS, rows)).astype(jnp.bfloat16)
                low = jnp.broadcast_to(low_ref[row, :], (SLOTS, rows)).astype(jnp.bfloat16)
                for j in range(HALVES):
                    here = high == place + jnp.asarray(SLOTS * j, jnp.bfloat16)
                    left += [jnp.where(here, g_all[...], zero), jnp.where(here, h_all[...], zero)]
                for j in range(LOW // SLOTS):
                    here = low == place + jnp.asarray(SLOTS * j, jnp.bfloat16)
                    right.append(jnp.where(here, one, zero))
            acc_ref[...] = lax.dot_general(
                jnp.concatenate(left, 0),
                jnp.concatenate(right, 0),
                (((1,), (1,)), ((), ())),
                preferred_element_type=jnp.float32,
            )
            for i in range(GROUP):
                parts = []
                for j in range(HALVES):
                    top = (i * HALVES + j) * LINES
                    parts.append(acc_ref[top : top + LINES, i * LOW : (i + 1) * LOW])
                stage[s, first + i] = jnp.concatenate(parts, 1)
        return carry

    lax.fori_loop(0, steps, step, 0)

    def drain(s, carry):
        send(s).wait()
        return carry

    lax.fori_loop(0, sent, drain, 0)

    lane = lax.broadcasted_iota(jnp.int32, (block * 2 * TOPS * NODES, LANES), 1)

    def finish(c, top_gain):
        def add(k, total):
            return total + landed[k * chunks + c]

        x = lax.fori_loop(0, n - 1, add, stage[sent + c])
        x = x.reshape(block * LINES, LANES)
        shift = 1
        while shift < LANES:
            x = x + jnp.where(lane >= shift, pltpu.roll(x, shift, 1), 0.0)
            shift *= 2
        x = x.reshape(block, 2, TOPS, NODES, LANES)
        left, total = [], jnp.zeros((block, 2, NODES, LANES), jnp.float32)
        for t in range(TOPS):
            left.append(x[:, :, t] + total)
            total = total + jnp.broadcast_to(x[:, :, t, :, LANES - 1 :], total.shape)
        gt, ht = total[:, 0], total[:, 1]
        base = gt * gt / (ht + 1.0)
        for t in range(TOPS):
            gl, hl = left[t][:, 0], left[t][:, 1]
            gain = gl * gl / (hl + 1.0)
            gain = gain + (gt - gl) * (gt - gl) / (ht - hl + 1.0)
            gain = gain - base
            out_ref[pl.ds(c * block, block), :, t * LANES : (t + 1) * LANES] = gain
            top_gain = jnp.maximum(top_gain, jnp.max(gain, axis=0))
        return top_gain

    top_gain = lax.fori_loop(0, chunks, finish, jnp.full((NODES, LANES), -jnp.inf, jnp.float32))

    def exchange(value, slots, count, axis, index, sems, arrived):
        slots[0] = jnp.broadcast_to(jnp.max(value, axis=1, keepdims=True), (NODES, LANES))
        copies = []
        for k in range(1, count):
            copies.append(
                pltpu.make_async_remote_copy(
                    src_ref=slots.at[0],
                    dst_ref=slots.at[k],
                    send_sem=sems.at[k - 1],
                    recv_sem=arrived.at[k - 1],
                    device_id={axis: (index + k) % count},
                    device_id_type=MESH,
                )
            )
            copies[-1].start()
        for copy in copies:
            copy.wait()
        best = slots[0]
        for k in range(1, count):
            best = jnp.maximum(best, slots[k])
        return best

    best = exchange(top_gain, row_best, n, "row", me, row_send, row_recv)
    best = exchange(best, feat_best, m, "feat", mine, feat_send, feat_recv)
    across = lax.broadcasted_iota(jnp.int32, (NODES, LANES), 1)
    down = lax.broadcasted_iota(jnp.int32, (NODES, LANES), 0)
    flat = jnp.max(jnp.where(across == down, best, -jnp.inf), axis=0, keepdims=True)
    best_ref[...] = flat[:, :NODES]


def take(x, index):
    return jnp.take_along_axis(x, index, axis=1, mode="promise_in_bounds")


def regroup(
    bins_hbm, node_ref, g_ref, h_ref, words_ref, gh_ref, keep_ref, last_ref,
    bins, pieces, pattern, spots_v, spots_s, load_sem, spots_sem,
):
    f32, bf16, i32 = jnp.float32, jnp.bfloat16, jnp.int32
    tiles = node_ref.shape[0]
    groups = bins.shape[0] // 32
    chunks = tiles // CHUNK

    def load(c):
        cols = pl.ds(pl.multiple_of(c * (CHUNK * LANES), CHUNK * LANES), CHUNK * LANES)
        return pltpu.make_async_copy(bins_hbm.at[:, cols], bins.at[:, cols], load_sem.at[c])

    for c in range(chunks):
        load(c).start()
    node = node_ref[...]
    pieces[0] = g_ref[...].astype(f32)
    pieces[1] = h_ref[...].astype(f32)
    row = lax.broadcasted_iota(i32, (LANES, LANES), 0)
    col = lax.broadcasted_iota(i32, (LANES, LANES), 1)
    upper = jnp.where(row <= col, 1.0, 0.0).astype(bf16)
    ones = jnp.ones((LANES, LANES), bf16)
    above = lax.broadcasted_iota(i32, (tiles, tiles), 1) < lax.broadcasted_iota(i32, (tiles, tiles), 0)
    lower = jnp.where(above, 1.0, 0.0).astype(bf16)
    dot = functools.partial(jnp.dot, preferred_element_type=f32)
    lane = lax.broadcasted_iota(i32, (tiles, LANES), 1)
    slot = lax.broadcasted_iota(i32, keep_ref.shape, 0)
    keep = jnp.ones(keep_ref.shape, f32)
    base = jnp.zeros((1, LANES), i32)
    last = jnp.zeros((1, LANES), i32)
    dest = jnp.zeros((tiles, LANES), i32)
    spots = jnp.zeros((tiles, LANES), i32)
    for n in range(NODES):
        hit = node == n
        x = jnp.where(hit, 1.0, 0.0).astype(bf16)
        rank = dot(x, upper).astype(i32)
        count = dot(x, ones)
        ahead = dot(lower, count.astype(bf16)).astype(i32)
        count = count.astype(i32)
        total = (ahead + count)[tiles - 1 : tiles]
        start = ahead + base
        dest = jnp.where(hit, start + rank - 1, dest)
        spots = jnp.where(lane == n, start, jnp.where(lane == NODES + n, start + count, spots))
        keep = jnp.where(slot * SLOT == base, 0.0, keep)
        base = base + jnp.maximum((total + (SLOT - 1)) // SLOT, 1) * SLOT
        last = jnp.where(lane[:1] == n, base // SLOT - 1, last)
    keep_ref[...] = keep
    last_ref[...] = last
    spots_v[...] = spots
    to_scalar = pltpu.make_async_copy(spots_v, spots_s, spots_sem)
    to_scalar.start()

    spot = dest & (LANES - 1)
    sub = lax.broadcasted_iota(i32, (NODES, LANES), 0)
    across = lax.broadcasted_iota(i32, (NODES, LANES), 1)
    none = jnp.zeros((NODES, LANES), i32)
    for b in range(0, tiles, 2):
        left, right = [], []
        for i in range(2):
            here = jnp.where(jnp.broadcast_to(node[b + i : b + i + 1], (NODES, LANES)) == sub, across, 0)
            left.append(jnp.concatenate([none] * i + [here] + [none] * (1 - i), 1))
            right.append(jnp.where(jnp.broadcast_to(spot[b + i : b + i + 1], (LANES, LANES)) == row, 1.0, 0.0))
        found = lax.dot_general(
            jnp.concatenate(left, 0).astype(f32).astype(bf16),
            jnp.concatenate(right, 1).astype(bf16),
            (((1,), (1,)), ((), ())),
            preferred_element_type=f32,
        ).astype(i32)
        pattern[b] = found[:NODES]
        pattern[b + 1] = found[NODES:]
    gh_ref[...] = jnp.zeros(gh_ref.shape, f32)
    to_scalar.wait()

    def place(b):
        cols = pl.ds(pl.multiple_of(b * LANES, LANES), LANES)
        words = []
        for t in range(groups):
            word = bins[32 * t : 32 * t + SUBLANES, cols]
            for k in range(1, PACK):
                word = word | lax.shift_left(bins[32 * t + SUBLANES * k : 32 * t + SUBLANES * (k + 1), cols], 8 * k)
            words.append(word)
        for t in range(0, groups, 2):
            one, two = words[t], words[t + 1]
            words[t], words[t + 1] = jnp.where(sub < 4, one, two), jnp.where(sub < 4, two, one)
        piece = [jnp.broadcast_to(pieces[i, pl.ds(b, 1), :], (SUBLANES, LANES)) for i in range(2)]
        gh = jnp.where(sub == 0, piece[0], piece[1])
        for n in range(NODES):
            first = spots_s[b, n]
            tile = lax.shift_right_logical(first, 7)
            low = first & (LANES - 1)
            high = low + spots_s[b, NODES + n] - first
            source = jnp.broadcast_to(pattern[b, n : n + 1, :], (SUBLANES, LANES))
            near = (across >= low) & (across < high)
            far = across < high - LANES
            for t in range(groups):
                moved = take(words[t], source)
                pltpu.store(words_ref.at[tile, t], moved, mask=near)
                pltpu.store(words_ref.at[tile + 1, t], moved, mask=far)
            moved = take(gh, source)
            pltpu.store(gh_ref.at[tile], moved, mask=near)
            pltpu.store(gh_ref.at[tile + 1], moved, mask=far)

    def chunk(c, carry):
        load(c).wait()
        for j in range(CHUNK):
            place(c * CHUNK + j)
        return carry

    lax.fori_loop(0, chunks, chunk, 0)


def sweep(
    n, m, words_hbm, gh_ref, keep_ref, last_ref, out_ref, best_ref,
    words, keys, gh, snap, stage, near, relay, far, row_best, feat_best,
    load_sem, near_send, near_recv, far_send, far_recv, row_send, row_recv, feat_send, feat_recv,
):
    f32 = jnp.float32
    tiles = words.shape[1]
    slots = tiles * LANES // SLOT
    pairs = n // 2
    order = [(0, 0), (0, 1)] + [(k, h) for h in range(2) for k in range(1, pairs - 1)] + [(pairs - 1, 0), (pairs - 1, 1)]
    steps, away = 2 * pairs, 2 * (pairs - 1)
    me = lax.axis_index("row")
    mine = lax.axis_index("feat")
    chip, core = me // 2, me % 2

    def part(u, which):
        value = order[0][which]
        for i in range(1, steps):
            value = jnp.where(u >= i, order[i][which], value)
        return value

    def to_chip(u):
        return partner(chip, pairs - 1 - part(u, 0), pairs)

    def load(u, e):
        tile = 2 * to_chip(u) + part(u, 1)
        return pltpu.make_async_copy(words_hbm.at[pl.ds(0, tiles), tile], words.at[e], load_sem.at[e])

    def send_near(u):
        return pltpu.make_async_remote_copy(
            src_ref=stage.at[u],
            dst_ref=near.at[u],
            send_sem=near_send.at[u],
            recv_sem=near_recv.at[u],
            device_id={"row": 2 * chip + 1 - core},
            device_id_type=MESH,
        )

    def send_far(u):
        return pltpu.make_async_remote_copy(
            src_ref=relay.at[u],
            dst_ref=far.at[u],
            send_sem=far_send.at[u],
            recv_sem=far_recv.at[u],
            device_id={"row": 2 * to_chip(u) + core},
            device_id_type=MESH,
        )

    load(0, 0).start()
    load(1, 1).start()
    barrier = pltpu.get_barrier_semaphore()
    for k in range(1, n):
        pl.semaphore_signal(barrier, inc=1, device_id={"row": (me + k) % n}, device_id_type=MESH)
    for k in range(1, m):
        pl.semaphore_signal(barrier, inc=1, device_id={"feat": (mine + k) % m}, device_id_type=MESH)
    for p in range(2):
        for q in range(tiles):
            gh[p, :, q * LANES : (q + 1) * LANES] = jnp.broadcast_to(gh_ref[q, p : p + 1, :], (16, LANES)).astype(jnp.bfloat16)
    pl.semaphore_wait(barrier, n + m - 2)

    wide = (32, SLOT)
    down = lax.broadcasted_iota(jnp.int32, wide, 0) % SUBLANES
    high_at = (down[:16] * DIGIT).astype(jnp.int16)
    low_at = [(down + SUBLANES * j).astype(jnp.int8) for j in range(4)]
    zero, one = jnp.zeros(wide, F8), jnp.ones(wide, F8)
    nil = jnp.zeros((16, SLOT), jnp.bfloat16)
    lane = lax.broadcasted_iota(jnp.int32, (SUBLANES, LANES), 1)
    sub = lax.broadcasted_iota(jnp.int32, (SUBLANES, LANES), 0)
    byte = (lane // SUBLANES) % PACK
    of = [byte == f for f in range(PACK - 1)]

    def unpack(e, q):
        for k in range(PACK):
            keys[e, k, :, q * LANES : (q + 1) * LANES] = lax.shift_right_logical(words[e, q], 8 * k)

    def one_hots(e, w, cols):
        rows = [jnp.broadcast_to(keys[e, k, pl.ds(w, 1), cols], (SUBLANES, SLOT)) for k in range(PACK)]
        twos = [jnp.concatenate(rows[i : i + 2], 0).astype(jnp.int16) for i in (0, 2)]
        low = jnp.concatenate(rows, 0).astype(jnp.int8) & jnp.int8(DIGIT - 1)
        left = []
        for two in twos:
            apart = (two & jnp.int16(BINS - DIGIT)) != high_at
            left += [jnp.where(apart, nil, gh[v, :, cols]) for v in range(2)]
        right = [jnp.where(low != low_at[j], zero, one) for j in range(4)]
        return left, right

    def block(e, w, side, hook):
        total = [jnp.zeros((SUBLANES, LANES), f32) for _ in range(4)]
        for s in range(slots):
            cols = slice(s * SLOT, (s + 1) * SLOT)
            left0, right0 = one_hots(e, w, cols)
            left1, right1 = one_hots(e, w + 1, cols)
            found = lax.dot_general(
                jnp.concatenate(left0 + left1, 0),
                jnp.concatenate(right0 + right1, 0),
                (((1,), (1,)), ((), ())),
                preferred_element_type=f32,
            )
            kept = jnp.broadcast_to(keep_ref[s : s + 1, :], (SUBLANES, LANES))
            for q in range(2):
                square = found[64 * q : 64 * (q + 1), q * LANES : (q + 1) * LANES]
                for v in range(2):
                    piece = [square[at : at + SUBLANES] for at in (16 * v, 16 * v + 8, 16 * v + 32, 16 * v + 40)]
                    dense = jnp.where(of[0], piece[0], jnp.where(of[1], piece[1], jnp.where(of[2], piece[2], piece[3])))
                    at = 2 * q + v
                    total[at] = total[at] * kept + dense
                    snap[side, s, at] = total[at]
            hook(s)

    def store(ref, u, b, side):
        for node in range(NODES):
            for at in range(4):
                ref[u, b, node, at] = snap[side, last_ref[0, node], at]

    def merge(u):
        for b in range(2):
            for node in range(NODES):
                for at in range(4):
                    relay[u, b, node, at] += near[u, b, node, at]

    middle = min(6, slots - 1)
    load(0, 0).wait()
    for q in range(tiles):
        unpack(0, q)

    def step(u, e):
        @pl.when(u >= 2)
        def _():
            send_near(u - 2).wait_recv()
            merge(u - 2)

        @pl.when(u >= 1)
        def _():
            send_near(u - 1).start()

        @pl.when(u < steps - 1)
        def _():
            load(u + 1, 1 - e).wait()

        @pl.when(u < steps - 2)
        def _():
            load(u + 2, e).start()

        @pl.when((u >= 2) & (u - 2 < away))
        def _():
            send_far(u - 2).start()

        half = part(u, 1)
        give = 4 * ((1 - core + half) % 2)
        hold = 4 * ((core + half) % 2)

        def at_middle(*args):
            def hook(s):
                if s == middle:
                    store(*args)

            return hook

        def third(s):
            if s == middle:
                store(stage, u, 1, 1)
            for q in range(2 * s, 2 * s + 2):
                unpack(1 - e, q)

        block(e, give, 0, at_middle(relay, jnp.maximum(u - 1, 0), 1, 1))
        block(e, give + 2, 1, at_middle(stage, u, 0, 0))
        block(e, hold, 0, third)
        block(e, hold + 2, 1, at_middle(relay, u, 0, 0))

    def both(i, carry):
        step(2 * i, 0)
        step(2 * i + 1, 1)
        return carry

    lax.fori_loop(0, pairs, both, 0)
    send_near(steps - 1).start()
    store(relay, steps - 1, 1, 1)

    tens, units = lane // (SUBLANES * PACK), lane % SUBLANES
    end_of_run = lane - units + (SUBLANES - 1)
    end_of_row = (LANES - DIGIT) + byte * SUBLANES + (SUBLANES - 1)

    def running(x):
        for shift in (1, 2, 4):
            x = x + jnp.where(units >= shift, pltpu.roll(x, shift, 1), 0.0)
        run = take(x, end_of_run)
        for j in range(1, 4):
            x = x + jnp.where(tens >= j, pltpu.roll(run, j * DIGIT, 1), 0.0)
        row = take(x, end_of_row)
        whole = row
        for shift in (1, 2, 4):
            whole = whole + jnp.where(sub >= shift, pltpu.roll(whole, shift, 0), 0.0)
        return x + (whole - row), jnp.broadcast_to(whole[SUBLANES - 1 :], whole.shape)

    def gains(h, best):
        u = steps - 2 + h
        sources = [v for v in range(away) if order[v][1] == h]
        send_near(u).wait_recv()
        for v in sources:
            send_far(v).wait_recv()

        def one_block(b, best):
            tops = []
            for node in range(NODES):
                for q in range(2):
                    sums = []
                    for at in (2 * q, 2 * q + 1):
                        x = relay[u, b, node, at] + near[u, b, node, at]
                        for v in sources:
                            x = x + far[v, b, node, at]
                        sums.append(running(x))
                    (gl, gt), (hl, ht) = sums
                    gain = gl * gl / (hl + 1.0)
                    gain = gain + (gt - gl) * (gt - gl) / (ht - hl + 1.0)
                    gain = gain - gt * gt / (ht + 1.0)
                    relay[u, b, node, 2 * q] = gain
                    top = gain if q == 0 else jnp.maximum(top, gain)
                tops.append(jnp.max(top, axis=0))
            return jnp.maximum(best, jnp.stack(tops, 0))

        return lax.fori_loop(0, 2, one_block, best)

    def layout(h):
        u = steps - 2 + h

        def one_block(b, carry):
            for q in range(2):
                turned = jnp.swapaxes(jnp.stack([relay[u, b, node, 2 * q] for node in range(NODES)], 0), 0, 1)
                for f in range(PACK):
                    source = ((lane // SUBLANES) % 4) * DIGIT + f * SUBLANES + units
                    for t in range(TOPS):
                        piece = [take(turned[4 * t + j], source) for j in range(4)]
                        line = jnp.where(tens == 0, piece[0], jnp.where(tens == 1, piece[1], jnp.where(tens == 2, piece[2], piece[3])))
                        feature = SUBLANES * f + 4 * ((core + h) % 2) + 2 * b + q
                        out_ref[feature, :, t * LANES : (t + 1) * LANES] = line
            return carry

        lax.fori_loop(0, 2, one_block, 0)

    def exchange(value, parts, count, axis, index, sems, arrived, during):
        parts[0] = jnp.broadcast_to(jnp.max(value, axis=1, keepdims=True), (NODES, LANES))
        copies = []
        for k in range(1, count):
            copies.append(
                pltpu.make_async_remote_copy(
                    src_ref=parts.at[0],
                    dst_ref=parts.at[k],
                    send_sem=sems.at[k - 1],
                    recv_sem=arrived.at[k - 1],
                    device_id={axis: (index + k) % count},
                    device_id_type=MESH,
                )
            )
            copies[-1].start()
        during()
        for copy in copies:
            copy.wait()
        best = parts[0]
        for k in range(1, count):
            best = jnp.maximum(best, parts[k])
        return best

    top_gain = jnp.full((NODES, LANES), -jnp.inf, f32)
    send_near(steps - 2).wait_send()
    for h in range(2):
        top_gain = gains(h, top_gain)
    best = exchange(top_gain, row_best, n, "row", me, row_send, row_recv, lambda: layout(0))
    best = exchange(best, feat_best, m, "feat", mine, feat_send, feat_recv, lambda: layout(1))
    flat = jnp.max(jnp.where(lane == sub, best, -jnp.inf), axis=0, keepdims=True)
    best_ref[...] = flat[:, :NODES]
    for u in range(steps):
        if u != steps - 2:
            send_near(u).wait_send()
        if u < away:
            send_far(u).wait_send()


def grouped(n, m, bins, grads, hess, node):
    features, rows = bins.shape
    groups, tiles = features // 32, rows // LANES
    slots = rows // SLOT + NODES - 1
    held = 2 * slots
    vmem = pl.BlockSpec(memory_space=pltpu.VMEM)
    smem = pl.BlockSpec(memory_space=pltpu.SMEM)
    hbm = pl.BlockSpec(memory_space=pl.ANY)
    words, gh, keep, last = pl.pallas_call(
        regroup,
        in_specs=[hbm, vmem, vmem, vmem],
        out_specs=(vmem, vmem, vmem, vmem),
        out_shape=(
            jax.ShapeDtypeStruct((held + 1, groups, SUBLANES, LANES), jnp.int32),
            jax.ShapeDtypeStruct((held + 1, SUBLANES, LANES), jnp.float32),
            jax.ShapeDtypeStruct((-(-slots // SUBLANES) * SUBLANES, LANES), jnp.float32),
            jax.ShapeDtypeStruct((1, LANES), jnp.int32),
        ),
        scratch_shapes=[
            pltpu.VMEM((features, rows), jnp.int32),
            pltpu.VMEM((2, tiles, LANES), jnp.float32),
            pltpu.VMEM((tiles, NODES, LANES), jnp.int32),
            pltpu.VMEM((tiles, LANES), jnp.int32),
            pltpu.SMEM((tiles, LANES), jnp.int32),
            pltpu.SemaphoreType.DMA((tiles // CHUNK,)),
            pltpu.SemaphoreType.DMA,
        ],
        compiler_params=pltpu.CompilerParams(vmem_limit_bytes=56 << 20),
    )(bins, node.reshape(-1, LANES), grads.reshape(-1, LANES), hess.reshape(-1, LANES))
    pairs = n // 2
    piece = (2, NODES, 4, SUBLANES, LANES)
    steps, away = 2 * pairs, 2 * (pairs - 1)
    out, best = pl.pallas_call(
        functools.partial(sweep, n, m),
        in_specs=[hbm, vmem, vmem, smem],
        out_specs=(vmem, vmem),
        out_shape=(
            jax.ShapeDtypeStruct((32, NODES, BINS), jnp.float32),
            jax.ShapeDtypeStruct((1, NODES), jnp.float32),
        ),
        scratch_shapes=[
            pltpu.VMEM((2, held, SUBLANES, LANES), jnp.int32),
            pltpu.VMEM((2, PACK, SUBLANES, held * LANES), jnp.int32),
            pltpu.VMEM((2, 16, held * LANES), jnp.bfloat16),
            pltpu.VMEM((2, slots, 4, SUBLANES, LANES), jnp.float32),
            pltpu.VMEM((steps,) + piece, jnp.float32),
            pltpu.VMEM((steps,) + piece, jnp.float32),
            pltpu.VMEM((steps,) + piece, jnp.float32),
            pltpu.VMEM((away,) + piece, jnp.float32),
            pltpu.VMEM((n, NODES, LANES), jnp.float32),
            pltpu.VMEM((m, NODES, LANES), jnp.float32),
            pltpu.SemaphoreType.DMA((2,)),
            pltpu.SemaphoreType.DMA((steps,)),
            pltpu.SemaphoreType.DMA((steps,)),
            pltpu.SemaphoreType.DMA((away,)),
            pltpu.SemaphoreType.DMA((away,)),
            pltpu.SemaphoreType.DMA((n - 1,)),
            pltpu.SemaphoreType.DMA((n - 1,)),
            pltpu.SemaphoreType.DMA((m - 1,)),
            pltpu.SemaphoreType.DMA((m - 1,)),
        ],
        compiler_params=pltpu.CompilerParams(
            collective_id=0, has_side_effects=True, vmem_limit_bytes=56 << 20
        ),
    )(words, gh, keep, last)
    best = best.reshape(NODES)
    return out - best[None, :, None], best


def solution(mesh):
    n, m = mesh.shape["row"], mesh.shape["feat"]

    def per_device(bins, grads, hess, node):
        features, rows = bins.shape
        own = features // n
        if own == 32 and n % 2 == 0 and n > 2 and rows % (CHUNK * LANES) == 0:
            return grouped(n, m, bins, grads, hess, node)
        block = own if own < SUBLANES else next(b for b in (2 * SUBLANES, SUBLANES) if own % b == 0)
        held = max(block, SUBLANES)
        chunks = own // block
        vmem = pl.BlockSpec(memory_space=pltpu.VMEM)
        piece = (block, LINES, LANES)
        out, best = pl.pallas_call(
            functools.partial(direct, n, m, block, chunks),
            in_specs=[pl.BlockSpec(memory_space=pl.ANY), vmem, vmem, vmem],
            out_specs=(vmem, vmem),
            out_shape=(
                jax.ShapeDtypeStruct((own, NODES, BINS), jnp.float32),
                jax.ShapeDtypeStruct((1, NODES), jnp.float32),
            ),
            scratch_shapes=[
                pltpu.VMEM((2, held, rows), jnp.int32),
                pltpu.VMEM((held, rows), jnp.float32),
                pltpu.VMEM((held, rows), jnp.float32),
                pltpu.VMEM((SLOTS, rows), jnp.bfloat16),
                pltpu.VMEM((SLOTS, rows), jnp.bfloat16),
                pltpu.VMEM((GROUP * HALVES * LINES, TILE), jnp.float32),
                pltpu.VMEM((n * chunks,) + piece, jnp.float32),
                pltpu.VMEM(((n - 1) * chunks,) + piece, jnp.float32),
                pltpu.VMEM((n, NODES, LANES), jnp.float32),
                pltpu.VMEM((m, NODES, LANES), jnp.float32),
                pltpu.SemaphoreType.DMA((2,)),
                pltpu.SemaphoreType.DMA(((n - 1) * chunks,)),
                pltpu.SemaphoreType.DMA(((n - 1) * chunks,)),
                pltpu.SemaphoreType.DMA((n - 1,)),
                pltpu.SemaphoreType.DMA((n - 1,)),
                pltpu.SemaphoreType.DMA((m - 1,)),
                pltpu.SemaphoreType.DMA((m - 1,)),
            ],
            compiler_params=pltpu.CompilerParams(
                collective_id=0, has_side_effects=True, vmem_limit_bytes=56 << 20
            ),
        )(bins, node.reshape(1, rows), grads.reshape(-1, LANES), hess.reshape(-1, LANES))
        best = best.reshape(NODES)
        return out - best[None, :, None], best

    return jax.shard_map(
        per_device,
        mesh=mesh,
        in_specs=(P("feat", "row"), P("row"), P("row"), P("row")),
        out_specs=(P(("feat", "row"), None, None), P()),
        check_vma=False,
    )
```

```python
import functools
import jax
import jax.numpy as jnp
from jax import lax
from jax.experimental import pallas as pl
from jax.experimental.pallas import tpu as pltpu
from jax.sharding import PartitionSpec as P

BINS = 256
NODES = 8
LANES = 128
SUBLANES = 8
LOW = 64
TILE = 256
GROUP = TILE // LOW
HALVES = LANES // LOW
TOPS = BINS // LANES
SLOTS = NODES * TOPS
LINES = 2 * SLOTS
MESH = pl.DeviceIdType.MESH
F8 = jnp.float8_e4m3fn
SLOT = 256
PACK = 4
CHUNK = 8
DIGIT = 32


def partner(me, k, n):
    if n & (n - 1):
        return (me + k) % n
    out, weight = 0, 1
    while weight < n:
        out = out + (((me // weight) % 2 + (k // weight) % 2) % 2) * weight
        weight *= 2
    return out


def direct(
    n, m, block, chunks, bins_hbm, node_ref, g_ref, h_ref, out_ref, best_ref,
    bins_buf, high_ref, low_ref, g_all, h_all, acc_ref, stage, landed, row_best, feat_best,
    load_sem, send_sem, recv_sem, row_send, row_recv, feat_send, feat_recv,
):
    rows = bins_buf.shape[2]
    me = lax.axis_index("row")
    mine = lax.axis_index("feat")
    steps = n * chunks
    sent = (n - 1) * chunks

    def place_of(s):
        return (partner(me, n - 1 - s // chunks, n) * chunks + s % chunks) * block

    def load(s):
        start = pl.multiple_of((place_of(s) // SUBLANES) * SUBLANES, SUBLANES)
        return pltpu.make_async_copy(
            bins_hbm.at[pl.ds(start, bins_buf.shape[1]), :], bins_buf.at[s % 2], load_sem.at[s % 2]
        )

    def send(s):
        k = n - 1 - s // chunks
        return pltpu.make_async_remote_copy(
            src_ref=stage.at[s],
            dst_ref=landed.at[s],
            send_sem=send_sem.at[s],
            recv_sem=recv_sem.at[s],
            device_id={"row": partner(me, k, n)},
            device_id_type=MESH,
        )

    load(0).start()
    barrier = pltpu.get_barrier_semaphore()
    for k in range(1, n):
        pl.semaphore_signal(barrier, inc=1, device_id={"row": (me + k) % n}, device_id_type=MESH)
    for k in range(1, m):
        pl.semaphore_signal(barrier, inc=1, device_id={"feat": (mine + k) % m}, device_id_type=MESH)

    g = g_ref[...].astype(jnp.float32)
    h = h_ref[...].astype(jnp.float32)
    for i in range(rows // LANES):
        cols = slice(i * LANES, (i + 1) * LANES)
        g_all[:, cols] = jnp.broadcast_to(g[i : i + 1, :], (SLOTS, LANES)).astype(jnp.bfloat16)
        h_all[:, cols] = jnp.broadcast_to(h[i : i + 1, :], (SLOTS, LANES)).astype(jnp.bfloat16)
    pl.semaphore_wait(barrier, n + m - 2)

    def step(s, carry):
        load(s).wait()

        @pl.when(s + 1 < steps)
        def _():
            load(s + 1).start()

        @pl.when((s >= 1) & (s <= sent))
        def _():
            send(s - 1).start()

        offset = 0 if block % SUBLANES == 0 else place_of(s) % SUBLANES
        bins = bins_buf[s % 2]
        upper = bins >= LANES
        rest = jnp.where(upper, bins - LANES, bins)
        second = rest >= LOW
        slot = node_ref[...] + jnp.where(upper, NODES, 0)
        high_ref[...] = jnp.where(second, slot + SLOTS, slot).astype(jnp.float32)
        low_ref[...] = jnp.where(second, rest - LOW, rest).astype(jnp.float32)
        place = lax.broadcasted_iota(jnp.int32, (SLOTS, rows), 0).astype(jnp.bfloat16)
        zero = jnp.zeros((SLOTS, rows), jnp.bfloat16)
        one = jnp.ones((SLOTS, rows), jnp.bfloat16)
        for first in range(0, block, GROUP):
            left, right = [], []
            for f in range(first, first + GROUP):
                row = pl.ds(offset + f, 1)
                high = jnp.broadcast_to(high_ref[row, :], (SLOTS, rows)).astype(jnp.bfloat16)
                low = jnp.broadcast_to(low_ref[row, :], (SLOTS, rows)).astype(jnp.bfloat16)
                for j in range(HALVES):
                    here = high == place + jnp.asarray(SLOTS * j, jnp.bfloat16)
                    left += [jnp.where(here, g_all[...], zero), jnp.where(here, h_all[...], zero)]
                for j in range(LOW // SLOTS):
                    here = low == place + jnp.asarray(SLOTS * j, jnp.bfloat16)
                    right.append(jnp.where(here, one, zero))
            acc_ref[...] = lax.dot_general(
                jnp.concatenate(left, 0),
                jnp.concatenate(right, 0),
                (((1,), (1,)), ((), ())),
                preferred_element_type=jnp.float32,
            )
            for i in range(GROUP):
                parts = []
                for j in range(HALVES):
                    top = (i * HALVES + j) * LINES
                    parts.append(acc_ref[top : top + LINES, i * LOW : (i + 1) * LOW])
                stage[s, first + i] = jnp.concatenate(parts, 1)
        return carry

    lax.fori_loop(0, steps, step, 0)

    def drain(s, carry):
        send(s).wait()
        return carry

    lax.fori_loop(0, sent, drain, 0)

    lane = lax.broadcasted_iota(jnp.int32, (block * 2 * TOPS * NODES, LANES), 1)

    def finish(c, top_gain):
        def add(k, total):
            return total + landed[k * chunks + c]

        x = lax.fori_loop(0, n - 1, add, stage[sent + c])
        x = x.reshape(block * LINES, LANES)
        shift = 1
        while shift < LANES:
            x = x + jnp.where(lane >= shift, pltpu.roll(x, shift, 1), 0.0)
            shift *= 2
        x = x.reshape(block, 2, TOPS, NODES, LANES)
        left, total = [], jnp.zeros((block, 2, NODES, LANES), jnp.float32)
        for t in range(TOPS):
            left.append(x[:, :, t] + total)
            total = total + jnp.broadcast_to(x[:, :, t, :, LANES - 1 :], total.shape)
        gt, ht = total[:, 0], total[:, 1]
        base = gt * gt / (ht + 1.0)
        for t in range(TOPS):
            gl, hl = left[t][:, 0], left[t][:, 1]
            gain = gl * gl / (hl + 1.0)
            gain = gain + (gt - gl) * (gt - gl) / (ht - hl + 1.0)
            gain = gain - base
            out_ref[pl.ds(c * block, block), :, t * LANES : (t + 1) * LANES] = gain
            top_gain = jnp.maximum(top_gain, jnp.max(gain, axis=0))
        return top_gain

    top_gain = lax.fori_loop(0, chunks, finish, jnp.full((NODES, LANES), -jnp.inf, jnp.float32))

    def exchange(value, slots, count, axis, index, sems, arrived):
        slots[0] = jnp.broadcast_to(jnp.max(value, axis=1, keepdims=True), (NODES, LANES))
        copies = []
        for k in range(1, count):
            copies.append(
                pltpu.make_async_remote_copy(
                    src_ref=slots.at[0],
                    dst_ref=slots.at[k],
                    send_sem=sems.at[k - 1],
                    recv_sem=arrived.at[k - 1],
                    device_id={axis: (index + k) % count},
                    device_id_type=MESH,
                )
            )
            copies[-1].start()
        for copy in copies:
            copy.wait()
        best = slots[0]
        for k in range(1, count):
            best = jnp.maximum(best, slots[k])
        return best

    best = exchange(top_gain, row_best, n, "row", me, row_send, row_recv)
    best = exchange(best, feat_best, m, "feat", mine, feat_send, feat_recv)
    across = lax.broadcasted_iota(jnp.int32, (NODES, LANES), 1)
    down = lax.broadcasted_iota(jnp.int32, (NODES, LANES), 0)
    flat = jnp.max(jnp.where(across == down, best, -jnp.inf), axis=0, keepdims=True)
    best_ref[...] = flat[:, :NODES]


def take(x, index):
    return jnp.take_along_axis(x, index, axis=1, mode="promise_in_bounds")


def regroup(
    bins_hbm, node_ref, g_ref, h_ref, words_ref, gh_ref, keep_ref, last_ref,
    bins, pieces, pattern, spots_v, spots_s, load_sem, spots_sem,
):
    f32, bf16, i32 = jnp.float32, jnp.bfloat16, jnp.int32
    tiles = node_ref.shape[0]
    groups = bins.shape[0] // 32
    chunks = tiles // CHUNK

    def load(c):
        cols = pl.ds(pl.multiple_of(c * (CHUNK * LANES), CHUNK * LANES), CHUNK * LANES)
        return pltpu.make_async_copy(bins_hbm.at[:, cols], bins.at[:, cols], load_sem.at[c])

    for c in range(chunks):
        load(c).start()
    node = node_ref[...]
    pieces[0] = g_ref[...].astype(f32)
    pieces[1] = h_ref[...].astype(f32)
    row = lax.broadcasted_iota(i32, (LANES, LANES), 0)
    col = lax.broadcasted_iota(i32, (LANES, LANES), 1)
    upper = jnp.where(row <= col, 1.0, 0.0).astype(bf16)
    ones = jnp.ones((LANES, LANES), bf16)
    above = lax.broadcasted_iota(i32, (tiles, tiles), 1) < lax.broadcasted_iota(i32, (tiles, tiles), 0)
    lower = jnp.where(above, 1.0, 0.0).astype(bf16)
    dot = functools.partial(jnp.dot, preferred_element_type=f32)
    lane = lax.broadcasted_iota(i32, (tiles, LANES), 1)
    slot = lax.broadcasted_iota(i32, keep_ref.shape, 0)
    keep = jnp.ones(keep_ref.shape, f32)
    base = jnp.zeros((1, LANES), i32)
    last = jnp.zeros((1, LANES), i32)
    dest = jnp.zeros((tiles, LANES), i32)
    spots = jnp.zeros((tiles, LANES), i32)
    for n in range(NODES):
        hit = node == n
        x = jnp.where(hit, 1.0, 0.0).astype(bf16)
        rank = dot(x, upper).astype(i32)
        count = dot(x, ones)
        ahead = dot(lower, count.astype(bf16)).astype(i32)
        count = count.astype(i32)
        total = (ahead + count)[tiles - 1 : tiles]
        start = ahead + base
        dest = jnp.where(hit, start + rank - 1, dest)
        spots = jnp.where(lane == n, start, jnp.where(lane == NODES + n, start + count, spots))
        keep = jnp.where(slot * SLOT == base, 0.0, keep)
        base = base + jnp.maximum((total + (SLOT - 1)) // SLOT, 1) * SLOT
        last = jnp.where(lane[:1] == n, base // SLOT - 1, last)
    keep_ref[...] = keep
    last_ref[...] = last
    spots_v[...] = spots
    to_scalar = pltpu.make_async_copy(spots_v, spots_s, spots_sem)
    to_scalar.start()

    spot = dest & (LANES - 1)
    sub = lax.broadcasted_iota(i32, (NODES, LANES), 0)
    across = lax.broadcasted_iota(i32, (NODES, LANES), 1)
    none = jnp.zeros((NODES, LANES), i32)
    for b in range(0, tiles, 2):
        left, right = [], []
        for i in range(2):
            here = jnp.where(jnp.broadcast_to(node[b + i : b + i + 1], (NODES, LANES)) == sub, across, 0)
            left.append(jnp.concatenate([none] * i + [here] + [none] * (1 - i), 1))
            right.append(jnp.where(jnp.broadcast_to(spot[b + i : b + i + 1], (LANES, LANES)) == row, 1.0, 0.0))
        found = lax.dot_general(
            jnp.concatenate(left, 0).astype(f32).astype(bf16),
            jnp.concatenate(right, 1).astype(bf16),
            (((1,), (1,)), ((), ())),
            preferred_element_type=f32,
        ).astype(i32)
        pattern[b] = found[:NODES]
        pattern[b + 1] = found[NODES:]
    gh_ref[...] = jnp.zeros(gh_ref.shape, f32)
    to_scalar.wait()

    def place(b):
        cols = pl.ds(pl.multiple_of(b * LANES, LANES), LANES)
        words = []
        for t in range(groups):
            word = bins[32 * t : 32 * t + SUBLANES, cols]
            for k in range(1, PACK):
                word = word | lax.shift_left(bins[32 * t + SUBLANES * k : 32 * t + SUBLANES * (k + 1), cols], 8 * k)
            words.append(word)
        for t in range(0, groups, 2):
            one, two = words[t], words[t + 1]
            words[t], words[t + 1] = jnp.where(sub < 4, one, two), jnp.where(sub < 4, two, one)
        piece = [jnp.broadcast_to(pieces[i, pl.ds(b, 1), :], (SUBLANES, LANES)) for i in range(2)]
        gh = jnp.where(sub == 0, piece[0], piece[1])
        for n in range(NODES):
            first = spots_s[b, n]
            tile = lax.shift_right_logical(first, 7)
            low = first & (LANES - 1)
            high = low + spots_s[b, NODES + n] - first
            source = jnp.broadcast_to(pattern[b, n : n + 1, :], (SUBLANES, LANES))
            near = (across >= low) & (across < high)
            far = across < high - LANES
            for t in range(groups):
                moved = take(words[t], source)
                pltpu.store(words_ref.at[tile, t], moved, mask=near)
                pltpu.store(words_ref.at[tile + 1, t], moved, mask=far)
            moved = take(gh, source)
            pltpu.store(gh_ref.at[tile], moved, mask=near)
            pltpu.store(gh_ref.at[tile + 1], moved, mask=far)

    def chunk(c, carry):
        load(c).wait()
        for j in range(CHUNK):
            place(c * CHUNK + j)
        return carry

    lax.fori_loop(0, chunks, chunk, 0)


def sweep(
    n, m, words_hbm, gh_ref, keep_ref, last_ref, out_ref, best_ref,
    words, keys, gh, snap, stage, near, relay, far, row_best, feat_best,
    load_sem, near_send, near_recv, far_send, far_recv, row_send, row_recv, feat_send, feat_recv,
):
    f32 = jnp.float32
    tiles = words.shape[1]
    slots = tiles * LANES // SLOT
    pairs = n // 2
    order = ((0, 0), (0, 1), (2, 0), (1, 1), (1, 0), (2, 1), (3, 0), (3, 1))
    route = (2, 1, 2, 1, 1, 2, 3, 3)
    steps, away = 2 * pairs, 2 * (pairs - 1)
    me = lax.axis_index("row")
    mine = lax.axis_index("feat")
    chip, core = me // 2, me % 2

    def pick(u, table):
        value = table[0]
        for i in range(1, steps):
            value = jnp.where(u >= i, table[i], value)
        return value

    def half_of(u):
        return pick(u, [h for _, h in order])

    def chip_at(k):
        return partner(chip, pairs - 1 - k, pairs)

    def load(u, e):
        tile = 2 * chip_at(pick(u, [k for k, _ in order])) + half_of(u)
        return pltpu.make_async_copy(words_hbm.at[pl.ds(0, tiles), tile], words.at[e], load_sem.at[e])

    def send_near(u):
        return pltpu.make_async_remote_copy(
            src_ref=stage.at[u],
            dst_ref=near.at[u],
            send_sem=near_send.at[u],
            recv_sem=near_recv.at[u],
            device_id={"row": 2 * chip + 1 - core},
            device_id_type=MESH,
        )

    def send_far(u):
        return pltpu.make_async_remote_copy(
            src_ref=relay.at[u],
            dst_ref=far.at[u],
            send_sem=far_send.at[u],
            recv_sem=far_recv.at[u],
            device_id={"row": 2 * chip_at(pick(u, route)) + core},
            device_id_type=MESH,
        )

    load(0, 0).start()
    load(1, 1).start()
    barrier = pltpu.get_barrier_semaphore()
    for k in range(1, n):
        pl.semaphore_signal(barrier, inc=1, device_id={"row": (me + k) % n}, device_id_type=MESH)
    for k in range(1, m):
        pl.semaphore_signal(barrier, inc=1, device_id={"feat": (mine + k) % m}, device_id_type=MESH)
    for p in range(2):
        for q in range(tiles):
            gh[p, :, q * LANES : (q + 1) * LANES] = jnp.broadcast_to(gh_ref[q, p : p + 1, :], (16, LANES)).astype(jnp.bfloat16)
    pl.semaphore_wait(barrier, n + m - 2)

    wide = (32, SLOT)
    down = lax.broadcasted_iota(jnp.int32, wide, 0) % SUBLANES
    high_at = (down[:16] * DIGIT).astype(jnp.int16)
    low_at = [(down + SUBLANES * j).astype(jnp.int8) for j in range(4)]
    zero, one = jnp.zeros(wide, F8), jnp.ones(wide, F8)
    nil = jnp.zeros((16, SLOT), jnp.bfloat16)
    lane = lax.broadcasted_iota(jnp.int32, (SUBLANES, LANES), 1)
    sub = lax.broadcasted_iota(jnp.int32, (SUBLANES, LANES), 0)
    byte = (lane // SUBLANES) % PACK
    of = [byte == f for f in range(PACK - 1)]

    def unpack(e, q):
        for k in range(PACK):
            keys[e, k, :, q * LANES : (q + 1) * LANES] = lax.shift_right_logical(words[e, q], 8 * k)

    def one_hots(e, w, cols):
        rows = [jnp.broadcast_to(keys[e, k, pl.ds(w, 1), cols], (SUBLANES, SLOT)) for k in range(PACK)]
        twos = [jnp.concatenate(rows[i : i + 2], 0).astype(jnp.int16) for i in (0, 2)]
        low = jnp.concatenate(rows, 0).astype(jnp.int8) & jnp.int8(DIGIT - 1)
        left = []
        for two in twos:
            apart = (two & jnp.int16(BINS - DIGIT)) != high_at
            left += [jnp.where(apart, nil, gh[v, :, cols]) for v in range(2)]
        right = [jnp.where(low != low_at[j], zero, one) for j in range(4)]
        return left, right

    def block(e, w, side, hook):
        total = [jnp.zeros((SUBLANES, LANES), f32) for _ in range(4)]
        for s in range(slots):
            cols = slice(s * SLOT, (s + 1) * SLOT)
            left0, right0 = one_hots(e, w, cols)
            left1, right1 = one_hots(e, w + 1, cols)
            found = lax.dot_general(
                jnp.concatenate(left0 + left1, 0),
                jnp.concatenate(right0 + right1, 0),
                (((1,), (1,)), ((), ())),
                preferred_element_type=f32,
            )
            kept = jnp.broadcast_to(keep_ref[s : s + 1, :], (SUBLANES, LANES))
            for q in range(2):
                square = found[64 * q : 64 * (q + 1), q * LANES : (q + 1) * LANES]
                for v in range(2):
                    piece = [square[at : at + SUBLANES] for at in (16 * v, 16 * v + 8, 16 * v + 32, 16 * v + 40)]
                    dense = jnp.where(of[0], piece[0], jnp.where(of[1], piece[1], jnp.where(of[2], piece[2], piece[3])))
                    at = 2 * q + v
                    total[at] = total[at] * kept + dense
                    snap[side, s, at] = total[at]
            hook(s)

    def store(ref, u, b, side):
        for node in range(NODES):
            for at in range(4):
                ref[u, b, node, at] = snap[side, last_ref[0, node], at]

    def merge(u, ref, v):
        for b in range(2):
            for node in range(NODES):
                for at in range(4):
                    relay[u, b, node, at] += ref[v, b, node, at]

    middle = min(6, slots - 1)
    load(0, 0).wait()
    for q in range(tiles):
        unpack(0, q)

    def step(u, e):
        @pl.when(u >= 1)
        def _():
            send_near(u - 1).start()

        @pl.when(u >= 2)
        def _():
            send_near(u - 2).wait_recv()
            merge(u - 2, near, u - 2)

        @pl.when(u >= away)
        def _():
            send_far(u - away).wait_recv()
            merge(u - 2, far, u - away)

        @pl.when(u < steps - 1)
        def _():
            load(u + 1, 1 - e).wait()

        @pl.when(u < steps - 2)
        def _():
            load(u + 2, e).start()

        @pl.when((u >= 2) & (u - 2 < away))
        def _():
            send_far(u - 2).start()

        half = half_of(u)
        give = 4 * ((1 - core + half) % 2)
        hold = 4 * ((core + half) % 2)

        def at_middle(*args):
            def hook(s):
                if s == middle:
                    store(*args)

            return hook

        def third(s):
            if s == middle:
                store(stage, u, 1, 1)
            for q in range(2 * s, 2 * s + 2):
                unpack(1 - e, q)

        block(e, give, 0, at_middle(relay, jnp.maximum(u - 1, 0), 1, 1))
        block(e, give + 2, 1, at_middle(stage, u, 0, 0))
        block(e, hold, 0, third)
        block(e, hold + 2, 1, at_middle(relay, u, 0, 0))

    def both(i, carry):
        step(2 * i, 0)
        step(2 * i + 1, 1)
        return carry

    lax.fori_loop(0, pairs, both, 0)
    send_near(steps - 1).start()
    store(relay, steps - 1, 1, 1)

    tens, units = lane // (SUBLANES * PACK), lane % SUBLANES
    end_of_run = lane - units + (SUBLANES - 1)
    end_of_row = (LANES - DIGIT) + byte * SUBLANES + (SUBLANES - 1)

    def running(x):
        for shift in (1, 2, 4):
            x = x + jnp.where(units >= shift, pltpu.roll(x, shift, 1), 0.0)
        run = take(x, end_of_run)
        for j in range(1, 4):
            x = x + jnp.where(tens >= j, pltpu.roll(run, j * DIGIT, 1), 0.0)
        row = take(x, end_of_row)
        whole = row
        for shift in (1, 2, 4):
            whole = whole + jnp.where(sub >= shift, pltpu.roll(whole, shift, 0), 0.0)
        return x + (whole - row), jnp.broadcast_to(whole[SUBLANES - 1 :], whole.shape)

    def gains(h, best):
        u = steps - 2 + h
        sources = [v for v in range(2, away) if order[v][1] == h]
        send_near(u).wait_recv()
        for v in sources:
            send_far(v).wait_recv()

        def one_block(b, best):
            tops = []
            for node in range(NODES):
                for q in range(2):
                    sums = []
                    for at in (2 * q, 2 * q + 1):
                        x = relay[u, b, node, at] + near[u, b, node, at]
                        for v in sources:
                            x = x + far[v, b, node, at]
                        sums.append(running(x))
                    (gl, gt), (hl, ht) = sums
                    gain = gl * gl / (hl + 1.0)
                    gain = gain + (gt - gl) * (gt - gl) / (ht - hl + 1.0)
                    gain = gain - gt * gt / (ht + 1.0)
                    relay[u, b, node, 2 * q] = gain
                    top = gain if q == 0 else jnp.maximum(top, gain)
                tops.append(jnp.max(top, axis=0))
            return jnp.maximum(best, jnp.stack(tops, 0))

        return lax.fori_loop(0, 2, one_block, best)

    def layout(h):
        u = steps - 2 + h

        def one_block(b, carry):
            for q in range(2):
                turned = jnp.swapaxes(jnp.stack([relay[u, b, node, 2 * q] for node in range(NODES)], 0), 0, 1)
                for f in range(PACK):
                    source = ((lane // SUBLANES) % 4) * DIGIT + f * SUBLANES + units
                    for t in range(TOPS):
                        piece = [take(turned[4 * t + j], source) for j in range(4)]
                        line = jnp.where(tens == 0, piece[0], jnp.where(tens == 1, piece[1], jnp.where(tens == 2, piece[2], piece[3])))
                        feature = SUBLANES * f + 4 * ((core + h) % 2) + 2 * b + q
                        out_ref[feature, :, t * LANES : (t + 1) * LANES] = line
            return carry

        lax.fori_loop(0, 2, one_block, 0)

    def exchange(value, parts, count, axis, index, sems, arrived, during):
        parts[0] = jnp.broadcast_to(jnp.max(value, axis=1, keepdims=True), (NODES, LANES))
        copies = []
        for k in range(1, count):
            copies.append(
                pltpu.make_async_remote_copy(
                    src_ref=parts.at[0],
                    dst_ref=parts.at[k],
                    send_sem=sems.at[k - 1],
                    recv_sem=arrived.at[k - 1],
                    device_id={axis: (index + k) % count},
                    device_id_type=MESH,
                )
            )
            copies[-1].start()
        during()
        for copy in copies:
            copy.wait()
        best = parts[0]
        for k in range(1, count):
            best = jnp.maximum(best, parts[k])
        return best

    top_gain = jnp.full((NODES, LANES), -jnp.inf, f32)
    send_near(steps - 2).wait_send()
    for h in range(2):
        top_gain = gains(h, top_gain)
    best = exchange(top_gain, row_best, n, "row", me, row_send, row_recv, lambda: layout(0))
    best = exchange(best, feat_best, m, "feat", mine, feat_send, feat_recv, lambda: layout(1))
    flat = jnp.max(jnp.where(lane == sub, best, -jnp.inf), axis=0, keepdims=True)
    best_ref[...] = flat[:, :NODES]
    for u in range(steps):
        if u != steps - 2:
            send_near(u).wait_send()
        if u < away:
            send_far(u).wait_send()


def grouped(n, m, bins, grads, hess, node):
    features, rows = bins.shape
    groups, tiles = features // 32, rows // LANES
    slots = rows // SLOT + NODES - 1
    held = 2 * slots
    vmem = pl.BlockSpec(memory_space=pltpu.VMEM)
    smem = pl.BlockSpec(memory_space=pltpu.SMEM)
    hbm = pl.BlockSpec(memory_space=pl.ANY)
    words, gh, keep, last = pl.pallas_call(
        regroup,
        in_specs=[hbm, vmem, vmem, vmem],
        out_specs=(vmem, vmem, vmem, vmem),
        out_shape=(
            jax.ShapeDtypeStruct((held + 1, groups, SUBLANES, LANES), jnp.int32),
            jax.ShapeDtypeStruct((held + 1, SUBLANES, LANES), jnp.float32),
            jax.ShapeDtypeStruct((-(-slots // SUBLANES) * SUBLANES, LANES), jnp.float32),
            jax.ShapeDtypeStruct((1, LANES), jnp.int32),
        ),
        scratch_shapes=[
            pltpu.VMEM((features, rows), jnp.int32),
            pltpu.VMEM((2, tiles, LANES), jnp.float32),
            pltpu.VMEM((tiles, NODES, LANES), jnp.int32),
            pltpu.VMEM((tiles, LANES), jnp.int32),
            pltpu.SMEM((tiles, LANES), jnp.int32),
            pltpu.SemaphoreType.DMA((tiles // CHUNK,)),
            pltpu.SemaphoreType.DMA,
        ],
        compiler_params=pltpu.CompilerParams(vmem_limit_bytes=56 << 20),
    )(bins, node.reshape(-1, LANES), grads.reshape(-1, LANES), hess.reshape(-1, LANES))
    pairs = n // 2
    piece = (2, NODES, 4, SUBLANES, LANES)
    steps, away = 2 * pairs, 2 * (pairs - 1)
    out, best = pl.pallas_call(
        functools.partial(sweep, n, m),
        in_specs=[hbm, vmem, vmem, smem],
        out_specs=(vmem, vmem),
        out_shape=(
            jax.ShapeDtypeStruct((32, NODES, BINS), jnp.float32),
            jax.ShapeDtypeStruct((1, NODES), jnp.float32),
        ),
        scratch_shapes=[
            pltpu.VMEM((2, held, SUBLANES, LANES), jnp.int32),
            pltpu.VMEM((2, PACK, SUBLANES, held * LANES), jnp.int32),
            pltpu.VMEM((2, 16, held * LANES), jnp.bfloat16),
            pltpu.VMEM((2, slots, 4, SUBLANES, LANES), jnp.float32),
            pltpu.VMEM((steps,) + piece, jnp.float32),
            pltpu.VMEM((steps,) + piece, jnp.float32),
            pltpu.VMEM((steps,) + piece, jnp.float32),
            pltpu.VMEM((away,) + piece, jnp.float32),
            pltpu.VMEM((n, NODES, LANES), jnp.float32),
            pltpu.VMEM((m, NODES, LANES), jnp.float32),
            pltpu.SemaphoreType.DMA((2,)),
            pltpu.SemaphoreType.DMA((steps,)),
            pltpu.SemaphoreType.DMA((steps,)),
            pltpu.SemaphoreType.DMA((away,)),
            pltpu.SemaphoreType.DMA((away,)),
            pltpu.SemaphoreType.DMA((n - 1,)),
            pltpu.SemaphoreType.DMA((n - 1,)),
            pltpu.SemaphoreType.DMA((m - 1,)),
            pltpu.SemaphoreType.DMA((m - 1,)),
        ],
        compiler_params=pltpu.CompilerParams(
            collective_id=0, has_side_effects=True, vmem_limit_bytes=56 << 20
        ),
    )(words, gh, keep, last)
    best = best.reshape(NODES)
    return out - best[None, :, None], best


def solution(mesh):
    n, m = mesh.shape["row"], mesh.shape["feat"]

    def per_device(bins, grads, hess, node):
        features, rows = bins.shape
        own = features // n
        if own == 32 and n == 8 and rows % (CHUNK * LANES) == 0:
            return grouped(n, m, bins, grads, hess, node)
        block = own if own < SUBLANES else next(b for b in (2 * SUBLANES, SUBLANES) if own % b == 0)
        held = max(block, SUBLANES)
        chunks = own // block
        vmem = pl.BlockSpec(memory_space=pltpu.VMEM)
        piece = (block, LINES, LANES)
        out, best = pl.pallas_call(
            functools.partial(direct, n, m, block, chunks),
            in_specs=[pl.BlockSpec(memory_space=pl.ANY), vmem, vmem, vmem],
            out_specs=(vmem, vmem),
            out_shape=(
                jax.ShapeDtypeStruct((own, NODES, BINS), jnp.float32),
                jax.ShapeDtypeStruct((1, NODES), jnp.float32),
            ),
            scratch_shapes=[
                pltpu.VMEM((2, held, rows), jnp.int32),
                pltpu.VMEM((held, rows), jnp.float32),
                pltpu.VMEM((held, rows), jnp.float32),
                pltpu.VMEM((SLOTS, rows), jnp.bfloat16),
                pltpu.VMEM((SLOTS, rows), jnp.bfloat16),
                pltpu.VMEM((GROUP * HALVES * LINES, TILE), jnp.float32),
                pltpu.VMEM((n * chunks,) + piece, jnp.float32),
                pltpu.VMEM(((n - 1) * chunks,) + piece, jnp.float32),
                pltpu.VMEM((n, NODES, LANES), jnp.float32),
                pltpu.VMEM((m, NODES, LANES), jnp.float32),
                pltpu.SemaphoreType.DMA((2,)),
                pltpu.SemaphoreType.DMA(((n - 1) * chunks,)),
                pltpu.SemaphoreType.DMA(((n - 1) * chunks,)),
                pltpu.SemaphoreType.DMA((n - 1,)),
                pltpu.SemaphoreType.DMA((n - 1,)),
                pltpu.SemaphoreType.DMA((m - 1,)),
                pltpu.SemaphoreType.DMA((m - 1,)),
            ],
            compiler_params=pltpu.CompilerParams(
                collective_id=0, has_side_effects=True, vmem_limit_bytes=56 << 20
            ),
        )(bins, node.reshape(1, rows), grads.reshape(-1, LANES), hess.reshape(-1, LANES))
        best = best.reshape(NODES)
        return out - best[None, :, None], best

    return jax.shard_map(
        per_device,
        mesh=mesh,
        in_specs=(P("feat", "row"), P("row"), P("row"), P("row")),
        out_specs=(P(("feat", "row"), None, None), P()),
        check_vma=False,
    )
```

```python
import functools
import jax
import jax.numpy as jnp
from jax import lax
from jax.experimental import pallas as pl
from jax.experimental.pallas import tpu as pltpu
from jax.sharding import PartitionSpec as P

BINS = 256
NODES = 8
LANES = 128
SUBLANES = 8
LOW = 64
TILE = 256
GROUP = TILE // LOW
HALVES = LANES // LOW
TOPS = BINS // LANES
SLOTS = NODES * TOPS
LINES = 2 * SLOTS
MESH = pl.DeviceIdType.MESH
F8 = jnp.float8_e4m3fn
SLOT = 256
PACK = 4
CHUNK = 8
DIGIT = 32


def partner(me, k, n):
    if n & (n - 1):
        return (me + k) % n
    out, weight = 0, 1
    while weight < n:
        out = out + (((me // weight) % 2 + (k // weight) % 2) % 2) * weight
        weight *= 2
    return out


def direct(
    n, m, block, chunks, bins_hbm, node_ref, g_ref, h_ref, out_ref, best_ref,
    bins_buf, high_ref, low_ref, g_all, h_all, acc_ref, stage, landed, row_best, feat_best,
    load_sem, send_sem, recv_sem, row_send, row_recv, feat_send, feat_recv,
):
    rows = bins_buf.shape[2]
    me = lax.axis_index("row")
    mine = lax.axis_index("feat")
    steps = n * chunks
    sent = (n - 1) * chunks

    def place_of(s):
        return (partner(me, n - 1 - s // chunks, n) * chunks + s % chunks) * block

    def load(s):
        start = pl.multiple_of((place_of(s) // SUBLANES) * SUBLANES, SUBLANES)
        return pltpu.make_async_copy(
            bins_hbm.at[pl.ds(start, bins_buf.shape[1]), :], bins_buf.at[s % 2], load_sem.at[s % 2]
        )

    def send(s):
        k = n - 1 - s // chunks
        return pltpu.make_async_remote_copy(
            src_ref=stage.at[s],
            dst_ref=landed.at[s],
            send_sem=send_sem.at[s],
            recv_sem=recv_sem.at[s],
            device_id={"row": partner(me, k, n)},
            device_id_type=MESH,
        )

    load(0).start()
    barrier = pltpu.get_barrier_semaphore()
    for k in range(1, n):
        pl.semaphore_signal(barrier, inc=1, device_id={"row": (me + k) % n}, device_id_type=MESH)
    for k in range(1, m):
        pl.semaphore_signal(barrier, inc=1, device_id={"feat": (mine + k) % m}, device_id_type=MESH)

    g = g_ref[...].astype(jnp.float32)
    h = h_ref[...].astype(jnp.float32)
    for i in range(rows // LANES):
        cols = slice(i * LANES, (i + 1) * LANES)
        g_all[:, cols] = jnp.broadcast_to(g[i : i + 1, :], (SLOTS, LANES)).astype(jnp.bfloat16)
        h_all[:, cols] = jnp.broadcast_to(h[i : i + 1, :], (SLOTS, LANES)).astype(jnp.bfloat16)
    pl.semaphore_wait(barrier, n + m - 2)

    def step(s, carry):
        load(s).wait()

        @pl.when(s + 1 < steps)
        def _():
            load(s + 1).start()

        @pl.when((s >= 1) & (s <= sent))
        def _():
            send(s - 1).start()

        offset = 0 if block % SUBLANES == 0 else place_of(s) % SUBLANES
        bins = bins_buf[s % 2]
        upper = bins >= LANES
        rest = jnp.where(upper, bins - LANES, bins)
        second = rest >= LOW
        slot = node_ref[...] + jnp.where(upper, NODES, 0)
        high_ref[...] = jnp.where(second, slot + SLOTS, slot).astype(jnp.float32)
        low_ref[...] = jnp.where(second, rest - LOW, rest).astype(jnp.float32)
        place = lax.broadcasted_iota(jnp.int32, (SLOTS, rows), 0).astype(jnp.bfloat16)
        zero = jnp.zeros((SLOTS, rows), jnp.bfloat16)
        one = jnp.ones((SLOTS, rows), jnp.bfloat16)
        for first in range(0, block, GROUP):
            left, right = [], []
            for f in range(first, first + GROUP):
                row = pl.ds(offset + f, 1)
                high = jnp.broadcast_to(high_ref[row, :], (SLOTS, rows)).astype(jnp.bfloat16)
                low = jnp.broadcast_to(low_ref[row, :], (SLOTS, rows)).astype(jnp.bfloat16)
                for j in range(HALVES):
                    here = high == place + jnp.asarray(SLOTS * j, jnp.bfloat16)
                    left += [jnp.where(here, g_all[...], zero), jnp.where(here, h_all[...], zero)]
                for j in range(LOW // SLOTS):
                    here = low == place + jnp.asarray(SLOTS * j, jnp.bfloat16)
                    right.append(jnp.where(here, one, zero))
            acc_ref[...] = lax.dot_general(
                jnp.concatenate(left, 0),
                jnp.concatenate(right, 0),
                (((1,), (1,)), ((), ())),
                preferred_element_type=jnp.float32,
            )
            for i in range(GROUP):
                parts = []
                for j in range(HALVES):
                    top = (i * HALVES + j) * LINES
                    parts.append(acc_ref[top : top + LINES, i * LOW : (i + 1) * LOW])
                stage[s, first + i] = jnp.concatenate(parts, 1)
        return carry

    lax.fori_loop(0, steps, step, 0)

    def drain(s, carry):
        send(s).wait()
        return carry

    lax.fori_loop(0, sent, drain, 0)

    lane = lax.broadcasted_iota(jnp.int32, (block * 2 * TOPS * NODES, LANES), 1)

    def finish(c, top_gain):
        def add(k, total):
            return total + landed[k * chunks + c]

        x = lax.fori_loop(0, n - 1, add, stage[sent + c])
        x = x.reshape(block * LINES, LANES)
        shift = 1
        while shift < LANES:
            x = x + jnp.where(lane >= shift, pltpu.roll(x, shift, 1), 0.0)
            shift *= 2
        x = x.reshape(block, 2, TOPS, NODES, LANES)
        left, total = [], jnp.zeros((block, 2, NODES, LANES), jnp.float32)
        for t in range(TOPS):
            left.append(x[:, :, t] + total)
            total = total + jnp.broadcast_to(x[:, :, t, :, LANES - 1 :], total.shape)
        gt, ht = total[:, 0], total[:, 1]
        base = gt * gt / (ht + 1.0)
        for t in range(TOPS):
            gl, hl = left[t][:, 0], left[t][:, 1]
            gain = gl * gl / (hl + 1.0)
            gain = gain + (gt - gl) * (gt - gl) / (ht - hl + 1.0)
            gain = gain - base
            out_ref[pl.ds(c * block, block), :, t * LANES : (t + 1) * LANES] = gain
            top_gain = jnp.maximum(top_gain, jnp.max(gain, axis=0))
        return top_gain

    top_gain = lax.fori_loop(0, chunks, finish, jnp.full((NODES, LANES), -jnp.inf, jnp.float32))

    def exchange(value, slots, count, axis, index, sems, arrived):
        slots[0] = jnp.broadcast_to(jnp.max(value, axis=1, keepdims=True), (NODES, LANES))
        copies = []
        for k in range(1, count):
            copies.append(
                pltpu.make_async_remote_copy(
                    src_ref=slots.at[0],
                    dst_ref=slots.at[k],
                    send_sem=sems.at[k - 1],
                    recv_sem=arrived.at[k - 1],
                    device_id={axis: (index + k) % count},
                    device_id_type=MESH,
                )
            )
            copies[-1].start()
        for copy in copies:
            copy.wait()
        best = slots[0]
        for k in range(1, count):
            best = jnp.maximum(best, slots[k])
        return best

    best = exchange(top_gain, row_best, n, "row", me, row_send, row_recv)
    best = exchange(best, feat_best, m, "feat", mine, feat_send, feat_recv)
    across = lax.broadcasted_iota(jnp.int32, (NODES, LANES), 1)
    down = lax.broadcasted_iota(jnp.int32, (NODES, LANES), 0)
    flat = jnp.max(jnp.where(across == down, best, -jnp.inf), axis=0, keepdims=True)
    best_ref[...] = flat[:, :NODES]


def take(x, index):
    return jnp.take_along_axis(x, index, axis=1, mode="promise_in_bounds")


def regroup(
    bins_hbm, node_ref, g_ref, h_ref, words_ref, gh_ref, keep_ref, last_ref,
    bins, pieces, pattern, spots_v, spots_s, load_sem, spots_sem,
):
    f32, bf16, i32 = jnp.float32, jnp.bfloat16, jnp.int32
    tiles = node_ref.shape[0]
    groups = bins.shape[0] // 32
    chunks = tiles // CHUNK

    def load(c):
        cols = pl.ds(pl.multiple_of(c * (CHUNK * LANES), CHUNK * LANES), CHUNK * LANES)
        return pltpu.make_async_copy(bins_hbm.at[:, cols], bins.at[:, cols], load_sem.at[c])

    for c in range(chunks):
        load(c).start()
    node = node_ref[...]
    pieces[0] = g_ref[...].astype(f32)
    pieces[1] = h_ref[...].astype(f32)
    row = lax.broadcasted_iota(i32, (LANES, LANES), 0)
    col = lax.broadcasted_iota(i32, (LANES, LANES), 1)
    upper = jnp.where(row <= col, 1.0, 0.0).astype(bf16)
    ones = jnp.ones((LANES, LANES), bf16)
    above = lax.broadcasted_iota(i32, (tiles, tiles), 1) < lax.broadcasted_iota(i32, (tiles, tiles), 0)
    lower = jnp.where(above, 1.0, 0.0).astype(bf16)
    dot = functools.partial(jnp.dot, preferred_element_type=f32)
    lane = lax.broadcasted_iota(i32, (tiles, LANES), 1)
    slot = lax.broadcasted_iota(i32, keep_ref.shape, 0)
    keep = jnp.ones(keep_ref.shape, f32)
    base = jnp.zeros((1, LANES), i32)
    last = jnp.zeros((1, LANES), i32)
    dest = jnp.zeros((tiles, LANES), i32)
    spots = jnp.zeros((tiles, LANES), i32)
    for n in range(NODES):
        hit = node == n
        x = jnp.where(hit, 1.0, 0.0).astype(bf16)
        rank = dot(x, upper).astype(i32)
        count = dot(x, ones)
        ahead = dot(lower, count.astype(bf16)).astype(i32)
        count = count.astype(i32)
        total = (ahead + count)[tiles - 1 : tiles]
        start = ahead + base
        dest = jnp.where(hit, start + rank - 1, dest)
        spots = jnp.where(lane == n, start, jnp.where(lane == NODES + n, start + count, spots))
        keep = jnp.where(slot * SLOT == base, 0.0, keep)
        base = base + jnp.maximum((total + (SLOT - 1)) // SLOT, 1) * SLOT
        last = jnp.where(lane[:1] == n, base // SLOT - 1, last)
    keep_ref[...] = keep
    last_ref[...] = last
    spots_v[...] = spots
    to_scalar = pltpu.make_async_copy(spots_v, spots_s, spots_sem)
    to_scalar.start()

    spot = dest & (LANES - 1)
    sub = lax.broadcasted_iota(i32, (NODES, LANES), 0)
    across = lax.broadcasted_iota(i32, (NODES, LANES), 1)
    none = jnp.zeros((NODES, LANES), i32)
    for b in range(0, tiles, 2):
        left, right = [], []
        for i in range(2):
            here = jnp.where(jnp.broadcast_to(node[b + i : b + i + 1], (NODES, LANES)) == sub, across, 0)
            left.append(jnp.concatenate([none] * i + [here] + [none] * (1 - i), 1))
            right.append(jnp.where(jnp.broadcast_to(spot[b + i : b + i + 1], (LANES, LANES)) == row, 1.0, 0.0))
        found = lax.dot_general(
            jnp.concatenate(left, 0).astype(f32).astype(bf16),
            jnp.concatenate(right, 1).astype(bf16),
            (((1,), (1,)), ((), ())),
            preferred_element_type=f32,
        ).astype(i32)
        pattern[b] = found[:NODES]
        pattern[b + 1] = found[NODES:]
    gh_ref[...] = jnp.zeros(gh_ref.shape, f32)
    to_scalar.wait()

    def place(b):
        cols = pl.ds(pl.multiple_of(b * LANES, LANES), LANES)
        words = []
        for t in range(groups):
            word = bins[32 * t : 32 * t + SUBLANES, cols]
            for k in range(1, PACK):
                word = word | lax.shift_left(bins[32 * t + SUBLANES * k : 32 * t + SUBLANES * (k + 1), cols], 8 * k)
            words.append(word)
        for t in range(0, groups, 2):
            one, two = words[t], words[t + 1]
            words[t], words[t + 1] = jnp.where(sub < 4, one, two), jnp.where(sub < 4, two, one)
        piece = [jnp.broadcast_to(pieces[i, pl.ds(b, 1), :], (SUBLANES, LANES)) for i in range(2)]
        gh = jnp.where(sub == 0, piece[0], piece[1])
        for n in range(NODES):
            first = spots_s[b, n]
            tile = lax.shift_right_logical(first, 7)
            low = first & (LANES - 1)
            high = low + spots_s[b, NODES + n] - first
            source = jnp.broadcast_to(pattern[b, n : n + 1, :], (SUBLANES, LANES))
            near = (across >= low) & (across < high)
            far = across < high - LANES
            for t in range(groups):
                moved = take(words[t], source)
                pltpu.store(words_ref.at[tile, t], moved, mask=near)
                pltpu.store(words_ref.at[tile + 1, t], moved, mask=far)
            moved = take(gh, source)
            pltpu.store(gh_ref.at[tile], moved, mask=near)
            pltpu.store(gh_ref.at[tile + 1], moved, mask=far)

    def chunk(c, carry):
        load(c).wait()
        for j in range(CHUNK):
            place(c * CHUNK + j)
        return carry

    lax.fori_loop(0, chunks, chunk, 0)


def sweep(
    n, m, words_hbm, gh_ref, keep_ref, last_ref, out_ref, best_ref,
    words, keys, gh, snap, stage, near, relay, far, row_best, feat_best,
    load_sem, near_send, near_recv, far_send, far_recv, row_send, row_recv, feat_send, feat_recv,
):
    f32 = jnp.float32
    tiles = words.shape[1]
    slots = tiles * LANES // SLOT
    pairs = n // 2
    order = ((0, 0), (0, 1), (2, 0), (1, 1), (1, 0), (2, 1), (3, 0), (3, 1))
    route = (2, 1, 2, 1, 1, 2, 3, 3)
    steps, away = 2 * pairs, 2 * (pairs - 1)
    me = lax.axis_index("row")
    mine = lax.axis_index("feat")
    chip, core = me // 2, me % 2

    def pick(u, table):
        value = table[0]
        for i in range(1, steps):
            value = jnp.where(u >= i, table[i], value)
        return value

    def half_of(u):
        return pick(u, [h for _, h in order])

    def chip_at(k):
        return partner(chip, pairs - 1 - k, pairs)

    def load(u, e):
        tile = 2 * chip_at(pick(u, [k for k, _ in order])) + half_of(u)
        return pltpu.make_async_copy(words_hbm.at[pl.ds(0, tiles), tile], words.at[e], load_sem.at[e])

    def send_near(u):
        return pltpu.make_async_remote_copy(
            src_ref=stage.at[u],
            dst_ref=near.at[u],
            send_sem=near_send.at[u],
            recv_sem=near_recv.at[u],
            device_id={"row": 2 * chip + 1 - core},
            device_id_type=MESH,
        )

    def send_far(u):
        return pltpu.make_async_remote_copy(
            src_ref=relay.at[u],
            dst_ref=far.at[u],
            send_sem=far_send.at[u],
            recv_sem=far_recv.at[u],
            device_id={"row": 2 * chip_at(pick(u, route)) + core},
            device_id_type=MESH,
        )

    load(0, 0).start()
    load(1, 1).start()
    barrier = pltpu.get_barrier_semaphore()
    for k in range(1, n):
        pl.semaphore_signal(barrier, inc=1, device_id={"row": (me + k) % n}, device_id_type=MESH)
    for k in range(1, m):
        pl.semaphore_signal(barrier, inc=1, device_id={"feat": (mine + k) % m}, device_id_type=MESH)
    for p in range(2):
        for q in range(tiles):
            gh[p, :, q * LANES : (q + 1) * LANES] = jnp.broadcast_to(gh_ref[q, p : p + 1, :], (16, LANES)).astype(jnp.bfloat16)
    pl.semaphore_wait(barrier, n + m - 2)

    wide = (32, SLOT)
    down = lax.broadcasted_iota(jnp.int32, wide, 0) % SUBLANES
    high_at = (down[:16] * DIGIT).astype(jnp.int16)
    low_at = [(down + SUBLANES * j).astype(jnp.int8) for j in range(4)]
    zero, one = jnp.zeros(wide, F8), jnp.ones(wide, F8)
    nil = jnp.zeros((16, SLOT), jnp.bfloat16)
    lane = lax.broadcasted_iota(jnp.int32, (SUBLANES, LANES), 1)
    sub = lax.broadcasted_iota(jnp.int32, (SUBLANES, LANES), 0)
    byte = (lane // SUBLANES) % PACK
    of = [byte == f for f in range(PACK - 1)]

    def unpack(e, q):
        for k in range(PACK):
            keys[e, k, :, q * LANES : (q + 1) * LANES] = lax.shift_right_logical(words[e, q], 8 * k)

    def one_hots(e, w, cols):
        rows = [jnp.broadcast_to(keys[e, k, pl.ds(w, 1), cols], (SUBLANES, SLOT)) for k in range(PACK)]
        twos = [jnp.concatenate(rows[i : i + 2], 0).astype(jnp.int16) for i in (0, 2)]
        low = jnp.concatenate(rows, 0).astype(jnp.int8) & jnp.int8(DIGIT - 1)
        left = []
        for two in twos:
            apart = (two & jnp.int16(BINS - DIGIT)) != high_at
            left += [jnp.where(apart, nil, gh[v, :, cols]) for v in range(2)]
        right = [jnp.where(low != low_at[j], zero, one) for j in range(4)]
        return left, right

    def block(e, w, side, hook):
        total = [jnp.zeros((SUBLANES, LANES), f32) for _ in range(4)]
        for s in range(slots):
            cols = slice(s * SLOT, (s + 1) * SLOT)
            left0, right0 = one_hots(e, w, cols)
            left1, right1 = one_hots(e, w + 1, cols)
            found = lax.dot_general(
                jnp.concatenate(left0 + left1, 0),
                jnp.concatenate(right0 + right1, 0),
                (((1,), (1,)), ((), ())),
                preferred_element_type=f32,
            )
            kept = jnp.broadcast_to(keep_ref[s : s + 1, :], (SUBLANES, LANES))
            for q in range(2):
                square = found[64 * q : 64 * (q + 1), q * LANES : (q + 1) * LANES]
                for v in range(2):
                    piece = [square[at : at + SUBLANES] for at in (16 * v, 16 * v + 8, 16 * v + 32, 16 * v + 40)]
                    dense = jnp.where(of[0], piece[0], jnp.where(of[1], piece[1], jnp.where(of[2], piece[2], piece[3])))
                    at = 2 * q + v
                    total[at] = total[at] * kept + dense
                    snap[side, s, at] = total[at]
            hook(s)

    def store(ref, u, b, side):
        for node in range(NODES):
            for at in range(4):
                ref[u, b, node, at] = snap[side, last_ref[0, node], at]

    def merge(u, ref, v):
        for b in range(2):
            for node in range(NODES):
                for at in range(4):
                    relay[u, b, node, at] += ref[v, b, node, at]

    middle = min(6, slots - 1)
    load(0, 0).wait()
    for q in range(tiles):
        unpack(0, q)

    def step(u, e):
        @pl.when(u >= 1)
        def _():
            store(relay, u - 1, 1, 1)
            send_near(u - 1).wait_recv()
            merge(u - 1, near, u - 1)

        @pl.when((u >= away - 1) & (u < steps - 1))
        def _():
            send_far(u - away + 1).wait_recv()
            merge(u - 1, far, u - away + 1)

        @pl.when(u < steps - 1)
        def _():
            load(u + 1, 1 - e).wait()

        @pl.when(u < steps - 2)
        def _():
            load(u + 2, e).start()

        @pl.when((u >= 1) & (u <= away))
        def _():
            send_far(u - 1).start()

        half = half_of(u)
        give = 4 * ((1 - core + half) % 2)
        hold = 4 * ((core + half) % 2)

        def at_middle(*args):
            def hook(s):
                if s == middle:
                    store(*args)

            return hook

        def third(s):
            if s == middle:
                store(stage, u, 1, 1)
            if s == slots // 2:
                send_near(u).start()
            for q in range(2 * s, 2 * s + 2):
                unpack(1 - e, q)

        block(e, give, 0, lambda s: None)
        block(e, give + 2, 1, at_middle(stage, u, 0, 0))
        block(e, hold, 0, third)
        block(e, hold + 2, 1, at_middle(relay, u, 0, 0))

    def both(i, carry):
        step(2 * i, 0)
        step(2 * i + 1, 1)
        return carry

    lax.fori_loop(0, pairs, both, 0)
    store(relay, steps - 1, 1, 1)
    send_near(steps - 1).wait_recv()
    merge(steps - 1, near, steps - 1)

    tens, units = lane // (SUBLANES * PACK), lane % SUBLANES
    end_of_run = lane - units + (SUBLANES - 1)
    end_of_row = (LANES - DIGIT) + byte * SUBLANES + (SUBLANES - 1)

    def running(x):
        for shift in (1, 2, 4):
            x = x + jnp.where(units >= shift, pltpu.roll(x, shift, 1), 0.0)
        run = take(x, end_of_run)
        for j in range(1, 4):
            x = x + jnp.where(tens >= j, pltpu.roll(run, j * DIGIT, 1), 0.0)
        row = take(x, end_of_row)
        whole = row
        for shift in (1, 2, 4):
            whole = whole + jnp.where(sub >= shift, pltpu.roll(whole, shift, 0), 0.0)
        return x + (whole - row), jnp.broadcast_to(whole[SUBLANES - 1 :], whole.shape)

    def gains(h, best):
        u = steps - 2 + h
        sources = [v for v in range(2, away) if order[v][1] == h]
        for v in sources:
            send_far(v).wait_recv()

        def one_block(b, best):
            tops = []
            for node in range(NODES):
                for q in range(2):
                    sums = []
                    for at in (2 * q, 2 * q + 1):
                        x = relay[u, b, node, at]
                        for v in sources:
                            x = x + far[v, b, node, at]
                        sums.append(running(x))
                    (gl, gt), (hl, ht) = sums
                    gain = gl * gl / (hl + 1.0)
                    gain = gain + (gt - gl) * (gt - gl) / (ht - hl + 1.0)
                    gain = gain - gt * gt / (ht + 1.0)
                    relay[u, b, node, 2 * q] = gain
                    top = gain if q == 0 else jnp.maximum(top, gain)
                tops.append(jnp.max(top, axis=0))
            return jnp.maximum(best, jnp.stack(tops, 0))

        return lax.fori_loop(0, 2, one_block, best)

    def layout(h):
        u = steps - 2 + h

        def one_block(b, carry):
            for q in range(2):
                turned = jnp.swapaxes(jnp.stack([relay[u, b, node, 2 * q] for node in range(NODES)], 0), 0, 1)
                for f in range(PACK):
                    source = ((lane // SUBLANES) % 4) * DIGIT + f * SUBLANES + units
                    for t in range(TOPS):
                        piece = [take(turned[4 * t + j], source) for j in range(4)]
                        line = jnp.where(tens == 0, piece[0], jnp.where(tens == 1, piece[1], jnp.where(tens == 2, piece[2], piece[3])))
                        feature = SUBLANES * f + 4 * ((core + h) % 2) + 2 * b + q
                        out_ref[feature, :, t * LANES : (t + 1) * LANES] = line
            return carry

        lax.fori_loop(0, 2, one_block, 0)

    def exchange(value, parts, count, axis, index, sems, arrived, during):
        parts[0] = jnp.broadcast_to(jnp.max(value, axis=1, keepdims=True), (NODES, LANES))
        copies = []
        for k in range(1, count):
            copies.append(
                pltpu.make_async_remote_copy(
                    src_ref=parts.at[0],
                    dst_ref=parts.at[k],
                    send_sem=sems.at[k - 1],
                    recv_sem=arrived.at[k - 1],
                    device_id={axis: (index + k) % count},
                    device_id_type=MESH,
                )
            )
            copies[-1].start()
        during()
        for copy in copies:
            copy.wait()
        best = parts[0]
        for k in range(1, count):
            best = jnp.maximum(best, parts[k])
        return best

    top_gain = jnp.full((NODES, LANES), -jnp.inf, f32)
    for h in range(2):
        top_gain = gains(h, top_gain)
    best = exchange(top_gain, row_best, n, "row", me, row_send, row_recv, lambda: layout(0))
    best = exchange(best, feat_best, m, "feat", mine, feat_send, feat_recv, lambda: layout(1))
    flat = jnp.max(jnp.where(lane == sub, best, -jnp.inf), axis=0, keepdims=True)
    best_ref[...] = flat[:, :NODES]
    for u in range(steps):
        send_near(u).wait_send()
        if u < away:
            send_far(u).wait_send()


def grouped(n, m, bins, grads, hess, node):
    features, rows = bins.shape
    groups, tiles = features // 32, rows // LANES
    slots = rows // SLOT + NODES - 1
    held = 2 * slots
    vmem = pl.BlockSpec(memory_space=pltpu.VMEM)
    smem = pl.BlockSpec(memory_space=pltpu.SMEM)
    hbm = pl.BlockSpec(memory_space=pl.ANY)
    words, gh, keep, last = pl.pallas_call(
        regroup,
        in_specs=[hbm, vmem, vmem, vmem],
        out_specs=(vmem, vmem, vmem, vmem),
        out_shape=(
            jax.ShapeDtypeStruct((held + 1, groups, SUBLANES, LANES), jnp.int32),
            jax.ShapeDtypeStruct((held + 1, SUBLANES, LANES), jnp.float32),
            jax.ShapeDtypeStruct((-(-slots // SUBLANES) * SUBLANES, LANES), jnp.float32),
            jax.ShapeDtypeStruct((1, LANES), jnp.int32),
        ),
        scratch_shapes=[
            pltpu.VMEM((features, rows), jnp.int32),
            pltpu.VMEM((2, tiles, LANES), jnp.float32),
            pltpu.VMEM((tiles, NODES, LANES), jnp.int32),
            pltpu.VMEM((tiles, LANES), jnp.int32),
            pltpu.SMEM((tiles, LANES), jnp.int32),
            pltpu.SemaphoreType.DMA((tiles // CHUNK,)),
            pltpu.SemaphoreType.DMA,
        ],
        compiler_params=pltpu.CompilerParams(vmem_limit_bytes=56 << 20),
    )(bins, node.reshape(-1, LANES), grads.reshape(-1, LANES), hess.reshape(-1, LANES))
    pairs = n // 2
    piece = (2, NODES, 4, SUBLANES, LANES)
    steps, away = 2 * pairs, 2 * (pairs - 1)
    out, best = pl.pallas_call(
        functools.partial(sweep, n, m),
        in_specs=[hbm, vmem, vmem, smem],
        out_specs=(vmem, vmem),
        out_shape=(
            jax.ShapeDtypeStruct((32, NODES, BINS), jnp.float32),
            jax.ShapeDtypeStruct((1, NODES), jnp.float32),
        ),
        scratch_shapes=[
            pltpu.VMEM((2, held, SUBLANES, LANES), jnp.int32),
            pltpu.VMEM((2, PACK, SUBLANES, held * LANES), jnp.int32),
            pltpu.VMEM((2, 16, held * LANES), jnp.bfloat16),
            pltpu.VMEM((2, slots, 4, SUBLANES, LANES), jnp.float32),
            pltpu.VMEM((steps,) + piece, jnp.float32),
            pltpu.VMEM((steps,) + piece, jnp.float32),
            pltpu.VMEM((steps,) + piece, jnp.float32),
            pltpu.VMEM((away,) + piece, jnp.float32),
            pltpu.VMEM((n, NODES, LANES), jnp.float32),
            pltpu.VMEM((m, NODES, LANES), jnp.float32),
            pltpu.SemaphoreType.DMA((2,)),
            pltpu.SemaphoreType.DMA((steps,)),
            pltpu.SemaphoreType.DMA((steps,)),
            pltpu.SemaphoreType.DMA((away,)),
            pltpu.SemaphoreType.DMA((away,)),
            pltpu.SemaphoreType.DMA((n - 1,)),
            pltpu.SemaphoreType.DMA((n - 1,)),
            pltpu.SemaphoreType.DMA((m - 1,)),
            pltpu.SemaphoreType.DMA((m - 1,)),
        ],
        compiler_params=pltpu.CompilerParams(
            collective_id=0, has_side_effects=True, vmem_limit_bytes=56 << 20
        ),
    )(words, gh, keep, last)
    best = best.reshape(NODES)
    return out - best[None, :, None], best


def solution(mesh):
    n, m = mesh.shape["row"], mesh.shape["feat"]

    def per_device(bins, grads, hess, node):
        features, rows = bins.shape
        own = features // n
        if own == 32 and n == 8 and rows % (CHUNK * LANES) == 0:
            return grouped(n, m, bins, grads, hess, node)
        block = own if own < SUBLANES else next(b for b in (2 * SUBLANES, SUBLANES) if own % b == 0)
        held = max(block, SUBLANES)
        chunks = own // block
        vmem = pl.BlockSpec(memory_space=pltpu.VMEM)
        piece = (block, LINES, LANES)
        out, best = pl.pallas_call(
            functools.partial(direct, n, m, block, chunks),
            in_specs=[pl.BlockSpec(memory_space=pl.ANY), vmem, vmem, vmem],
            out_specs=(vmem, vmem),
            out_shape=(
                jax.ShapeDtypeStruct((own, NODES, BINS), jnp.float32),
                jax.ShapeDtypeStruct((1, NODES), jnp.float32),
            ),
            scratch_shapes=[
                pltpu.VMEM((2, held, rows), jnp.int32),
                pltpu.VMEM((held, rows), jnp.float32),
                pltpu.VMEM((held, rows), jnp.float32),
                pltpu.VMEM((SLOTS, rows), jnp.bfloat16),
                pltpu.VMEM((SLOTS, rows), jnp.bfloat16),
                pltpu.VMEM((GROUP * HALVES * LINES, TILE), jnp.float32),
                pltpu.VMEM((n * chunks,) + piece, jnp.float32),
                pltpu.VMEM(((n - 1) * chunks,) + piece, jnp.float32),
                pltpu.VMEM((n, NODES, LANES), jnp.float32),
                pltpu.VMEM((m, NODES, LANES), jnp.float32),
                pltpu.SemaphoreType.DMA((2,)),
                pltpu.SemaphoreType.DMA(((n - 1) * chunks,)),
                pltpu.SemaphoreType.DMA(((n - 1) * chunks,)),
                pltpu.SemaphoreType.DMA((n - 1,)),
                pltpu.SemaphoreType.DMA((n - 1,)),
                pltpu.SemaphoreType.DMA((m - 1,)),
                pltpu.SemaphoreType.DMA((m - 1,)),
            ],
            compiler_params=pltpu.CompilerParams(
                collective_id=0, has_side_effects=True, vmem_limit_bytes=56 << 20
            ),
        )(bins, node.reshape(1, rows), grads.reshape(-1, LANES), hess.reshape(-1, LANES))
        best = best.reshape(NODES)
        return out - best[None, :, None], best

    return jax.shard_map(
        per_device,
        mesh=mesh,
        in_specs=(P("feat", "row"), P("row"), P("row"), P("row")),
        out_specs=(P(("feat", "row"), None, None), P()),
        check_vma=False,
    )
```

```python
import functools
import jax
import jax.numpy as jnp
from jax import lax
from jax.experimental import pallas as pl
from jax.experimental.pallas import tpu as pltpu
from jax.sharding import PartitionSpec as P

BINS = 256
NODES = 8
LANES = 128
SUBLANES = 8
LOW = 64
TILE = 256
GROUP = TILE // LOW
HALVES = LANES // LOW
TOPS = BINS // LANES
SLOTS = NODES * TOPS
LINES = 2 * SLOTS
MESH = pl.DeviceIdType.MESH
F8 = jnp.float8_e4m3fn
SLOT = 256
PACK = 4
CHUNK = 8
DIGIT = 32


def partner(me, k, n):
    if n & (n - 1):
        return (me + k) % n
    out, weight = 0, 1
    while weight < n:
        out = out + (((me // weight) % 2 + (k // weight) % 2) % 2) * weight
        weight *= 2
    return out


def direct(
    n, m, block, chunks, bins_hbm, node_ref, g_ref, h_ref, out_ref, best_ref,
    bins_buf, high_ref, low_ref, g_all, h_all, acc_ref, stage, landed, row_best, feat_best,
    load_sem, send_sem, recv_sem, row_send, row_recv, feat_send, feat_recv,
):
    rows = bins_buf.shape[2]
    me = lax.axis_index("row")
    mine = lax.axis_index("feat")
    steps = n * chunks
    sent = (n - 1) * chunks

    def place_of(s):
        return (partner(me, n - 1 - s // chunks, n) * chunks + s % chunks) * block

    def load(s):
        start = pl.multiple_of((place_of(s) // SUBLANES) * SUBLANES, SUBLANES)
        return pltpu.make_async_copy(
            bins_hbm.at[pl.ds(start, bins_buf.shape[1]), :], bins_buf.at[s % 2], load_sem.at[s % 2]
        )

    def send(s):
        k = n - 1 - s // chunks
        return pltpu.make_async_remote_copy(
            src_ref=stage.at[s],
            dst_ref=landed.at[s],
            send_sem=send_sem.at[s],
            recv_sem=recv_sem.at[s],
            device_id={"row": partner(me, k, n)},
            device_id_type=MESH,
        )

    load(0).start()
    barrier = pltpu.get_barrier_semaphore()
    for k in range(1, n):
        pl.semaphore_signal(barrier, inc=1, device_id={"row": (me + k) % n}, device_id_type=MESH)
    for k in range(1, m):
        pl.semaphore_signal(barrier, inc=1, device_id={"feat": (mine + k) % m}, device_id_type=MESH)

    g = g_ref[...].astype(jnp.float32)
    h = h_ref[...].astype(jnp.float32)
    for i in range(rows // LANES):
        cols = slice(i * LANES, (i + 1) * LANES)
        g_all[:, cols] = jnp.broadcast_to(g[i : i + 1, :], (SLOTS, LANES)).astype(jnp.bfloat16)
        h_all[:, cols] = jnp.broadcast_to(h[i : i + 1, :], (SLOTS, LANES)).astype(jnp.bfloat16)
    pl.semaphore_wait(barrier, n + m - 2)

    def step(s, carry):
        load(s).wait()

        @pl.when(s + 1 < steps)
        def _():
            load(s + 1).start()

        @pl.when((s >= 1) & (s <= sent))
        def _():
            send(s - 1).start()

        offset = 0 if block % SUBLANES == 0 else place_of(s) % SUBLANES
        bins = bins_buf[s % 2]
        upper = bins >= LANES
        rest = jnp.where(upper, bins - LANES, bins)
        second = rest >= LOW
        slot = node_ref[...] + jnp.where(upper, NODES, 0)
        high_ref[...] = jnp.where(second, slot + SLOTS, slot).astype(jnp.float32)
        low_ref[...] = jnp.where(second, rest - LOW, rest).astype(jnp.float32)
        place = lax.broadcasted_iota(jnp.int32, (SLOTS, rows), 0).astype(jnp.bfloat16)
        zero = jnp.zeros((SLOTS, rows), jnp.bfloat16)
        one = jnp.ones((SLOTS, rows), jnp.bfloat16)
        for first in range(0, block, GROUP):
            left, right = [], []
            for f in range(first, first + GROUP):
                row = pl.ds(offset + f, 1)
                high = jnp.broadcast_to(high_ref[row, :], (SLOTS, rows)).astype(jnp.bfloat16)
                low = jnp.broadcast_to(low_ref[row, :], (SLOTS, rows)).astype(jnp.bfloat16)
                for j in range(HALVES):
                    here = high == place + jnp.asarray(SLOTS * j, jnp.bfloat16)
                    left += [jnp.where(here, g_all[...], zero), jnp.where(here, h_all[...], zero)]
                for j in range(LOW // SLOTS):
                    here = low == place + jnp.asarray(SLOTS * j, jnp.bfloat16)
                    right.append(jnp.where(here, one, zero))
            acc_ref[...] = lax.dot_general(
                jnp.concatenate(left, 0),
                jnp.concatenate(right, 0),
                (((1,), (1,)), ((), ())),
                preferred_element_type=jnp.float32,
            )
            for i in range(GROUP):
                parts = []
                for j in range(HALVES):
                    top = (i * HALVES + j) * LINES
                    parts.append(acc_ref[top : top + LINES, i * LOW : (i + 1) * LOW])
                stage[s, first + i] = jnp.concatenate(parts, 1)
        return carry

    lax.fori_loop(0, steps, step, 0)

    def drain(s, carry):
        send(s).wait()
        return carry

    lax.fori_loop(0, sent, drain, 0)

    lane = lax.broadcasted_iota(jnp.int32, (block * 2 * TOPS * NODES, LANES), 1)

    def finish(c, top_gain):
        def add(k, total):
            return total + landed[k * chunks + c]

        x = lax.fori_loop(0, n - 1, add, stage[sent + c])
        x = x.reshape(block * LINES, LANES)
        shift = 1
        while shift < LANES:
            x = x + jnp.where(lane >= shift, pltpu.roll(x, shift, 1), 0.0)
            shift *= 2
        x = x.reshape(block, 2, TOPS, NODES, LANES)
        left, total = [], jnp.zeros((block, 2, NODES, LANES), jnp.float32)
        for t in range(TOPS):
            left.append(x[:, :, t] + total)
            total = total + jnp.broadcast_to(x[:, :, t, :, LANES - 1 :], total.shape)
        gt, ht = total[:, 0], total[:, 1]
        base = gt * gt / (ht + 1.0)
        for t in range(TOPS):
            gl, hl = left[t][:, 0], left[t][:, 1]
            gain = gl * gl / (hl + 1.0)
            gain = gain + (gt - gl) * (gt - gl) / (ht - hl + 1.0)
            gain = gain - base
            out_ref[pl.ds(c * block, block), :, t * LANES : (t + 1) * LANES] = gain
            top_gain = jnp.maximum(top_gain, jnp.max(gain, axis=0))
        return top_gain

    top_gain = lax.fori_loop(0, chunks, finish, jnp.full((NODES, LANES), -jnp.inf, jnp.float32))

    def exchange(value, slots, count, axis, index, sems, arrived):
        slots[0] = jnp.broadcast_to(jnp.max(value, axis=1, keepdims=True), (NODES, LANES))
        copies = []
        for k in range(1, count):
            copies.append(
                pltpu.make_async_remote_copy(
                    src_ref=slots.at[0],
                    dst_ref=slots.at[k],
                    send_sem=sems.at[k - 1],
                    recv_sem=arrived.at[k - 1],
                    device_id={axis: (index + k) % count},
                    device_id_type=MESH,
                )
            )
            copies[-1].start()
        for copy in copies:
            copy.wait()
        best = slots[0]
        for k in range(1, count):
            best = jnp.maximum(best, slots[k])
        return best

    best = exchange(top_gain, row_best, n, "row", me, row_send, row_recv)
    best = exchange(best, feat_best, m, "feat", mine, feat_send, feat_recv)
    across = lax.broadcasted_iota(jnp.int32, (NODES, LANES), 1)
    down = lax.broadcasted_iota(jnp.int32, (NODES, LANES), 0)
    flat = jnp.max(jnp.where(across == down, best, -jnp.inf), axis=0, keepdims=True)
    best_ref[...] = flat[:, :NODES]


def take(x, index):
    return jnp.take_along_axis(x, index, axis=1, mode="promise_in_bounds")


def regroup(
    bins_hbm, node_ref, g_ref, h_ref, words_ref, gh_ref, keep_ref, last_ref,
    bins, pieces, pattern, spots_v, spots_s, load_sem, spots_sem,
):
    f32, bf16, i32 = jnp.float32, jnp.bfloat16, jnp.int32
    tiles = node_ref.shape[0]
    groups = bins.shape[0] // 32
    chunks = tiles // CHUNK

    def load(c):
        cols = pl.ds(pl.multiple_of(c * (CHUNK * LANES), CHUNK * LANES), CHUNK * LANES)
        return pltpu.make_async_copy(bins_hbm.at[:, cols], bins.at[:, cols], load_sem.at[c])

    for c in range(chunks):
        load(c).start()
    node = node_ref[...]
    pieces[0] = g_ref[...].astype(f32)
    pieces[1] = h_ref[...].astype(f32)
    row = lax.broadcasted_iota(i32, (LANES, LANES), 0)
    col = lax.broadcasted_iota(i32, (LANES, LANES), 1)
    upper = jnp.where(row <= col, 1.0, 0.0).astype(bf16)
    ones = jnp.ones((LANES, LANES), bf16)
    above = lax.broadcasted_iota(i32, (tiles, tiles), 1) < lax.broadcasted_iota(i32, (tiles, tiles), 0)
    lower = jnp.where(above, 1.0, 0.0).astype(bf16)
    dot = functools.partial(jnp.dot, preferred_element_type=f32)
    lane = lax.broadcasted_iota(i32, (tiles, LANES), 1)
    slot = lax.broadcasted_iota(i32, keep_ref.shape, 0)
    keep = jnp.ones(keep_ref.shape, f32)
    base = jnp.zeros((1, LANES), i32)
    last = jnp.zeros((1, LANES), i32)
    dest = jnp.zeros((tiles, LANES), i32)
    spots = jnp.zeros((tiles, LANES), i32)
    for n in range(NODES):
        hit = node == n
        x = jnp.where(hit, 1.0, 0.0).astype(bf16)
        rank = dot(x, upper).astype(i32)
        count = dot(x, ones)
        ahead = dot(lower, count.astype(bf16)).astype(i32)
        count = count.astype(i32)
        total = (ahead + count)[tiles - 1 : tiles]
        start = ahead + base
        dest = jnp.where(hit, start + rank - 1, dest)
        spots = jnp.where(lane == n, start, jnp.where(lane == NODES + n, start + count, spots))
        keep = jnp.where(slot * SLOT == base, 0.0, keep)
        base = base + jnp.maximum((total + (SLOT - 1)) // SLOT, 1) * SLOT
        last = jnp.where(lane[:1] == n, base // SLOT - 1, last)
    keep_ref[...] = keep
    last_ref[...] = last
    spots_v[...] = spots
    to_scalar = pltpu.make_async_copy(spots_v, spots_s, spots_sem)
    to_scalar.start()

    spot = dest & (LANES - 1)
    sub = lax.broadcasted_iota(i32, (NODES, LANES), 0)
    across = lax.broadcasted_iota(i32, (NODES, LANES), 1)
    none = jnp.zeros((NODES, LANES), i32)
    for b in range(0, tiles, 2):
        left, right = [], []
        for i in range(2):
            here = jnp.where(jnp.broadcast_to(node[b + i : b + i + 1], (NODES, LANES)) == sub, across, 0)
            left.append(jnp.concatenate([none] * i + [here] + [none] * (1 - i), 1))
            right.append(jnp.where(jnp.broadcast_to(spot[b + i : b + i + 1], (LANES, LANES)) == row, 1.0, 0.0))
        found = lax.dot_general(
            jnp.concatenate(left, 0).astype(f32).astype(bf16),
            jnp.concatenate(right, 1).astype(bf16),
            (((1,), (1,)), ((), ())),
            preferred_element_type=f32,
        ).astype(i32)
        pattern[b] = found[:NODES]
        pattern[b + 1] = found[NODES:]
    gh_ref[...] = jnp.zeros(gh_ref.shape, f32)
    to_scalar.wait()

    def place(b):
        cols = pl.ds(pl.multiple_of(b * LANES, LANES), LANES)
        words = []
        for t in range(groups):
            word = bins[32 * t : 32 * t + SUBLANES, cols]
            for k in range(1, PACK):
                word = word | lax.shift_left(bins[32 * t + SUBLANES * k : 32 * t + SUBLANES * (k + 1), cols], 8 * k)
            words.append(word)
        for t in range(0, groups, 2):
            one, two = words[t], words[t + 1]
            words[t], words[t + 1] = jnp.where(sub < 4, one, two), jnp.where(sub < 4, two, one)
        piece = [jnp.broadcast_to(pieces[i, pl.ds(b, 1), :], (SUBLANES, LANES)) for i in range(2)]
        gh = jnp.where(sub == 0, piece[0], piece[1])
        for n in range(NODES):
            first = spots_s[b, n]
            tile = lax.shift_right_logical(first, 7)
            low = first & (LANES - 1)
            high = low + spots_s[b, NODES + n] - first
            source = jnp.broadcast_to(pattern[b, n : n + 1, :], (SUBLANES, LANES))
            near = (across >= low) & (across < high)
            far = across < high - LANES
            for t in range(groups):
                moved = take(words[t], source)
                pltpu.store(words_ref.at[tile, t], moved, mask=near)
                pltpu.store(words_ref.at[tile + 1, t], moved, mask=far)
            moved = take(gh, source)
            pltpu.store(gh_ref.at[tile], moved, mask=near)
            pltpu.store(gh_ref.at[tile + 1], moved, mask=far)

    def chunk(c, carry):
        load(c).wait()
        for j in range(CHUNK):
            place(c * CHUNK + j)
        return carry

    lax.fori_loop(0, chunks, chunk, 0)


def sweep(
    n, m, words_hbm, gh_ref, keep_ref, last_ref, out_ref, best_ref,
    words, keys, gh, snap, stage, near, relay, far, row_best, feat_best,
    load_sem, near_send, near_recv, far_send, far_recv, row_send, row_recv, feat_send, feat_recv,
):
    f32 = jnp.float32
    tiles = words.shape[1]
    slots = tiles * LANES // SLOT
    pairs = n // 2
    order = ((0, 0), (0, 1), (2, 0), (1, 1), (1, 0), (2, 1), (3, 0), (3, 1))
    route = (2, 1, 2, 1, 1, 2, 3, 3)
    steps, away = 2 * pairs, 2 * (pairs - 1)
    me = lax.axis_index("row")
    mine = lax.axis_index("feat")
    chip, core = me // 2, me % 2

    def pick(u, table):
        value = table[0]
        for i in range(1, steps):
            value = jnp.where(u >= i, table[i], value)
        return value

    def half_of(u):
        return pick(u, [h for _, h in order])

    def chip_at(k):
        return partner(chip, pairs - 1 - k, pairs)

    def load(u, e):
        tile = 2 * chip_at(pick(u, [k for k, _ in order])) + half_of(u)
        return pltpu.make_async_copy(words_hbm.at[pl.ds(0, tiles), tile], words.at[e], load_sem.at[e])

    def send_near(u):
        return pltpu.make_async_remote_copy(
            src_ref=stage.at[u],
            dst_ref=near.at[u],
            send_sem=near_send.at[u],
            recv_sem=near_recv.at[u],
            device_id={"row": 2 * chip + 1 - core},
            device_id_type=MESH,
        )

    def send_far(u):
        return pltpu.make_async_remote_copy(
            src_ref=relay.at[u],
            dst_ref=far.at[u],
            send_sem=far_send.at[u],
            recv_sem=far_recv.at[u],
            device_id={"row": 2 * chip_at(pick(u, route)) + core},
            device_id_type=MESH,
        )

    load(0, 0).start()
    load(1, 1).start()
    barrier = pltpu.get_barrier_semaphore()
    for k in range(1, n):
        pl.semaphore_signal(barrier, inc=1, device_id={"row": (me + k) % n}, device_id_type=MESH)
    for k in range(1, m):
        pl.semaphore_signal(barrier, inc=1, device_id={"feat": (mine + k) % m}, device_id_type=MESH)
    for p in range(2):
        for q in range(tiles):
            gh[p, :, q * LANES : (q + 1) * LANES] = jnp.broadcast_to(gh_ref[q, p : p + 1, :], (16, LANES)).astype(jnp.bfloat16)
    pl.semaphore_wait(barrier, n + m - 2)

    wide = (32, SLOT)
    down = lax.broadcasted_iota(jnp.int32, wide, 0) % SUBLANES
    high_at = (down[:16] * DIGIT).astype(jnp.int16)
    low_at = [(down + SUBLANES * j).astype(jnp.int8) for j in range(4)]
    zero, one = jnp.zeros(wide, F8), jnp.ones(wide, F8)
    nil = jnp.zeros((16, SLOT), jnp.bfloat16)
    lane = lax.broadcasted_iota(jnp.int32, (SUBLANES, LANES), 1)
    sub = lax.broadcasted_iota(jnp.int32, (SUBLANES, LANES), 0)
    byte = (lane // SUBLANES) % PACK
    of = [byte == f for f in range(PACK - 1)]

    def unpack(e, q):
        for k in range(PACK):
            keys[e, k, :, q * LANES : (q + 1) * LANES] = lax.shift_right_logical(words[e, q], 8 * k)

    def one_hots(e, w, cols):
        rows = [jnp.broadcast_to(keys[e, k, pl.ds(w, 1), cols], (SUBLANES, SLOT)) for k in range(PACK)]
        twos = [jnp.concatenate(rows[i : i + 2], 0).astype(jnp.int16) for i in (0, 2)]
        low = jnp.concatenate(rows, 0).astype(jnp.int8) & jnp.int8(DIGIT - 1)
        left = []
        for two in twos:
            apart = (two & jnp.int16(BINS - DIGIT)) != high_at
            left += [jnp.where(apart, nil, gh[v, :, cols]) for v in range(2)]
        right = [jnp.where(low != low_at[j], zero, one) for j in range(4)]
        return left, right

    def block(e, w, side, hook):
        total = [jnp.zeros((SUBLANES, LANES), f32) for _ in range(4)]
        for s in range(slots):
            cols = slice(s * SLOT, (s + 1) * SLOT)
            left0, right0 = one_hots(e, w, cols)
            left1, right1 = one_hots(e, w + 1, cols)
            found = lax.dot_general(
                jnp.concatenate(left0 + left1, 0),
                jnp.concatenate(right0 + right1, 0),
                (((1,), (1,)), ((), ())),
                preferred_element_type=f32,
            )
            kept = jnp.broadcast_to(keep_ref[s : s + 1, :], (SUBLANES, LANES))
            for q in range(2):
                square = found[64 * q : 64 * (q + 1), q * LANES : (q + 1) * LANES]
                for v in range(2):
                    piece = [square[at : at + SUBLANES] for at in (16 * v, 16 * v + 8, 16 * v + 32, 16 * v + 40)]
                    dense = jnp.where(of[0], piece[0], jnp.where(of[1], piece[1], jnp.where(of[2], piece[2], piece[3])))
                    at = 2 * q + v
                    total[at] = total[at] * kept + dense
                    snap[side, s, at] = total[at]
            hook(s)

    def store(ref, u, b, side):
        for node in range(NODES):
            for at in range(4):
                ref[u, b, node, at] = snap[side, last_ref[0, node], at]

    def merge(u, ref, v):
        for b in range(2):
            for node in range(NODES):
                for at in range(4):
                    relay[u, b, node, at] += ref[v, b, node, at]

    middle = min(6, slots - 1)
    load(0, 0).wait()
    for q in range(tiles):
        unpack(0, q)

    def step(u, e):
        @pl.when(u >= 1)
        def _():
            store(relay, u - 1, 1, 1)
            send_near(u - 1).wait_recv()
            merge(u - 1, near, u - 1)

        @pl.when((u >= away - 1) & (u < steps - 1))
        def _():
            send_far(u - away + 1).wait_recv()
            merge(u - 1, far, u - away + 1)

        @pl.when(u < steps - 1)
        def _():
            load(u + 1, 1 - e).wait()

        @pl.when(u < steps - 2)
        def _():
            load(u + 2, e).start()

        @pl.when((u >= 1) & (u <= away))
        def _():
            send_far(u - 1).start()

        half = half_of(u)
        give = 4 * ((1 - core + half) % 2)
        hold = 4 * ((core + half) % 2)

        def at_middle(*args):
            def hook(s):
                if s == middle:
                    store(*args)

            return hook

        def third(s):
            if s == middle:
                store(stage, u, 1, 1)
            if s == slots // 2:
                send_near(u).start()
            for q in range(2 * s, 2 * s + 2):
                unpack(1 - e, q)

        block(e, give, 0, lambda s: None)
        block(e, give + 2, 1, at_middle(stage, u, 0, 0))
        block(e, hold, 0, third)
        block(e, hold + 2, 1, at_middle(relay, u, 0, 0))

    def both(i, carry):
        step(2 * i, 0)
        step(2 * i + 1, 1)
        return carry

    lax.fori_loop(0, pairs, both, 0)
    store(relay, steps - 1, 1, 1)
    send_near(steps - 1).wait_recv()
    merge(steps - 1, near, steps - 1)

    tens, units = lane // (SUBLANES * PACK), lane % SUBLANES
    end_of_run = lane - units + (SUBLANES - 1)
    end_of_row = (LANES - DIGIT) + byte * SUBLANES + (SUBLANES - 1)

    def running(x):
        for shift in (1, 2, 4):
            x = x + jnp.where(units >= shift, pltpu.roll(x, shift, 1), 0.0)
        run = take(x, end_of_run)
        for j in range(1, 4):
            x = x + jnp.where(tens >= j, pltpu.roll(run, j * DIGIT, 1), 0.0)
        row = take(x, end_of_row)
        whole = row
        for shift in (1, 2, 4):
            whole = whole + jnp.where(sub >= shift, pltpu.roll(whole, shift, 0), 0.0)
        return x + (whole - row), jnp.broadcast_to(whole[SUBLANES - 1 :], whole.shape)

    def gains(h, best):
        u = steps - 2 + h
        sources = [v for v in range(2, away) if order[v][1] == h]
        for v in sources:
            send_far(v).wait_recv()

        def one_block(b, best):
            tops = []
            for node in range(NODES):
                for q in range(2):
                    sums = []
                    for at in (2 * q, 2 * q + 1):
                        x = relay[u, b, node, at]
                        for v in sources:
                            x = x + far[v, b, node, at]
                        sums.append(running(x))
                    (gl, gt), (hl, ht) = sums
                    gain = gl * gl / (hl + 1.0)
                    gain = gain + (gt - gl) * (gt - gl) / (ht - hl + 1.0)
                    gain = gain - gt * gt / (ht + 1.0)
                    relay[u, b, node, 2 * q] = gain
                    top = gain if q == 0 else jnp.maximum(top, gain)
                tops.append(jnp.max(top, axis=0))
            return jnp.maximum(best, jnp.stack(tops, 0))

        return lax.fori_loop(0, 2, one_block, best)

    def layout(h):
        u = steps - 2 + h

        def one_block(b, carry):
            for q in range(2):
                turned = jnp.swapaxes(jnp.stack([relay[u, b, node, 2 * q] for node in range(NODES)], 0), 0, 1)
                for f in range(PACK):
                    source = ((lane // SUBLANES) % 4) * DIGIT + f * SUBLANES + units
                    for t in range(TOPS):
                        piece = [take(turned[4 * t + j], source) for j in range(4)]
                        line = jnp.where(tens == 0, piece[0], jnp.where(tens == 1, piece[1], jnp.where(tens == 2, piece[2], piece[3])))
                        feature = SUBLANES * f + 4 * ((core + h) % 2) + 2 * b + q
                        out_ref[feature, :, t * LANES : (t + 1) * LANES] = line
            return carry

        lax.fori_loop(0, 2, one_block, 0)

    def exchange(value, parts, count, axis, index, sems, arrived, during):
        parts[0] = jnp.broadcast_to(jnp.max(value, axis=1, keepdims=True), (NODES, LANES))
        copies = []
        for k in range(1, count):
            copies.append(
                pltpu.make_async_remote_copy(
                    src_ref=parts.at[0],
                    dst_ref=parts.at[k],
                    send_sem=sems.at[k - 1],
                    recv_sem=arrived.at[k - 1],
                    device_id={axis: (index + k) % count},
                    device_id_type=MESH,
                )
            )
            copies[-1].start()
        during()
        for copy in copies:
            copy.wait()
        best = parts[0]
        for k in range(1, count):
            best = jnp.maximum(best, parts[k])
        return best

    top_gain = jnp.full((NODES, LANES), -jnp.inf, f32)
    for h in range(2):
        top_gain = gains(h, top_gain)
    best = exchange(top_gain, row_best, n, "row", me, row_send, row_recv, lambda: layout(0))
    best = exchange(best, feat_best, m, "feat", mine, feat_send, feat_recv, lambda: layout(1))
    flat = jnp.max(jnp.where(lane == sub, best, -jnp.inf), axis=0, keepdims=True)
    best_ref[...] = flat[:, :NODES]
    for u in range(steps):
        send_near(u).wait_send()
        if u < away:
            send_far(u).wait_send()


def grouped(n, m, bins, grads, hess, node):
    features, rows = bins.shape
    groups, tiles = features // 32, rows // LANES
    slots = rows // SLOT + NODES - 1
    held = 2 * slots
    vmem = pl.BlockSpec(memory_space=pltpu.VMEM)
    smem = pl.BlockSpec(memory_space=pltpu.SMEM)
    hbm = pl.BlockSpec(memory_space=pl.ANY)
    words, gh, keep, last = pl.pallas_call(
        regroup,
        in_specs=[hbm, vmem, vmem, vmem],
        out_specs=(vmem, vmem, vmem, vmem),
        out_shape=(
            jax.ShapeDtypeStruct((held + 1, groups, SUBLANES, LANES), jnp.int32),
            jax.ShapeDtypeStruct((held + 1, SUBLANES, LANES), jnp.float32),
            jax.ShapeDtypeStruct((-(-slots // SUBLANES) * SUBLANES, LANES), jnp.float32),
            jax.ShapeDtypeStruct((1, LANES), jnp.int32),
        ),
        scratch_shapes=[
            pltpu.VMEM((features, rows), jnp.int32),
            pltpu.VMEM((2, tiles, LANES), jnp.float32),
            pltpu.VMEM((tiles, NODES, LANES), jnp.int32),
            pltpu.VMEM((tiles, LANES), jnp.int32),
            pltpu.SMEM((tiles, LANES), jnp.int32),
            pltpu.SemaphoreType.DMA((tiles // CHUNK,)),
            pltpu.SemaphoreType.DMA,
        ],
        compiler_params=pltpu.CompilerParams(vmem_limit_bytes=50 << 20),
    )(bins, node.reshape(-1, LANES), grads.reshape(-1, LANES), hess.reshape(-1, LANES))
    pairs = n // 2
    piece = (2, NODES, 4, SUBLANES, LANES)
    steps, away = 2 * pairs, 2 * (pairs - 1)
    out, best = pl.pallas_call(
        functools.partial(sweep, n, m),
        in_specs=[hbm, vmem, vmem, smem],
        out_specs=(vmem, vmem),
        out_shape=(
            jax.ShapeDtypeStruct((32, NODES, BINS), jnp.float32),
            jax.ShapeDtypeStruct((1, NODES), jnp.float32),
        ),
        scratch_shapes=[
            pltpu.VMEM((2, held, SUBLANES, LANES), jnp.int32),
            pltpu.VMEM((2, PACK, SUBLANES, held * LANES), jnp.int32),
            pltpu.VMEM((2, 16, held * LANES), jnp.bfloat16),
            pltpu.VMEM((2, slots, 4, SUBLANES, LANES), jnp.float32),
            pltpu.VMEM((steps,) + piece, jnp.float32),
            pltpu.VMEM((steps,) + piece, jnp.float32),
            pltpu.VMEM((steps,) + piece, jnp.float32),
            pltpu.VMEM((away,) + piece, jnp.float32),
            pltpu.VMEM((n, NODES, LANES), jnp.float32),
            pltpu.VMEM((m, NODES, LANES), jnp.float32),
            pltpu.SemaphoreType.DMA((2,)),
            pltpu.SemaphoreType.DMA((steps,)),
            pltpu.SemaphoreType.DMA((steps,)),
            pltpu.SemaphoreType.DMA((away,)),
            pltpu.SemaphoreType.DMA((away,)),
            pltpu.SemaphoreType.DMA((n - 1,)),
            pltpu.SemaphoreType.DMA((n - 1,)),
            pltpu.SemaphoreType.DMA((m - 1,)),
            pltpu.SemaphoreType.DMA((m - 1,)),
        ],
        compiler_params=pltpu.CompilerParams(
            collective_id=0, has_side_effects=True, vmem_limit_bytes=20 << 20
        ),
    )(words, gh, keep, last)
    best = best.reshape(NODES)
    return out - best[None, :, None], best


def solution(mesh):
    n, m = mesh.shape["row"], mesh.shape["feat"]

    def per_device(bins, grads, hess, node):
        features, rows = bins.shape
        own = features // n
        if own == 32 and n == 8 and rows % (CHUNK * LANES) == 0:
            return grouped(n, m, bins, grads, hess, node)
        block = own if own < SUBLANES else next(b for b in (2 * SUBLANES, SUBLANES) if own % b == 0)
        held = max(block, SUBLANES)
        chunks = own // block
        vmem = pl.BlockSpec(memory_space=pltpu.VMEM)
        piece = (block, LINES, LANES)
        out, best = pl.pallas_call(
            functools.partial(direct, n, m, block, chunks),
            in_specs=[pl.BlockSpec(memory_space=pl.ANY), vmem, vmem, vmem],
            out_specs=(vmem, vmem),
            out_shape=(
                jax.ShapeDtypeStruct((own, NODES, BINS), jnp.float32),
                jax.ShapeDtypeStruct((1, NODES), jnp.float32),
            ),
            scratch_shapes=[
                pltpu.VMEM((2, held, rows), jnp.int32),
                pltpu.VMEM((held, rows), jnp.float32),
                pltpu.VMEM((held, rows), jnp.float32),
                pltpu.VMEM((SLOTS, rows), jnp.bfloat16),
                pltpu.VMEM((SLOTS, rows), jnp.bfloat16),
                pltpu.VMEM((GROUP * HALVES * LINES, TILE), jnp.float32),
                pltpu.VMEM((n * chunks,) + piece, jnp.float32),
                pltpu.VMEM(((n - 1) * chunks,) + piece, jnp.float32),
                pltpu.VMEM((n, NODES, LANES), jnp.float32),
                pltpu.VMEM((m, NODES, LANES), jnp.float32),
                pltpu.SemaphoreType.DMA((2,)),
                pltpu.SemaphoreType.DMA(((n - 1) * chunks,)),
                pltpu.SemaphoreType.DMA(((n - 1) * chunks,)),
                pltpu.SemaphoreType.DMA((n - 1,)),
                pltpu.SemaphoreType.DMA((n - 1,)),
                pltpu.SemaphoreType.DMA((m - 1,)),
                pltpu.SemaphoreType.DMA((m - 1,)),
            ],
            compiler_params=pltpu.CompilerParams(
                collective_id=0, has_side_effects=True, vmem_limit_bytes=56 << 20
            ),
        )(bins, node.reshape(1, rows), grads.reshape(-1, LANES), hess.reshape(-1, LANES))
        best = best.reshape(NODES)
        return out - best[None, :, None], best

    return jax.shard_map(
        per_device,
        mesh=mesh,
        in_specs=(P("feat", "row"), P("row"), P("row"), P("row")),
        out_specs=(P(("feat", "row"), None, None), P()),
        check_vma=False,
    )
```

```python
import functools
import jax
import jax.numpy as jnp
from jax import lax
from jax.experimental import pallas as pl
from jax.experimental.pallas import tpu as pltpu
from jax.sharding import PartitionSpec as P

BINS = 256
NODES = 8
LANES = 128
SUBLANES = 8
LOW = 64
TILE = 256
GROUP = TILE // LOW
HALVES = LANES // LOW
TOPS = BINS // LANES
SLOTS = NODES * TOPS
LINES = 2 * SLOTS
MESH = pl.DeviceIdType.MESH
F8 = jnp.float8_e4m3fn
SLOT = 256
PACK = 4
CHUNK = 8
DIGIT = 32


def partner(me, k, n):
    if n & (n - 1):
        return (me + k) % n
    out, weight = 0, 1
    while weight < n:
        out = out + (((me // weight) % 2 + (k // weight) % 2) % 2) * weight
        weight *= 2
    return out


def direct(
    n, m, block, chunks, bins_hbm, node_ref, g_ref, h_ref, out_ref, best_ref,
    bins_buf, high_ref, low_ref, g_all, h_all, acc_ref, stage, landed, row_best, feat_best,
    load_sem, send_sem, recv_sem, row_send, row_recv, feat_send, feat_recv,
):
    rows = bins_buf.shape[2]
    me = lax.axis_index("row")
    mine = lax.axis_index("feat")
    steps = n * chunks
    sent = (n - 1) * chunks

    def place_of(s):
        return (partner(me, n - 1 - s // chunks, n) * chunks + s % chunks) * block

    def load(s):
        start = pl.multiple_of((place_of(s) // SUBLANES) * SUBLANES, SUBLANES)
        return pltpu.make_async_copy(
            bins_hbm.at[pl.ds(start, bins_buf.shape[1]), :], bins_buf.at[s % 2], load_sem.at[s % 2]
        )

    def send(s):
        k = n - 1 - s // chunks
        return pltpu.make_async_remote_copy(
            src_ref=stage.at[s],
            dst_ref=landed.at[s],
            send_sem=send_sem.at[s],
            recv_sem=recv_sem.at[s],
            device_id={"row": partner(me, k, n)},
            device_id_type=MESH,
        )

    load(0).start()
    barrier = pltpu.get_barrier_semaphore()
    for k in range(1, n):
        pl.semaphore_signal(barrier, inc=1, device_id={"row": (me + k) % n}, device_id_type=MESH)
    for k in range(1, m):
        pl.semaphore_signal(barrier, inc=1, device_id={"feat": (mine + k) % m}, device_id_type=MESH)

    g = g_ref[...].astype(jnp.float32)
    h = h_ref[...].astype(jnp.float32)
    for i in range(rows // LANES):
        cols = slice(i * LANES, (i + 1) * LANES)
        g_all[:, cols] = jnp.broadcast_to(g[i : i + 1, :], (SLOTS, LANES)).astype(jnp.bfloat16)
        h_all[:, cols] = jnp.broadcast_to(h[i : i + 1, :], (SLOTS, LANES)).astype(jnp.bfloat16)
    pl.semaphore_wait(barrier, n + m - 2)

    def step(s, carry):
        load(s).wait()

        @pl.when(s + 1 < steps)
        def _():
            load(s + 1).start()

        @pl.when((s >= 1) & (s <= sent))
        def _():
            send(s - 1).start()

        offset = 0 if block % SUBLANES == 0 else place_of(s) % SUBLANES
        bins = bins_buf[s % 2]
        upper = bins >= LANES
        rest = jnp.where(upper, bins - LANES, bins)
        second = rest >= LOW
        slot = node_ref[...] + jnp.where(upper, NODES, 0)
        high_ref[...] = jnp.where(second, slot + SLOTS, slot).astype(jnp.float32)
        low_ref[...] = jnp.where(second, rest - LOW, rest).astype(jnp.float32)
        place = lax.broadcasted_iota(jnp.int32, (SLOTS, rows), 0).astype(jnp.bfloat16)
        zero = jnp.zeros((SLOTS, rows), jnp.bfloat16)
        one = jnp.ones((SLOTS, rows), jnp.bfloat16)
        for first in range(0, block, GROUP):
            left, right = [], []
            for f in range(first, first + GROUP):
                row = pl.ds(offset + f, 1)
                high = jnp.broadcast_to(high_ref[row, :], (SLOTS, rows)).astype(jnp.bfloat16)
                low = jnp.broadcast_to(low_ref[row, :], (SLOTS, rows)).astype(jnp.bfloat16)
                for j in range(HALVES):
                    here = high == place + jnp.asarray(SLOTS * j, jnp.bfloat16)
                    left += [jnp.where(here, g_all[...], zero), jnp.where(here, h_all[...], zero)]
                for j in range(LOW // SLOTS):
                    here = low == place + jnp.asarray(SLOTS * j, jnp.bfloat16)
                    right.append(jnp.where(here, one, zero))
            acc_ref[...] = lax.dot_general(
                jnp.concatenate(left, 0),
                jnp.concatenate(right, 0),
                (((1,), (1,)), ((), ())),
                preferred_element_type=jnp.float32,
            )
            for i in range(GROUP):
                parts = []
                for j in range(HALVES):
                    top = (i * HALVES + j) * LINES
                    parts.append(acc_ref[top : top + LINES, i * LOW : (i + 1) * LOW])
                stage[s, first + i] = jnp.concatenate(parts, 1)
        return carry

    lax.fori_loop(0, steps, step, 0)

    def drain(s, carry):
        send(s).wait()
        return carry

    lax.fori_loop(0, sent, drain, 0)

    lane = lax.broadcasted_iota(jnp.int32, (block * 2 * TOPS * NODES, LANES), 1)

    def finish(c, top_gain):
        def add(k, total):
            return total + landed[k * chunks + c]

        x = lax.fori_loop(0, n - 1, add, stage[sent + c])
        x = x.reshape(block * LINES, LANES)
        shift = 1
        while shift < LANES:
            x = x + jnp.where(lane >= shift, pltpu.roll(x, shift, 1), 0.0)
            shift *= 2
        x = x.reshape(block, 2, TOPS, NODES, LANES)
        left, total = [], jnp.zeros((block, 2, NODES, LANES), jnp.float32)
        for t in range(TOPS):
            left.append(x[:, :, t] + total)
            total = total + jnp.broadcast_to(x[:, :, t, :, LANES - 1 :], total.shape)
        gt, ht = total[:, 0], total[:, 1]
        base = gt * gt / (ht + 1.0)
        for t in range(TOPS):
            gl, hl = left[t][:, 0], left[t][:, 1]
            gain = gl * gl / (hl + 1.0)
            gain = gain + (gt - gl) * (gt - gl) / (ht - hl + 1.0)
            gain = gain - base
            out_ref[pl.ds(c * block, block), :, t * LANES : (t + 1) * LANES] = gain
            top_gain = jnp.maximum(top_gain, jnp.max(gain, axis=0))
        return top_gain

    top_gain = lax.fori_loop(0, chunks, finish, jnp.full((NODES, LANES), -jnp.inf, jnp.float32))

    def exchange(value, slots, count, axis, index, sems, arrived):
        slots[0] = jnp.broadcast_to(jnp.max(value, axis=1, keepdims=True), (NODES, LANES))
        copies = []
        for k in range(1, count):
            copies.append(
                pltpu.make_async_remote_copy(
                    src_ref=slots.at[0],
                    dst_ref=slots.at[k],
                    send_sem=sems.at[k - 1],
                    recv_sem=arrived.at[k - 1],
                    device_id={axis: (index + k) % count},
                    device_id_type=MESH,
                )
            )
            copies[-1].start()
        for copy in copies:
            copy.wait()
        best = slots[0]
        for k in range(1, count):
            best = jnp.maximum(best, slots[k])
        return best

    best = exchange(top_gain, row_best, n, "row", me, row_send, row_recv)
    best = exchange(best, feat_best, m, "feat", mine, feat_send, feat_recv)
    across = lax.broadcasted_iota(jnp.int32, (NODES, LANES), 1)
    down = lax.broadcasted_iota(jnp.int32, (NODES, LANES), 0)
    flat = jnp.max(jnp.where(across == down, best, -jnp.inf), axis=0, keepdims=True)
    best_ref[...] = flat[:, :NODES]


def take(x, index):
    return jnp.take_along_axis(x, index, axis=1, mode="promise_in_bounds")


def regroup(
    bins_hbm, node_ref, g_ref, h_ref, words_ref, gh_ref, keep_ref, last_ref,
    bins, pieces, pattern, spots_v, spots_s, load_sem, spots_sem,
):
    f32, bf16, i32 = jnp.float32, jnp.bfloat16, jnp.int32
    tiles = node_ref.shape[0]
    groups = bins.shape[0] // 32
    chunks = tiles // CHUNK

    def load(c):
        cols = pl.ds(pl.multiple_of(c * (CHUNK * LANES), CHUNK * LANES), CHUNK * LANES)
        return pltpu.make_async_copy(bins_hbm.at[:, cols], bins.at[:, cols], load_sem.at[c])

    for c in range(chunks):
        load(c).start()
    node = node_ref[...].astype(i32)
    pieces[0] = g_ref[...].astype(f32)
    pieces[1] = h_ref[...].astype(f32)
    row = lax.broadcasted_iota(i32, (LANES, LANES), 0)
    col = lax.broadcasted_iota(i32, (LANES, LANES), 1)
    upper = jnp.where(row <= col, 1.0, 0.0).astype(bf16)
    ones = jnp.ones((LANES, LANES), bf16)
    above = lax.broadcasted_iota(i32, (tiles, tiles), 1) < lax.broadcasted_iota(i32, (tiles, tiles), 0)
    lower = jnp.where(above, 1.0, 0.0).astype(bf16)
    dot = functools.partial(jnp.dot, preferred_element_type=f32)
    lane = lax.broadcasted_iota(i32, (tiles, LANES), 1)
    slot = lax.broadcasted_iota(i32, keep_ref.shape, 0)
    keep = jnp.ones(keep_ref.shape, f32)
    base = jnp.zeros((1, LANES), i32)
    last = jnp.zeros((1, LANES), i32)
    dest = jnp.zeros((tiles, LANES), i32)
    spots = jnp.zeros((tiles, LANES), i32)
    for n in range(NODES):
        hit = node == n
        x = jnp.where(hit, 1.0, 0.0).astype(bf16)
        rank = dot(x, upper).astype(i32)
        count = dot(x, ones)
        ahead = dot(lower, count.astype(bf16)).astype(i32)
        count = count.astype(i32)
        total = (ahead + count)[tiles - 1 : tiles]
        start = ahead + base
        dest = jnp.where(hit, start + rank - 1, dest)
        spots = jnp.where(lane == n, start, jnp.where(lane == NODES + n, start + count, spots))
        keep = jnp.where(slot * SLOT == base, 0.0, keep)
        base = base + jnp.maximum((total + (SLOT - 1)) // SLOT, 1) * SLOT
        last = jnp.where(lane[:1] == n, base // SLOT - 1, last)
    keep_ref[...] = keep
    last_ref[...] = last
    spots_v[...] = spots
    to_scalar = pltpu.make_async_copy(spots_v, spots_s, spots_sem)
    to_scalar.start()

    spot = dest & (LANES - 1)
    sub = lax.broadcasted_iota(i32, (NODES, LANES), 0)
    across = lax.broadcasted_iota(i32, (NODES, LANES), 1)
    none = jnp.zeros((NODES, LANES), i32)
    for b in range(0, tiles, 2):
        left, right = [], []
        for i in range(2):
            here = jnp.where(jnp.broadcast_to(node[b + i : b + i + 1], (NODES, LANES)) == sub, across, 0)
            left.append(jnp.concatenate([none] * i + [here] + [none] * (1 - i), 1))
            right.append(jnp.where(jnp.broadcast_to(spot[b + i : b + i + 1], (LANES, LANES)) == row, 1.0, 0.0))
        found = lax.dot_general(
            jnp.concatenate(left, 0).astype(f32).astype(bf16),
            jnp.concatenate(right, 1).astype(bf16),
            (((1,), (1,)), ((), ())),
            preferred_element_type=f32,
        ).astype(i32)
        pattern[b] = found[:NODES]
        pattern[b + 1] = found[NODES:]
    gh_ref[...] = jnp.zeros(gh_ref.shape, f32)
    to_scalar.wait()

    def place(b):
        cols = pl.ds(pl.multiple_of(b * LANES, LANES), LANES)
        words = []
        for t in range(groups):
            word = bins[32 * t : 32 * t + SUBLANES, cols]
            for k in range(1, PACK):
                word = word | lax.shift_left(bins[32 * t + SUBLANES * k : 32 * t + SUBLANES * (k + 1), cols], 8 * k)
            words.append(word)
        for t in range(0, groups, 2):
            one, two = words[t], words[t + 1]
            words[t], words[t + 1] = jnp.where(sub < 4, one, two), jnp.where(sub < 4, two, one)
        piece = [jnp.broadcast_to(pieces[i, pl.ds(b, 1), :], (SUBLANES, LANES)) for i in range(2)]
        gh = jnp.where(sub == 0, piece[0], piece[1])
        for n in range(NODES):
            first = spots_s[b, n]
            tile = lax.shift_right_logical(first, 7)
            low = first & (LANES - 1)
            high = low + spots_s[b, NODES + n] - first
            source = jnp.broadcast_to(pattern[b, n : n + 1, :], (SUBLANES, LANES))
            near = (across >= low) & (across < high)
            far = across < high - LANES
            for t in range(groups):
                moved = take(words[t], source)
                pltpu.store(words_ref.at[tile, t], moved, mask=near)
                pltpu.store(words_ref.at[tile + 1, t], moved, mask=far)
            moved = take(gh, source)
            pltpu.store(gh_ref.at[tile], moved, mask=near)
            pltpu.store(gh_ref.at[tile + 1], moved, mask=far)

    def chunk(c, carry):
        load(c).wait()
        for j in range(CHUNK):
            place(c * CHUNK + j)
        return carry

    lax.fori_loop(0, chunks, chunk, 0)


def sweep(
    n, m, words_hbm, gh_ref, keep_ref, last_ref, out_ref, best_ref,
    words, keys, gh, snap, stage, near, relay, far, row_best, feat_best,
    load_sem, near_send, near_recv, far_send, far_recv, row_send, row_recv, feat_send, feat_recv,
):
    f32 = jnp.float32
    tiles = words.shape[1]
    slots = tiles * LANES // SLOT
    pairs = n // 2
    order = ((0, 0), (0, 1), (2, 0), (1, 1), (1, 0), (2, 1), (3, 0), (3, 1))
    route = (2, 1, 2, 1, 1, 2, 3, 3)
    steps, away = 2 * pairs, 2 * (pairs - 1)
    me = lax.axis_index("row")
    mine = lax.axis_index("feat")
    chip, core = me // 2, me % 2

    def pick(u, table):
        value = table[0]
        for i in range(1, steps):
            value = jnp.where(u >= i, table[i], value)
        return value

    def half_of(u):
        return pick(u, [h for _, h in order])

    def chip_at(k):
        return partner(chip, pairs - 1 - k, pairs)

    def load(u, e):
        tile = 2 * chip_at(pick(u, [k for k, _ in order])) + half_of(u)
        return pltpu.make_async_copy(words_hbm.at[pl.ds(0, tiles), tile], words.at[e], load_sem.at[e])

    def send_near(u):
        return pltpu.make_async_remote_copy(
            src_ref=stage.at[u],
            dst_ref=near.at[u],
            send_sem=near_send.at[u],
            recv_sem=near_recv.at[u],
            device_id={"row": 2 * chip + 1 - core},
            device_id_type=MESH,
        )

    def send_far(u):
        return pltpu.make_async_remote_copy(
            src_ref=relay.at[u],
            dst_ref=far.at[u],
            send_sem=far_send.at[u],
            recv_sem=far_recv.at[u],
            device_id={"row": 2 * chip_at(pick(u, route)) + core},
            device_id_type=MESH,
        )

    load(0, 0).start()
    load(1, 1).start()
    barrier = pltpu.get_barrier_semaphore()
    for k in range(1, n):
        pl.semaphore_signal(barrier, inc=1, device_id={"row": (me + k) % n}, device_id_type=MESH)
    for k in range(1, m):
        pl.semaphore_signal(barrier, inc=1, device_id={"feat": (mine + k) % m}, device_id_type=MESH)
    for p in range(2):
        for q in range(tiles):
            gh[p, :, q * LANES : (q + 1) * LANES] = jnp.broadcast_to(gh_ref[q, p : p + 1, :], (16, LANES)).astype(jnp.bfloat16)
    pl.semaphore_wait(barrier, n + m - 2)

    wide = (32, SLOT)
    down = lax.broadcasted_iota(jnp.int32, wide, 0) % SUBLANES
    high_at = (down[:16] * DIGIT).astype(jnp.int16)
    low_at = [(down + SUBLANES * j).astype(jnp.int8) for j in range(4)]
    zero, one = jnp.zeros(wide, F8), jnp.ones(wide, F8)
    nil = jnp.zeros((16, SLOT), jnp.bfloat16)
    lane = lax.broadcasted_iota(jnp.int32, (SUBLANES, LANES), 1)
    sub = lax.broadcasted_iota(jnp.int32, (SUBLANES, LANES), 0)
    byte = (lane // SUBLANES) % PACK
    of = [byte == f for f in range(PACK - 1)]

    def unpack(e, q):
        for k in range(PACK):
            keys[e, k, :, q * LANES : (q + 1) * LANES] = lax.shift_right_logical(words[e, q], 8 * k)

    def one_hots(e, w, cols):
        rows = [jnp.broadcast_to(keys[e, k, pl.ds(w, 1), cols], (SUBLANES, SLOT)) for k in range(PACK)]
        twos = [jnp.concatenate(rows[i : i + 2], 0).astype(jnp.int16) for i in (0, 2)]
        low = jnp.concatenate(rows, 0).astype(jnp.int8) & jnp.int8(DIGIT - 1)
        left = []
        for two in twos:
            apart = (two & jnp.int16(BINS - DIGIT)) != high_at
            left += [jnp.where(apart, nil, gh[v, :, cols]) for v in range(2)]
        right = [jnp.where(low != low_at[j], zero, one) for j in range(4)]
        return left, right

    def block(e, w, side, hook):
        total = [jnp.zeros((SUBLANES, LANES), f32) for _ in range(4)]
        for s in range(slots):
            cols = slice(s * SLOT, (s + 1) * SLOT)
            left0, right0 = one_hots(e, w, cols)
            left1, right1 = one_hots(e, w + 1, cols)
            found = lax.dot_general(
                jnp.concatenate(left0 + left1, 0),
                jnp.concatenate(right0 + right1, 0),
                (((1,), (1,)), ((), ())),
                preferred_element_type=f32,
            )
            kept = jnp.broadcast_to(keep_ref[s : s + 1, :], (SUBLANES, LANES))
            for q in range(2):
                square = found[64 * q : 64 * (q + 1), q * LANES : (q + 1) * LANES]
                for v in range(2):
                    piece = [square[at : at + SUBLANES] for at in (16 * v, 16 * v + 8, 16 * v + 32, 16 * v + 40)]
                    dense = jnp.where(of[0], piece[0], jnp.where(of[1], piece[1], jnp.where(of[2], piece[2], piece[3])))
                    at = 2 * q + v
                    total[at] = total[at] * kept + dense
                    snap[side, s, at] = total[at]
            hook(s)

    def store(ref, u, b, side):
        for node in range(NODES):
            for at in range(4):
                ref[u, b, node, at] = snap[side, last_ref[0, node], at]

    def merge(u, ref, v):
        for b in range(2):
            for node in range(NODES):
                for at in range(4):
                    relay[u, b, node, at] += ref[v, b, node, at]

    middle = min(6, slots - 1)
    load(0, 0).wait()
    for q in range(tiles):
        unpack(0, q)

    def step(u, e):
        @pl.when(u >= 1)
        def _():
            store(relay, u - 1, 1, 1)
            send_near(u - 1).wait_recv()
            merge(u - 1, near, u - 1)

        @pl.when((u >= away - 1) & (u < steps - 1))
        def _():
            send_far(u - away + 1).wait_recv()
            merge(u - 1, far, u - away + 1)

        @pl.when(u < steps - 1)
        def _():
            load(u + 1, 1 - e).wait()

        @pl.when(u < steps - 2)
        def _():
            load(u + 2, e).start()

        @pl.when((u >= 1) & (u <= away))
        def _():
            send_far(u - 1).start()

        half = half_of(u)
        give = 4 * ((1 - core + half) % 2)
        hold = 4 * ((core + half) % 2)

        def at_middle(*args):
            def hook(s):
                if s == middle:
                    store(*args)

            return hook

        def third(s):
            if s == middle:
                store(stage, u, 1, 1)
            if s == slots // 2:
                send_near(u).start()
            for q in range(2 * s, 2 * s + 2):
                unpack(1 - e, q)

        block(e, give, 0, lambda s: None)
        block(e, give + 2, 1, at_middle(stage, u, 0, 0))
        block(e, hold, 0, third)
        block(e, hold + 2, 1, at_middle(relay, u, 0, 0))

    def both(i, carry):
        step(2 * i, 0)
        step(2 * i + 1, 1)
        return carry

    lax.fori_loop(0, pairs, both, 0)
    store(relay, steps - 1, 1, 1)
    send_near(steps - 1).wait_recv()
    merge(steps - 1, near, steps - 1)

    tens, units = lane // (SUBLANES * PACK), lane % SUBLANES
    end_of_run = lane - units + (SUBLANES - 1)
    end_of_row = (LANES - DIGIT) + byte * SUBLANES + (SUBLANES - 1)

    def running(x):
        for shift in (1, 2, 4):
            x = x + jnp.where(units >= shift, pltpu.roll(x, shift, 1), 0.0)
        run = take(x, end_of_run)
        for j in range(1, 4):
            x = x + jnp.where(tens >= j, pltpu.roll(run, j * DIGIT, 1), 0.0)
        row = take(x, end_of_row)
        whole = row
        for shift in (1, 2, 4):
            whole = whole + jnp.where(sub >= shift, pltpu.roll(whole, shift, 0), 0.0)
        return x + (whole - row), jnp.broadcast_to(whole[SUBLANES - 1 :], whole.shape)

    def gains(h, best):
        u = steps - 2 + h
        sources = [v for v in range(2, away) if order[v][1] == h]
        for v in sources:
            send_far(v).wait_recv()

        def one_block(b, best):
            tops = []
            for node in range(NODES):
                for q in range(2):
                    sums = []
                    for at in (2 * q, 2 * q + 1):
                        x = relay[u, b, node, at]
                        for v in sources:
                            x = x + far[v, b, node, at]
                        sums.append(running(x))
                    (gl, gt), (hl, ht) = sums
                    gain = gl * gl / (hl + 1.0)
                    gain = gain + (gt - gl) * (gt - gl) / (ht - hl + 1.0)
                    gain = gain - gt * gt / (ht + 1.0)
                    relay[u, b, node, 2 * q] = gain
                    top = gain if q == 0 else jnp.maximum(top, gain)
                tops.append(jnp.max(top, axis=0))
            return jnp.maximum(best, jnp.stack(tops, 0))

        return lax.fori_loop(0, 2, one_block, best)

    def layout(h):
        u = steps - 2 + h

        def one_block(b, carry):
            for q in range(2):
                turned = jnp.swapaxes(jnp.stack([relay[u, b, node, 2 * q] for node in range(NODES)], 0), 0, 1)
                for f in range(PACK):
                    source = ((lane // SUBLANES) % 4) * DIGIT + f * SUBLANES + units
                    for t in range(TOPS):
                        piece = [take(turned[4 * t + j], source) for j in range(4)]
                        line = jnp.where(tens == 0, piece[0], jnp.where(tens == 1, piece[1], jnp.where(tens == 2, piece[2], piece[3])))
                        feature = SUBLANES * f + 4 * ((core + h) % 2) + 2 * b + q
                        out_ref[feature, :, t * LANES : (t + 1) * LANES] = line
            return carry

        lax.fori_loop(0, 2, one_block, 0)

    def exchange(value, parts, count, axis, index, sems, arrived, during):
        parts[0] = jnp.broadcast_to(jnp.max(value, axis=1, keepdims=True), (NODES, LANES))
        copies = []
        for k in range(1, count):
            copies.append(
                pltpu.make_async_remote_copy(
                    src_ref=parts.at[0],
                    dst_ref=parts.at[k],
                    send_sem=sems.at[k - 1],
                    recv_sem=arrived.at[k - 1],
                    device_id={axis: (index + k) % count},
                    device_id_type=MESH,
                )
            )
            copies[-1].start()
        during()
        for copy in copies:
            copy.wait()
        best = parts[0]
        for k in range(1, count):
            best = jnp.maximum(best, parts[k])
        return best

    top_gain = jnp.full((NODES, LANES), -jnp.inf, f32)
    for h in range(2):
        top_gain = gains(h, top_gain)
    best = exchange(top_gain, row_best, n, "row", me, row_send, row_recv, lambda: layout(0))
    best = exchange(best, feat_best, m, "feat", mine, feat_send, feat_recv, lambda: layout(1))
    flat = jnp.max(jnp.where(lane == sub, best, -jnp.inf), axis=0, keepdims=True)
    best_ref[...] = flat[:, :NODES]
    for u in range(steps):
        send_near(u).wait_send()
        if u < away:
            send_far(u).wait_send()


def grouped(n, m, bins, grads, hess, node):
    features, rows = bins.shape
    groups, tiles = features // 32, rows // LANES
    slots = rows // SLOT + NODES - 1
    held = 2 * slots
    vmem = pl.BlockSpec(memory_space=pltpu.VMEM)
    smem = pl.BlockSpec(memory_space=pltpu.SMEM)
    hbm = pl.BlockSpec(memory_space=pl.ANY)
    words, gh, keep, last = pl.pallas_call(
        regroup,
        in_specs=[hbm, vmem, vmem, vmem],
        out_specs=(vmem, vmem, vmem, vmem),
        out_shape=(
            jax.ShapeDtypeStruct((held + 1, groups, SUBLANES, LANES), jnp.int32),
            jax.ShapeDtypeStruct((held + 1, SUBLANES, LANES), jnp.float32),
            jax.ShapeDtypeStruct((-(-slots // SUBLANES) * SUBLANES, LANES), jnp.float32),
            jax.ShapeDtypeStruct((1, LANES), jnp.int32),
        ),
        scratch_shapes=[
            pltpu.VMEM((features, rows), jnp.int32),
            pltpu.VMEM((2, tiles, LANES), jnp.float32),
            pltpu.VMEM((tiles, NODES, LANES), jnp.int32),
            pltpu.VMEM((tiles, LANES), jnp.int32),
            pltpu.SMEM((tiles, LANES), jnp.int32),
            pltpu.SemaphoreType.DMA((tiles // CHUNK,)),
            pltpu.SemaphoreType.DMA,
        ],
        compiler_params=pltpu.CompilerParams(vmem_limit_bytes=50 << 20),
    )(bins, *(x.astype(jnp.float32).reshape(-1, LANES) for x in (node, grads, hess)))
    pairs = n // 2
    piece = (2, NODES, 4, SUBLANES, LANES)
    steps, away = 2 * pairs, 2 * (pairs - 1)
    out, best = pl.pallas_call(
        functools.partial(sweep, n, m),
        in_specs=[hbm, vmem, vmem, smem],
        out_specs=(vmem, vmem),
        out_shape=(
            jax.ShapeDtypeStruct((32, NODES, BINS), jnp.float32),
            jax.ShapeDtypeStruct((1, NODES), jnp.float32),
        ),
        scratch_shapes=[
            pltpu.VMEM((2, held, SUBLANES, LANES), jnp.int32),
            pltpu.VMEM((2, PACK, SUBLANES, held * LANES), jnp.int32),
            pltpu.VMEM((2, 16, held * LANES), jnp.bfloat16),
            pltpu.VMEM((2, slots, 4, SUBLANES, LANES), jnp.float32),
            pltpu.VMEM((steps,) + piece, jnp.float32),
            pltpu.VMEM((steps,) + piece, jnp.float32),
            pltpu.VMEM((steps,) + piece, jnp.float32),
            pltpu.VMEM((away,) + piece, jnp.float32),
            pltpu.VMEM((n, NODES, LANES), jnp.float32),
            pltpu.VMEM((m, NODES, LANES), jnp.float32),
            pltpu.SemaphoreType.DMA((2,)),
            pltpu.SemaphoreType.DMA((steps,)),
            pltpu.SemaphoreType.DMA((steps,)),
            pltpu.SemaphoreType.DMA((away,)),
            pltpu.SemaphoreType.DMA((away,)),
            pltpu.SemaphoreType.DMA((n - 1,)),
            pltpu.SemaphoreType.DMA((n - 1,)),
            pltpu.SemaphoreType.DMA((m - 1,)),
            pltpu.SemaphoreType.DMA((m - 1,)),
        ],
        compiler_params=pltpu.CompilerParams(
            collective_id=0, has_side_effects=True, vmem_limit_bytes=20 << 20
        ),
    )(words, gh, keep, last)
    best = best.reshape(NODES)
    return out - best[None, :, None], best


def solution(mesh):
    n, m = mesh.shape["row"], mesh.shape["feat"]

    def per_device(bins, grads, hess, node):
        features, rows = bins.shape
        own = features // n
        if own == 32 and n == 8 and rows % (CHUNK * LANES) == 0:
            return grouped(n, m, bins, grads, hess, node)
        block = own if own < SUBLANES else next(b for b in (2 * SUBLANES, SUBLANES) if own % b == 0)
        held = max(block, SUBLANES)
        chunks = own // block
        vmem = pl.BlockSpec(memory_space=pltpu.VMEM)
        piece = (block, LINES, LANES)
        out, best = pl.pallas_call(
            functools.partial(direct, n, m, block, chunks),
            in_specs=[pl.BlockSpec(memory_space=pl.ANY), vmem, vmem, vmem],
            out_specs=(vmem, vmem),
            out_shape=(
                jax.ShapeDtypeStruct((own, NODES, BINS), jnp.float32),
                jax.ShapeDtypeStruct((1, NODES), jnp.float32),
            ),
            scratch_shapes=[
                pltpu.VMEM((2, held, rows), jnp.int32),
                pltpu.VMEM((held, rows), jnp.float32),
                pltpu.VMEM((held, rows), jnp.float32),
                pltpu.VMEM((SLOTS, rows), jnp.bfloat16),
                pltpu.VMEM((SLOTS, rows), jnp.bfloat16),
                pltpu.VMEM((GROUP * HALVES * LINES, TILE), jnp.float32),
                pltpu.VMEM((n * chunks,) + piece, jnp.float32),
                pltpu.VMEM(((n - 1) * chunks,) + piece, jnp.float32),
                pltpu.VMEM((n, NODES, LANES), jnp.float32),
                pltpu.VMEM((m, NODES, LANES), jnp.float32),
                pltpu.SemaphoreType.DMA((2,)),
                pltpu.SemaphoreType.DMA(((n - 1) * chunks,)),
                pltpu.SemaphoreType.DMA(((n - 1) * chunks,)),
                pltpu.SemaphoreType.DMA((n - 1,)),
                pltpu.SemaphoreType.DMA((n - 1,)),
                pltpu.SemaphoreType.DMA((m - 1,)),
                pltpu.SemaphoreType.DMA((m - 1,)),
            ],
            compiler_params=pltpu.CompilerParams(
                collective_id=0, has_side_effects=True, vmem_limit_bytes=56 << 20
            ),
        )(bins, node.reshape(1, rows), grads.reshape(-1, LANES), hess.reshape(-1, LANES))
        best = best.reshape(NODES)
        return out - best[None, :, None], best

    return jax.shard_map(
        per_device,
        mesh=mesh,
        in_specs=(P("feat", "row"), P("row"), P("row"), P("row")),
        out_specs=(P(("feat", "row"), None, None), P()),
        check_vma=False,
    )
```
